32 devices in a mesh: clips: 2 (over y), sa: 4 (over z), wa: 2 (over x), hp: 2 (over core).
Axes of the slice: x: 2, y: 2, z: 4, core: 2. Of those that a mesh axis runs over, the one named last changes fastest.
Arguments:
- queries: bfloat16 [16, 8, 16, 3072], P(('clips', 'sa'), None, 'wa', 'hp'), parts along dimension 0, may hold values from -6 to 6
- keys: bfloat16 [16, 8, 16, 3072], P(('clips', 'sa'), None, 'wa', 'hp'), parts along dimension 0, may hold values from -6 to 6
- values: bfloat16 [16, 8, 16, 3072], P(('clips', 'sa'), None, 'wa', 'hp'), parts along dimension 0, may hold values from -6 to 6
- text_keys: bfloat16 [512, 3072], P(('clips', 'sa'), 'hp'), parts along dimension 0, may hold values from -6 to 6
- text_values: bfloat16 [512, 3072], P(('clips', 'sa'), 'hp'), parts along dimension 0, may hold values from -6 to 6
- out_grad: bfloat16 [16, 8, 16, 3072], P(('clips', 'sa'), None, 'wa', 'hp'), parts along dimension 0, may hold values from -6 to 6
- window_ext: int32 [24, 3], P('hp'), may hold values from 0 to 1, as said below
Outputs:
- attended: bfloat16 [16, 8, 16, 3072], P(('clips', 'sa'), None, 'wa', 'hp'), parts along dimension 0
- query_grad: bfloat16 [16, 8, 16, 3072], P(('clips', 'sa'), None, 'wa', 'hp'), parts along dimension 0
- key_grad: bfloat16 [16, 8, 16, 3072], P(('clips', 'sa'), None, 'wa', 'hp'), parts along dimension 0
- value_grad: bfloat16 [16, 8, 16, 3072], P(('clips', 'sa'), None, 'wa', 'hp'), parts along dimension 0
- text_key_grad: float32 [512, 3072], P(('clips', 'sa'), 'hp'), parts along dimension 0
- text_value_grad: float32 [512, 3072], P(('clips', 'sa'), 'hp'), parts along dimension 0
The draws below stay inside these ranges and needn't reach their ends.
There are 2 independent parts, one for each index of `clips`. The reference program is written for one: setup_inputs(seed, part) draws one part's arguments, and reference() takes and returns one part's arrays. A program takes and returns all parts, laid end to end along the dimension named above; an argument that names none is the same for every part. Nothing has to cross between parts.
Inputs may be any that keep to these rules, and one draw needn't show every extreme that they name: `window_ext`: columns 0, 1 and 2 are at most 1, 1 and 1; each of these bounds is reached by some head.
All inputs are finite; a program needn't handle non-finite values.
Results may differ from the reference program's by a relative error of at most 0.012.
The reference program's roundings to bfloat16 on the way count: a program that leaves them out, or rounds other values in their place, can miss the bound.
Values may be sent and summed in bfloat16 or wider, within the bound.
A program may use at most 128 MiB of HBM per device.

```python
import jax
import jax.numpy as jnp
from jax import lax

HEADS = 24
HEAD_DIM = 128
TEXT_TOKENS = 256
FRAMES_DEV = 2
HEIGHT = 8
COLS_DEV = 8
TILE_T = 2
TILE_H = 8
TILE_W = 8
EXT_T = 1
EXT_H = 1
EXT_W = 1
FRAMES = 8
WIDTH = 16
N_SA = 4
N_WA = 2


def draw_queries(key, part):
    full_shape = (FRAMES, HEIGHT, WIDTH, HEADS * HEAD_DIM)
    result = jax.random.truncated_normal(jax.random.fold_in(key, 1), -6.0, 6.0, full_shape, jnp.float32)
    return result.astype(jnp.bfloat16)


def draw_keys(key, part):
    full_shape = (FRAMES, HEIGHT, WIDTH, HEADS * HEAD_DIM)
    result = jax.random.truncated_normal(jax.random.fold_in(key, 2), -6.0, 6.0, full_shape, jnp.float32)
    return result.astype(jnp.bfloat16)


def draw_window_ext(key, part):
    columns_out = []
    bounds = (EXT_T, EXT_H, EXT_W)
    for axis_number in range(3):
        drawn = jax.random.randint(jax.random.fold_in(key, 20 + axis_number), (HEADS,), 0, bounds[axis_number] + 1)
        chosen = jax.random.randint(jax.random.fold_in(key, 30 + axis_number), (), 0, HEADS)
        drawn = jnp.where(jnp.arange(HEADS, dtype=jnp.int32) == chosen, bounds[axis_number], drawn)
        columns_out.append(drawn.astype(jnp.int32))
    return jnp.stack(columns_out, axis=1)


def level_of(stream_key, shape, pieces, low, largest):
    factor_of, own = 1.0, jax.random.fold_in(stream_key, 6)
    for position, shards_of in pieces:
        steps = jnp.exp(jax.random.uniform(jax.random.fold_in(own, position), (shards_of,), jnp.float32, low / len(pieces), largest / len(pieces)))
        factor_of = factor_of * jnp.repeat(steps, shape[position] // shards_of).reshape([-1 if axis == position else 1 for axis in range(len(shape))])
    return factor_of


def gaussian(stream_key, dims, scale, reach, shards=(), held_as=jnp.bfloat16):
    level = level_of(stream_key, dims, shards, -0.22, 0.18) if shards else 1.0
    values = jax.random.normal(stream_key, dims, jnp.float32) * scale * level
    return jnp.minimum(jnp.maximum(values, -reach), reach).astype(held_as)


def setup_inputs(seed: int = 0, part: int = 0) -> dict:
    key_of = jax.random.split(jax.random.key(seed), 8)
    part_splits = jax.random.split(jax.random.fold_in(key_of[7], part), 8)
    return {
        "queries": draw_queries(jax.random.fold_in(jax.random.fold_in(key_of[7], part), 71), part),
        "keys": draw_keys(jax.random.fold_in(jax.random.fold_in(key_of[7], part), 71), part),
        "values": gaussian(part_splits[2], (FRAMES, HEIGHT, WIDTH, HEADS * HEAD_DIM), 1.0, 6.0, ((0, 4), (2, 2), (3, 2))),
        "text_keys": gaussian(part_splits[3], (TEXT_TOKENS, HEADS * HEAD_DIM), 1.0, 6.0, ((0, 4), (1, 2))),
        "text_values": gaussian(part_splits[4], (TEXT_TOKENS, HEADS * HEAD_DIM), 1.0, 6.0, ((0, 4), (1, 2))),
        "out_grad": gaussian(part_splits[5], (FRAMES, HEIGHT, WIDTH, HEADS * HEAD_DIM), 1.0, 6.0, ((0, 4), (2, 2), (3, 2))),
        "window_ext": draw_window_ext(jax.random.fold_in(key_of[7], 71), part),
    }


def tile_coords(time_start, frame_count, row_count, col_start, col_count, total_frames, total_cols):
    times = time_start + jnp.arange(frame_count, dtype=jnp.int32)
    heights = jnp.arange(row_count, dtype=jnp.int32)
    columns = col_start + jnp.arange(col_count, dtype=jnp.int32)
    grid_shape = (frame_count, row_count, col_count)
    time_grid = jnp.broadcast_to(times[:, None, None], grid_shape).reshape(-1)
    height_grid = jnp.broadcast_to(heights[None, :, None], grid_shape).reshape(-1)
    col_grid = jnp.broadcast_to(columns[None, None, :], grid_shape).reshape(-1)
    inside = (time_grid >= 0) & (time_grid < total_frames) & (col_grid >= 0) & (col_grid < total_cols)
    return (time_grid // TILE_T, height_grid // TILE_H, col_grid // TILE_W, inside)


def pair_mask(first, second, window):
    allowed = first[3][:, None] & second[3][None, :]
    for axis_number in range(3):
        apart = jnp.abs(first[axis_number][:, None] - second[axis_number][None, :])
        allowed = allowed & (apart <= window[axis_number])
    return allowed


def forward_head(query_head, key_head, value_head, text_key, text_value, allowed):
    score_scale = HEAD_DIM ** -0.5
    video_scores = jnp.dot(query_head, key_head.T, preferred_element_type=jnp.float32) * score_scale
    video_scores = jnp.where(allowed, video_scores, -1e30)
    text_scores = jnp.dot(query_head, text_key.T, preferred_element_type=jnp.float32) * score_scale
    row_max = jnp.maximum(jnp.max(video_scores, axis=1), jnp.max(text_scores, axis=1))
    denom_sum = jnp.sum(jnp.exp(video_scores - row_max[:, None]), axis=1) + jnp.sum(jnp.exp(text_scores - row_max[:, None]), axis=1)
    log_total = row_max + jnp.log(denom_sum)
    video_weights = jnp.exp(video_scores - log_total[:, None]).astype(jnp.bfloat16)
    text_weights = jnp.exp(text_scores - log_total[:, None]).astype(jnp.bfloat16)
    attended_head = jnp.dot(video_weights, value_head, preferred_element_type=jnp.float32)
    attended_head = attended_head + jnp.dot(text_weights, text_value, preferred_element_type=jnp.float32)
    return attended_head.astype(jnp.bfloat16), log_total


def grads_head(query_head, grad_head, log_total, row_delta, key_head, value_head, text_key, text_value, allowed):
    score_scale = HEAD_DIM ** -0.5
    video_scores = jnp.dot(query_head, key_head.T, preferred_element_type=jnp.float32) * score_scale
    video_scores = jnp.where(allowed, video_scores, -1e30)
    text_scores = jnp.dot(query_head, text_key.T, preferred_element_type=jnp.float32) * score_scale
    video_probs = jnp.exp(video_scores - log_total[:, None])
    text_probs = jnp.exp(text_scores - log_total[:, None])
    video_dprobs = jnp.dot(grad_head, value_head.T, preferred_element_type=jnp.float32)
    text_dprobs = jnp.dot(grad_head, text_value.T, preferred_element_type=jnp.float32)
    video_dscores = (video_probs * (video_dprobs - row_delta[:, None]) * score_scale).astype(jnp.bfloat16)
    text_dscores = (text_probs * (text_dprobs - row_delta[:, None]) * score_scale).astype(jnp.bfloat16)
    query_term = jnp.dot(video_dscores, key_head, preferred_element_type=jnp.float32)
    query_term = query_term + jnp.dot(text_dscores, text_key, preferred_element_type=jnp.float32)
    key_term = jnp.dot(video_dscores.T, query_head, preferred_element_type=jnp.float32)
    value_term = jnp.dot(video_probs.astype(jnp.bfloat16).T, grad_head, preferred_element_type=jnp.float32)
    text_key_term = jnp.dot(text_dscores.T, query_head, preferred_element_type=jnp.float32)
    text_value_term = jnp.dot(text_probs.astype(jnp.bfloat16).T, grad_head, preferred_element_type=jnp.float32)
    return query_term, key_term, value_term, text_key_term, text_value_term


def reference(queries, keys, values, text_keys, text_values, out_grad, window_ext):
    rim_time = EXT_T * TILE_T
    rim_cols = EXT_W * TILE_W
    near_shape = (FRAMES_DEV + 2 * rim_time, HEIGHT, COLS_DEV + 2 * rim_cols, HEAD_DIM)
    own_shape = (FRAMES_DEV, HEIGHT, COLS_DEV, HEAD_DIM)

    def heads_first(tensor):
        return jnp.moveaxis(tensor.reshape(FRAMES, HEIGHT, WIDTH, HEADS, HEAD_DIM), 3, 0)

    def text_first(tensor):
        return jnp.moveaxis(tensor.reshape(TEXT_TOKENS, HEADS, HEAD_DIM), 1, 0)

    def one_head(operands):
        query_all, key_all, value_all, grad_all, text_key, text_value, window = operands
        padding = ((rim_time, rim_time), (0, 0), (rim_cols, rim_cols), (0, 0))
        key_padded = jnp.pad(key_all, padding)
        value_padded = jnp.pad(value_all, padding)

        def block(running, block_index):
            key_acc, value_acc, text_key_acc, text_value_acc = running
            time_start = (block_index // N_WA) * FRAMES_DEV
            col_start = (block_index % N_WA) * COLS_DEV
            corner = (time_start, jnp.int32(0), col_start, jnp.int32(0))
            query_block = lax.dynamic_slice(query_all, corner, own_shape).reshape(-1, HEAD_DIM)
            grad_block = lax.dynamic_slice(grad_all, corner, own_shape).reshape(-1, HEAD_DIM)
            key_block = lax.dynamic_slice(key_padded, corner, near_shape).reshape(-1, HEAD_DIM)
            value_block = lax.dynamic_slice(value_padded, corner, near_shape).reshape(-1, HEAD_DIM)
            own_cells = tile_coords(time_start, FRAMES_DEV, HEIGHT, col_start, COLS_DEV, FRAMES, WIDTH)
            near_cells = tile_coords(time_start - rim_time, FRAMES_DEV + 2 * rim_time, HEIGHT, col_start - rim_cols, COLS_DEV + 2 * rim_cols, FRAMES, WIDTH)
            allowed = pair_mask(own_cells, near_cells, window)
            attended_head, log_total = forward_head(query_block, key_block, value_block, text_key, text_value, allowed)
            row_delta = jnp.sum(grad_block.astype(jnp.float32) * attended_head.astype(jnp.float32), axis=1)
            query_term, key_term, value_term, text_key_term, text_value_term = grads_head(query_block, grad_block, log_total, row_delta, key_block, value_block, text_key, text_value, allowed)
            key_acc = lax.dynamic_update_slice(key_acc, lax.dynamic_slice(key_acc, corner, near_shape) + key_term.reshape(near_shape), corner)
            value_acc = lax.dynamic_update_slice(value_acc, lax.dynamic_slice(value_acc, corner, near_shape) + value_term.reshape(near_shape), corner)
            running = (key_acc, value_acc, text_key_acc + text_key_term, text_value_acc + text_value_term)
            return running, (attended_head.reshape(own_shape), query_term.astype(jnp.bfloat16).reshape(own_shape))

        padded_shape = (FRAMES + 2 * rim_time, HEIGHT, WIDTH + 2 * rim_cols, HEAD_DIM)
        start = (jnp.zeros(padded_shape, jnp.float32), jnp.zeros(padded_shape, jnp.float32), jnp.zeros((TEXT_TOKENS, HEAD_DIM), jnp.float32), jnp.zeros((TEXT_TOKENS, HEAD_DIM), jnp.float32))
        running, stacked = lax.scan(block, start, jnp.arange(N_SA * N_WA, dtype=jnp.int32))

        def regrid(blocks):
            blocks = blocks.reshape(N_SA, N_WA, FRAMES_DEV, HEIGHT, COLS_DEV, HEAD_DIM)
            return jnp.transpose(blocks, (0, 2, 3, 1, 4, 5)).reshape(FRAMES, HEIGHT, WIDTH, HEAD_DIM)

        key_grad_head = running[0][rim_time:rim_time + FRAMES, :, rim_cols:rim_cols + WIDTH].astype(jnp.bfloat16)
        value_grad_head = running[1][rim_time:rim_time + FRAMES, :, rim_cols:rim_cols + WIDTH].astype(jnp.bfloat16)
        return regrid(stacked[0]), regrid(stacked[1]), key_grad_head, value_grad_head, running[2], running[3]

    results = lax.map(one_head, (heads_first(queries), heads_first(keys), heads_first(values), heads_first(out_grad), text_first(text_keys), text_first(text_values), window_ext))

    def grid_back(tensor):
        return jnp.moveaxis(tensor, 0, 3).reshape(FRAMES, HEIGHT, WIDTH, HEADS * HEAD_DIM)

    def text_back(tensor):
        return jnp.moveaxis(tensor, 0, 1).reshape(TEXT_TOKENS, HEADS * HEAD_DIM)

    return (grid_back(results[0]), grid_back(results[1]), grid_back(results[2]), grid_back(results[3]), text_back(results[4]), text_back(results[5]))
```

```python
import functools

import jax
import jax.numpy as jnp
from jax import lax
from jax.experimental import pallas as pl
from jax.experimental.pallas import tpu as pltpu
from jax.sharding import PartitionSpec as P

HEAD_DIM = 128
NEG = -1e30
MESH = pl.DeviceIdType.MESH
F32 = jnp.float32
BF16 = jnp.bfloat16
KEY_BLOCK = 256
Q_BLOCK = 256
FEED = 3
RETURN_LAG = 2
FINISH_LAG = 4


def dot_nt(a, b):
    return lax.dot_general(a, b, (((1,), (1,)), ((), ())), preferred_element_type=F32)


def dot_tn(a, b):
    return lax.dot_general(a, b, (((0,), (0,)), ((), ())), preferred_element_type=F32)


def kernel(
    n_sa, n_wa, heads, near, cells, text_rows,
    window, k_in, v_in, q_in, g_in, tk_in, tv_in,
    res_out, text_out,
    cell_in, words_in, stage, kv, qg, oq, own_part, z_part, z_got, fin, t_part, t_got, t_fin, st, wb, db,
    load, x_send, x_recv, t_send, t_recv, z_send, z_recv,
    r_send, r_recv, y_send, y_recv, y_loc, g_send, g_recv, f_send, f_recv, f_loc,
):
    s = lax.axis_index("sa")
    w = lax.axis_index("wa")
    slab = n_wa * cells
    text = n_sa * text_rows
    own_base = 2 * slab
    text_base = 3 * slab
    scale = HEAD_DIM ** (-0.5)
    has_prev, has_next = s > 0, s < n_sa - 1
    before, after = lax.rem(s + n_sa - 1, n_sa), lax.rem(s + 1, n_sa)
    q_block = min(slab, Q_BLOCK)

    def rows_of(base, index, size):
        return pl.ds(pl.multiple_of(base + index * size, 16), size)

    def remote(src, dst, send, recv, **where):
        return pltpu.make_async_remote_copy(
            src_ref=src, dst_ref=dst, send_sem=send, recv_sem=recv,
            device_id=where, device_id_type=MESH,
        )

    def peer_of(d):
        return lax.rem(w + d, n_wa)

    def source_of(d):
        return lax.rem(w + n_wa - d, n_wa)

    loads = [
        pltpu.make_async_copy(ref, cell_in.at[kind], load.at[kind])
        for kind, ref in enumerate((k_in, v_in, q_in, g_in))
    ] + [
        pltpu.make_async_copy(ref, words_in.at[kind], load.at[4 + kind])
        for kind, ref in enumerate((tk_in, tv_in))
    ]
    for copy in loads:
        copy.start()

    barrier = pltpu.get_barrier_semaphore()
    for d in range(1, n_wa):
        pl.semaphore_signal(barrier, inc=1, device_id={"wa": peer_of(d)}, device_id_type=MESH)

    @pl.when(has_prev)
    def _():
        pl.semaphore_signal(barrier, inc=1, device_id={"sa": before}, device_id_type=MESH)

    @pl.when(has_next)
    def _():
        pl.semaphore_signal(barrier, inc=1, device_id={"sa": after}, device_id_type=MESH)

    def clear_side(side):
        def clear(h, c):
            if near:
                @pl.when(h < near)
                def _():
                    kv[h, :, pl.ds(side * slab, slab)] = jnp.zeros((2, slab, HEAD_DIM), BF16)
                    z_got[1 - side, h] = jnp.zeros((2, slab, HEAD_DIM), BF16)

            t_got[side, h, 0 if side == 0 else n_sa - 1] = jnp.zeros((2, text_rows, HEAD_DIM), BF16)
            return c

        lax.fori_loop(0, heads, clear, 0)

    @pl.when(jnp.logical_not(has_prev))
    def _():
        clear_side(0)

    @pl.when(jnp.logical_not(has_next))
    def _():
        clear_side(1)

    def columns(slot):
        return pl.ds(pl.multiple_of(slot * HEAD_DIM, HEAD_DIM), HEAD_DIM)

    for copy in loads:
        copy.wait()

    def arrange(h, c):
        here = columns(w * heads + h)
        for kind in range(2):
            kv[h, kind, rows_of(text_base, s, text_rows)] = words_in[kind, :, here]
            kv[h, kind, rows_of(own_base, w, cells)] = cell_in[kind, :, here]
            qg[h, kind, rows_of(0, w, cells)] = cell_in[2 + kind, :, here]
        for d in range(1, n_wa):
            slot = peer_of(d) * heads + h
            for kind in range(4):
                stage[d - 1, h, kind] = cell_in[kind, :, columns(slot)]
        return c

    lax.fori_loop(0, heads, arrange, 0)

    neighbours = n_wa - 1 + has_prev.astype(jnp.int32) + has_next.astype(jnp.int32)
    pl.semaphore_wait(barrier, neighbours)

    def x_slot(pair, h, source):
        if pair == 0:
            return kv.at[h, :, rows_of(own_base, source, cells)]
        return qg.at[h, :, rows_of(0, source, cells)]

    def x_copy(pair, h, d, source):
        return remote(
            stage.at[d - 1, h, pl.ds(2 * pair, 2)], x_slot(pair, h, source),
            x_send.at[d - 1], x_recv.at[d - 1, h, pair], wa=peer_of(d),
        )

    def x_wait(pair, h):
        for d in range(1, n_wa):
            x_copy(pair, h, d, source_of(d)).wait_recv()

    def t_slot(h, block):
        return kv.at[h, :, rows_of(text_base, block, text_rows)]

    def t_hop(side, h, hop, block):
        return remote(
            t_slot(h, block), t_slot(h, block), t_send.at[side, hop], t_recv.at[side, h, hop],
            sa=after if side == 0 else before,
        )

    def t_out(side, h, hop):
        return t_hop(side, h, hop, s - hop if side == 0 else s + hop)

    def t_in(side, h, hop):
        return t_hop(side, h, hop, s - 1 - hop if side == 0 else s + 1 + hop)

    def t_valid(side, hop):
        if side == 0:
            return jnp.logical_and(s >= hop, has_next)
        return jnp.logical_and(s + hop < n_sa, has_prev)

    def t_forward(h, hop):
        for side in range(2):
            @pl.when(t_valid(side, hop))
            def _():
                if hop:
                    t_in(side, h, hop - 1).wait_recv()
                t_out(side, h, hop).start()

    def z_copy(side, h):
        return remote(
            kv.at[h, :, pl.ds(own_base, slab)], kv.at[h, :, pl.ds(side * slab, slab)],
            z_send.at[side], z_recv.at[side, h], sa=after if side == 0 else before,
        )

    def r_copy(side, h, d):
        rows = rows_of(0, peer_of(d), cells)
        return remote(
            z_part.at[side, h, :, rows], z_got.at[side, h, :, rows],
            r_send.at[side], r_recv.at[side, h, d], sa=before if side == 0 else after,
        )

    def open_head(h, c):
        t_forward(h, 0)
        for d in range(1, n_wa):
            x_copy(0, h, d, w).start()

        @pl.when(h >= 1)
        def _():
            for d in range(1, n_wa):
                x_copy(1, h - 1, d, w).start()

        return c

    lax.fori_loop(0, heads, open_head, 0)
    for d in range(1, n_wa):
        x_copy(1, heads - 1, d, w).start()

    def feed(h):
        t_forward(h, 1)
        x_wait(0, h)
        if near:
            @pl.when(h < near)
            def _():
                @pl.when(has_next)
                def _():
                    z_copy(0, h).start()

                @pl.when(has_prev)
                def _():
                    z_copy(1, h).start()

    def compute(h, halo):
        ext_t = window[0, w * heads + h]
        ext_w = window[2, w * heads + h]
        base = 0 if halo else own_base
        span = text_base + text - base
        keys = pl.ds(base, span)
        spread = (
            jnp.logical_and(has_prev, ext_t >= 1),
            jnp.logical_and(has_next, ext_t >= 1),
            None,
        )
        for qb in range(slab // q_block):
            q_rows = pl.ds(qb * q_block, q_block)
            q = qg[h, 0, q_rows]
            g = qg[h, 1, q_rows]
            query_col = qb * (q_block // cells) + lax.broadcasted_iota(jnp.int32, (1, q_block), 1) // cells
            top = jnp.full((1, q_block), NEG, F32)
            blocks = []
            for j in range(0 if halo else 2, 3):
                far = 0.0 if spread[j] is None else jnp.where(spread[j], 0.0, NEG)
                for c in range(n_wa):
                    bias = jnp.where(jnp.abs(query_col - c) <= ext_w, far, NEG)
                    blocks.append(((j * n_wa + c) * cells, cells, bias))
            for b in range(0, text, KEY_BLOCK):
                blocks.append((text_base + b, min(KEY_BLOCK, text - b), None))
            for start, size, bias in blocks:
                sc = dot_nt(kv[h, 0, pl.ds(start, size)], q) * scale
                if bias is not None:
                    sc = sc + bias
                st[pl.ds(start, size)] = sc
                top = jnp.maximum(top, jnp.max(sc, axis=0, keepdims=True))
            total = jnp.zeros((1, q_block), F32)
            for start, size, _ in blocks:
                p = jnp.exp(st[pl.ds(start, size)] - top)
                st[pl.ds(start, size)] = p
                total = total + jnp.sum(p, axis=0, keepdims=True)
            inv = 1.0 / total
            for start, size, _ in blocks:
                wb[pl.ds(start, size)] = (st[pl.ds(start, size)] * inv).astype(BF16)
            attended = dot_tn(wb[keys], kv[h, 1, keys]).astype(BF16)
            oq[h, 0, q_rows] = attended
            product = g.astype(F32) * attended.astype(F32)
            delta = jnp.sum(product.T, axis=0, keepdims=True)
            inv_scale = inv * scale
            for start, size, _ in blocks:
                dp = dot_nt(kv[h, 1, pl.ds(start, size)], g)
                db[pl.ds(start, size)] = (st[pl.ds(start, size)] * inv_scale * (dp - delta)).astype(BF16)
            oq[h, 1, q_rows] = dot_tn(db[keys], kv[h, 0, keys]).astype(BF16)

            def put(ref, index, value):
                if qb == 0:
                    ref[index] = value.astype(ref.dtype)
                else:
                    ref[index] = (ref[index].astype(F32) + value).astype(ref.dtype)

            for kind, (left, right) in enumerate(((db, q), (wb, g))):
                part = jnp.dot(left[pl.ds(text_base, text)], right, preferred_element_type=F32)
                put(t_part, (h, kind), part)
                part = jnp.dot(left[pl.ds(own_base, slab)], right, preferred_element_type=F32)
                put(own_part, (h, kind), part)
                for side in range(2 if halo else 0):
                    part = jnp.dot(left[pl.ds(side * slab, slab)], right, preferred_element_type=F32)
                    put(z_part, (side, h, kind), part)

    def y_src(pair, h, owner):
        return (oq if pair == 0 else fin).at[h, :, rows_of(0, owner, cells)]

    def y_dst(pair, h, group):
        return res_out.at[group * heads + h, pl.ds(2 * pair, 2)]

    def y_copy(pair, h, d, source):
        return remote(
            y_src(pair, h, peer_of(d)), y_dst(pair, h, source),
            y_send.at[d - 1, pair], y_recv.at[d - 1, pair], wa=peer_of(d),
        )

    def y_local(pair, h):
        return pltpu.make_async_copy(y_src(pair, h, w), y_dst(pair, h, w), y_loc.at[pair])

    def g_copy(side, h, block):
        return remote(
            t_part.at[h, :, rows_of(0, block, text_rows)], t_got.at[side, h, block],
            g_send.at[side, block], g_recv.at[side, h, block],
            sa=after if side == 0 else before,
        )

    def g_valid(side, block):
        return s < block if side == 0 else s > block

    def g_relay(side, h):
        inward = has_prev if side == 0 else has_next
        blocks = range(n_sa)
        for block in (reversed(blocks) if side == 0 else blocks):
            @pl.when(g_valid(side, block))
            def _():
                @pl.when(inward)
                def _():
                    g_copy(side, h, block).wait_recv()
                    rows = pl.ds(block * text_rows, text_rows)
                    joined = t_part[h, :, rows].astype(F32) + t_got[side, h, block].astype(F32)
                    t_part[h, :, rows] = joined.astype(BF16)

                g_copy(side, h, block).start()

    def f_copy(h, d, source):
        return remote(
            t_fin.at[h], text_out.at[source * heads + h], f_send.at[d - 1], f_recv.at[d - 1], wa=peer_of(d),
        )

    def f_local(h):
        return pltpu.make_async_copy(t_fin.at[h], text_out.at[w * heads + h], f_loc)

    def finish(h, d):
        rows = rows_of(0, peer_of(d), cells)
        if near:
            @pl.when(jnp.logical_and(h < near, has_next))
            def _():
                r_copy(0, h, d).wait_recv()

            @pl.when(jnp.logical_and(h < near, has_prev))
            def _():
                r_copy(1, h, d).wait_recv()

            @pl.when(h < near)
            def _():
                whole = own_part[h, :, rows] + z_got[0, h, :, rows].astype(F32) + z_got[1, h, :, rows].astype(F32)
                fin[h, :, rows] = whole.astype(BF16)

        if near < heads:
            @pl.when(h >= near)
            def _():
                fin[h, :, rows] = own_part[h, :, rows].astype(BF16)

        if d:
            y_copy(1, h, d, w).start()
        else:
            y_local(1, h).start()

    def finish_text(h):
        @pl.when(has_prev)
        def _():
            g_copy(0, h, s).wait_recv()

        @pl.when(has_next)
        def _():
            g_copy(1, h, s).wait_recv()

        whole = t_part[h, :, rows_of(0, s, text_rows)].astype(F32)
        whole = whole + t_got[0, h, s].astype(F32) + t_got[1, h, s].astype(F32)
        t_fin[h] = whole.astype(BF16)
        for d in range(1, n_wa):
            f_copy(h, d, w).start()
        f_local(h).start()

    def attend(h):
        x_wait(1, h)

        @pl.when(jnp.logical_not(has_next))
        def _():
            for hop in range(n_sa - 1):
                t_in(0, h, hop).wait_recv()

        @pl.when(jnp.logical_not(has_prev))
        def _():
            for hop in range(n_sa - 1):
                t_in(1, h, hop).wait_recv()

        if near:
            @pl.when(jnp.logical_and(h < near, has_prev))
            def _():
                z_copy(0, h).wait_recv()

            @pl.when(jnp.logical_and(h < near, has_next))
            def _():
                z_copy(1, h).wait_recv()

            @pl.when(h < near)
            def _():
                compute(h, True)

        if near < heads:
            @pl.when(h >= near)
            def _():
                compute(h, False)

        for d in range(1, n_wa):
            y_copy(0, h, d, w).start()
        y_local(0, h).start()

    def give_back(h, d):
        @pl.when(has_prev)
        def _():
            r_copy(0, h, d).start()

        @pl.when(has_next)
        def _():
            r_copy(1, h, d).start()

    def at(h, count, body):
        @pl.when(jnp.logical_and(h >= 0, h < count))
        def _():
            body(h)

    def step(turn, c):
        i = turn - FEED
        at(turn, heads, feed)
        for hop in range(2, n_sa - 1):
            at(i + FEED - 1, heads, lambda h: t_forward(h, hop))
        at(i, heads, attend)
        for side in range(2):
            at(i - (s if side == 0 else n_sa - 1 - s), heads, lambda h: g_relay(side, h))
        if near:
            for d in range(1, n_wa):
                at(i - RETURN_LAG, near, lambda h: give_back(h, d))
            at(i - RETURN_LAG - 1, near, lambda h: give_back(h, 0))
        for d in range(1, n_wa):
            at(i - FINISH_LAG, heads, lambda h: finish(h, d))
        at(i - FINISH_LAG - 1, heads, lambda h: finish(h, 0))
        at(i - (n_sa - 1), heads, finish_text)
        return c

    lax.fori_loop(0, FEED + heads + max(n_sa - 1, FINISH_LAG + 1), step, 0)

    every = pl.ds(0, heads)
    for d in range(1, n_wa):
        remote(stage.at[d - 1], stage.at[d - 1], x_send.at[d - 1], x_recv.at[d - 1, 0, 0], wa=peer_of(d)).wait_send()
        for pair in range(2):
            for source, wait in ((w, "wait_send"), (source_of(d), "wait_recv")):
                group = res_out.at[pl.ds(source * heads, heads), pl.ds(2 * pair, 2)]
                getattr(remote(group, group, y_send.at[d - 1, pair], y_recv.at[d - 1, pair], wa=peer_of(d)), wait)()
        for source, wait in ((w, "wait_send"), (source_of(d), "wait_recv")):
            group = text_out.at[pl.ds(source * heads, heads)]
            getattr(remote(group, group, f_send.at[d - 1], f_recv.at[d - 1], wa=peer_of(d)), wait)()
    for pair in range(2):
        group = res_out.at[pl.ds(w * heads, heads), pl.ds(2 * pair, 2)]
        pltpu.make_async_copy(group, group, y_loc.at[pair]).wait()
    group = text_out.at[pl.ds(w * heads, heads)]
    pltpu.make_async_copy(group, group, f_loc).wait()
    for side in range(2):
        there = after if side == 0 else before
        block = kv.at[every, :, pl.ds(text_base, text_rows)]
        for hop in range(n_sa - 1):
            @pl.when(t_valid(side, hop))
            def _():
                remote(block, block, t_send.at[side, hop], t_recv.at[side, 0, hop], sa=there).wait_send()

        for owner in range(n_sa):
            @pl.when(g_valid(side, owner))
            def _():
                remote(block, block, g_send.at[side, owner], g_recv.at[side, 0, owner], sa=there).wait_send()

        if near:
            halo = kv.at[pl.ds(0, near), :, pl.ds(0, slab)]

            @pl.when(has_next if side == 0 else has_prev)
            def _():
                remote(halo, halo, z_send.at[side], z_recv.at[side, 0], sa=there).wait_send()

            @pl.when(has_prev if side == 0 else has_next)
            def _():
                remote(halo, halo, r_send.at[side], r_recv.at[side, 0, 0], sa=before if side == 0 else after).wait_send()


def hand_over(res, words, o_out, dq_out, dk_out, dv_out, dtk_out, dtv_out):
    def place(slot, c):
        columns = pl.ds(pl.multiple_of(slot * HEAD_DIM, HEAD_DIM), HEAD_DIM)
        for kind, out in enumerate((o_out, dq_out, dk_out, dv_out)):
            out[:, columns] = res[slot, kind]
        for kind, out in enumerate((dtk_out, dtv_out)):
            out[:, columns] = words[slot, kind].astype(F32)
        return c

    lax.fori_loop(0, res.shape[0], place, 0)


def attention(n_sa, n_wa, near, window, queries, keys, values, out_grad, text_keys, text_values):
    cells, channels = queries.shape
    heads = channels // HEAD_DIM // n_wa
    text_rows = text_keys.shape[0]
    slab, text = n_wa * cells, n_sa * text_rows
    n_keys = 3 * slab + text
    q_block = min(slab, Q_BLOCK)
    halo = max(near, 1)
    dma = pltpu.SemaphoreType.DMA
    anywhere = pl.BlockSpec(memory_space=pl.ANY)
    in_smem = pl.BlockSpec(memory_space=pltpu.SMEM)
    return pl.pallas_call(
        functools.partial(kernel, n_sa, n_wa, heads, near, cells, text_rows),
        out_shape=(
            jax.ShapeDtypeStruct((n_wa * heads, 4, cells, HEAD_DIM), BF16),
            jax.ShapeDtypeStruct((n_wa * heads, 2, text_rows, HEAD_DIM), BF16),
        ),
        in_specs=[in_smem] + [anywhere] * 6,
        out_specs=(anywhere,) * 2,
        scratch_shapes=[
            pltpu.VMEM((4, cells, channels), BF16),
            pltpu.VMEM((2, text_rows, channels), BF16),
            pltpu.VMEM((n_wa - 1, heads, 4, cells, HEAD_DIM), BF16),
            pltpu.VMEM((heads, 2, n_keys, HEAD_DIM), BF16),
            pltpu.VMEM((heads, 2, slab, HEAD_DIM), BF16),
            pltpu.VMEM((heads, 2, slab, HEAD_DIM), BF16),
            pltpu.VMEM((heads, 2, slab, HEAD_DIM), F32),
            pltpu.VMEM((2, halo, 2, slab, HEAD_DIM), BF16),
            pltpu.VMEM((2, halo, 2, slab, HEAD_DIM), BF16),
            pltpu.VMEM((heads, 2, slab, HEAD_DIM), BF16),
            pltpu.VMEM((heads, 2, text, HEAD_DIM), BF16),
            pltpu.VMEM((2, heads, n_sa, 2, text_rows, HEAD_DIM), BF16),
            pltpu.VMEM((heads, 2, text_rows, HEAD_DIM), BF16),
            pltpu.VMEM((n_keys, q_block), F32),
            pltpu.VMEM((n_keys, q_block), BF16),
            pltpu.VMEM((n_keys, q_block), BF16),
            dma((6,)),
            dma((n_wa - 1,)),
            dma((n_wa - 1, heads, 2)),
            dma((2, n_sa - 1)),
            dma((2, heads, n_sa - 1)),
            dma((2,)),
            dma((2, halo)),
            dma((2,)),
            dma((2, halo, n_wa)),
            dma((n_wa - 1, 2)),
            dma((n_wa - 1, 2)),
            dma((2,)),
            dma((2, n_sa)),
            dma((2, heads, n_sa)),
            dma((n_wa - 1,)),
            dma((n_wa - 1,)),
            dma(()),
        ],
        compiler_params=pltpu.CompilerParams(
            collective_id=near, has_side_effects=True, vmem_limit_bytes=VMEM_LIMIT
        ),
    )(window, keys, values, queries, out_grad, text_keys, text_values)


VMEM_LIMIT = 60 * 1024 * 1024


def shards(queries, keys, values, text_keys, text_values, out_grad, window_ext):
    n_sa, n_wa = lax.axis_size("sa"), lax.axis_size("wa")
    grid = queries.shape
    channels = grid[-1]
    cells = grid[0] * grid[1] * grid[2]
    text_rows = text_keys.shape[0]
    flat = (cells, channels)
    heads = channels // HEAD_DIM // n_wa
    res, words = attention(
        n_sa, n_wa, heads, window_ext.T, queries.reshape(flat), keys.reshape(flat),
        values.reshape(flat), out_grad.reshape(flat), text_keys, text_values,
    )
    in_vmem = pl.BlockSpec(memory_space=pltpu.VMEM)
    outs = pl.pallas_call(
        hand_over,
        out_shape=(jax.ShapeDtypeStruct(flat, BF16),) * 4
        + (jax.ShapeDtypeStruct((text_rows, channels), F32),) * 2,
        in_specs=[in_vmem] * 2,
        out_specs=(in_vmem,) * 6,
    )(res, words)
    return tuple(out.reshape(grid) for out in outs[:4]) + tuple(outs[4:])


def solution(mesh):
    cell = P(("clips", "sa"), None, "wa", "hp")
    text = P(("clips", "sa"), "hp")
    return jax.shard_map(
        shards,
        mesh=mesh,
        in_specs=(cell, cell, cell, text, text, cell, P("hp", None)),
        out_specs=(cell, cell, cell, cell, text, text),
        check_vma=False,
    )
```

```python
import functools

import jax
import jax.numpy as jnp
from jax import lax
from jax.experimental import pallas as pl
from jax.experimental.pallas import tpu as pltpu
from jax.sharding import PartitionSpec as P

HEAD_DIM = 128
NEG = -1e30
MESH = pl.DeviceIdType.MESH
F32 = jnp.float32
BF16 = jnp.bfloat16
KEY_BLOCK = 256
Q_BLOCK = 256
FEED = 3
RETURN_LAG = 2
FINISH_LAG = 4


def dot_nt(a, b):
    return lax.dot_general(a, b, (((1,), (1,)), ((), ())), preferred_element_type=F32)


def dot_tn(a, b):
    return lax.dot_general(a, b, (((0,), (0,)), ((), ())), preferred_element_type=F32)


def kernel(
    n_sa, n_wa, heads, near, cells, text_rows,
    window, order, k_in, v_in, q_in, g_in, tk_in, tv_in,
    res_out, text_out,
    cell_in, words_in, by_head, words_by_head, stage, kv, qg, oq, own_part, z_part, z_got, fin, t_part, t_got, t_fin, st, wb, db,
    load, x_send, x_recv, t_send, t_recv, z_send, z_recv,
    r_send, r_recv, y_send, y_recv, y_loc, g_send, g_recv, f_send, f_recv, f_loc,
):
    s = lax.axis_index("sa")
    w = lax.axis_index("wa")
    slab = n_wa * cells
    text = n_sa * text_rows
    own_base = 2 * slab
    text_base = 3 * slab
    scale = HEAD_DIM ** (-0.5)
    has_prev, has_next = s > 0, s < n_sa - 1
    before, after = lax.rem(s + n_sa - 1, n_sa), lax.rem(s + 1, n_sa)
    q_block = min(slab, Q_BLOCK)

    def rows_of(base, index, size):
        return pl.ds(pl.multiple_of(base + index * size, 16), size)

    def remote(src, dst, send, recv, **where):
        return pltpu.make_async_remote_copy(
            src_ref=src, dst_ref=dst, send_sem=send, recv_sem=recv,
            device_id=where, device_id_type=MESH,
        )

    def peer_of(d):
        return lax.rem(w + d, n_wa)

    def source_of(d):
        return lax.rem(w + n_wa - d, n_wa)

    loads = [
        pltpu.make_async_copy(ref, cell_in.at[kind], load.at[kind])
        for kind, ref in enumerate((k_in, v_in, q_in, g_in))
    ] + [
        pltpu.make_async_copy(ref, words_in.at[kind], load.at[4 + kind])
        for kind, ref in enumerate((tk_in, tv_in))
    ]
    for copy in loads:
        copy.start()

    barrier = pltpu.get_barrier_semaphore()
    for d in range(1, n_wa):
        pl.semaphore_signal(barrier, inc=1, device_id={"wa": peer_of(d)}, device_id_type=MESH)

    @pl.when(has_prev)
    def _():
        pl.semaphore_signal(barrier, inc=1, device_id={"sa": before}, device_id_type=MESH)

    @pl.when(has_next)
    def _():
        pl.semaphore_signal(barrier, inc=1, device_id={"sa": after}, device_id_type=MESH)

    def clear_side(side):
        def clear(h, c):
            if near:
                @pl.when(h < near)
                def _():
                    kv[h, :, pl.ds(side * slab, slab)] = jnp.zeros((2, slab, HEAD_DIM), BF16)
                    z_got[1 - side, h] = jnp.zeros((2, slab, HEAD_DIM), BF16)

            t_got[side, h, 0 if side == 0 else n_sa - 1] = jnp.zeros((2, text_rows, HEAD_DIM), BF16)
            return c

        lax.fori_loop(0, heads, clear, 0)

    @pl.when(jnp.logical_not(has_prev))
    def _():
        clear_side(0)

    @pl.when(jnp.logical_not(has_next))
    def _():
        clear_side(1)

    for copy in loads:
        copy.wait()

    def spread_heads(n, c):
        lanes = pl.ds(pl.multiple_of(n * HEAD_DIM, HEAD_DIM), HEAD_DIM)
        for kind in range(4):
            by_head[n, kind] = cell_in[kind, :, lanes]
        for kind in range(2):
            words_by_head[n, kind] = words_in[kind, :, lanes]
        return c

    lax.fori_loop(0, n_wa * heads, spread_heads, 0)

    def arrange(h, c):
        here = order[w * heads + h]
        kv[h, :, rows_of(text_base, s, text_rows)] = words_by_head[here]
        block = by_head[here]
        kv[h, :, rows_of(own_base, w, cells)] = block[:2]
        qg[h, :, rows_of(0, w, cells)] = block[2:]
        for d in range(1, n_wa):
            stage[d - 1, h] = by_head[order[peer_of(d) * heads + h]]
        return c

    lax.fori_loop(0, heads, arrange, 0)

    neighbours = n_wa - 1 + has_prev.astype(jnp.int32) + has_next.astype(jnp.int32)
    pl.semaphore_wait(barrier, neighbours)

    def x_slot(pair, h, source):
        if pair == 0:
            return kv.at[h, :, rows_of(own_base, source, cells)]
        return qg.at[h, :, rows_of(0, source, cells)]

    def x_copy(pair, h, d, source):
        return remote(
            stage.at[d - 1, h, pl.ds(2 * pair, 2)], x_slot(pair, h, source),
            x_send.at[d - 1], x_recv.at[d - 1, h, pair], wa=peer_of(d),
        )

    def x_wait(pair, h):
        for d in range(1, n_wa):
            x_copy(pair, h, d, source_of(d)).wait_recv()

    def t_slot(h, block):
        return kv.at[h, :, rows_of(text_base, block, text_rows)]

    def t_hop(side, h, hop, block):
        return remote(
            t_slot(h, block), t_slot(h, block), t_send.at[side, hop], t_recv.at[side, h, hop],
            sa=after if side == 0 else before,
        )

    def t_out(side, h, hop):
        return t_hop(side, h, hop, s - hop if side == 0 else s + hop)

    def t_in(side, h, hop):
        return t_hop(side, h, hop, s - 1 - hop if side == 0 else s + 1 + hop)

    def t_valid(side, hop):
        if side == 0:
            return jnp.logical_and(s >= hop, has_next)
        return jnp.logical_and(s + hop < n_sa, has_prev)

    def t_forward(h, hop):
        for side in range(2):
            @pl.when(t_valid(side, hop))
            def _():
                if hop:
                    t_in(side, h, hop - 1).wait_recv()
                t_out(side, h, hop).start()

    def z_copy(side, h):
        return remote(
            kv.at[h, :, pl.ds(own_base, slab)], kv.at[h, :, pl.ds(side * slab, slab)],
            z_send.at[side], z_recv.at[side, h], sa=after if side == 0 else before,
        )

    def r_copy(side, h, d):
        rows = rows_of(0, peer_of(d), cells)
        return remote(
            z_part.at[side, h, :, rows], z_got.at[side, h, :, rows],
            r_send.at[side], r_recv.at[side, h, d], sa=before if side == 0 else after,
        )

    def open_head(h, c):
        t_forward(h, 0)
        for d in range(1, n_wa):
            x_copy(0, h, d, w).start()

        @pl.when(h >= 1)
        def _():
            for d in range(1, n_wa):
                x_copy(1, h - 1, d, w).start()

        return c

    lax.fori_loop(0, heads, open_head, 0)
    for d in range(1, n_wa):
        x_copy(1, heads - 1, d, w).start()

    def feed(h):
        t_forward(h, 1)
        x_wait(0, h)
        if near:
            @pl.when(h < near)
            def _():
                @pl.when(has_next)
                def _():
                    z_copy(0, h).start()

                @pl.when(has_prev)
                def _():
                    z_copy(1, h).start()

    def compute(h, halo):
        ext_t = window[0, order[w * heads + h]]
        ext_w = window[2, order[w * heads + h]]
        base = 0 if halo else own_base
        span = text_base + text - base
        keys = pl.ds(base, span)
        spread = (
            jnp.logical_and(has_prev, ext_t >= 1),
            jnp.logical_and(has_next, ext_t >= 1),
            None,
        )
        for qb in range(slab // q_block):
            q_rows = pl.ds(qb * q_block, q_block)
            q = qg[h, 0, q_rows]
            g = qg[h, 1, q_rows]
            query_col = qb * (q_block // cells) + lax.broadcasted_iota(jnp.int32, (1, q_block), 1) // cells
            top = jnp.full((1, q_block), NEG, F32)
            blocks = []
            for j in range(0 if halo else 2, 3):
                far = 0.0 if spread[j] is None else jnp.where(spread[j], 0.0, NEG)
                for c in range(n_wa):
                    bias = jnp.where(jnp.abs(query_col - c) <= ext_w, far, NEG)
                    blocks.append(((j * n_wa + c) * cells, cells, bias))
            for b in range(0, text, KEY_BLOCK):
                blocks.append((text_base + b, min(KEY_BLOCK, text - b), None))
            for start, size, bias in blocks:
                sc = dot_nt(kv[h, 0, pl.ds(start, size)], q) * scale
                if bias is not None:
                    sc = sc + bias
                st[pl.ds(start, size)] = sc
                top = jnp.maximum(top, jnp.max(sc, axis=0, keepdims=True))
            total = jnp.zeros((1, q_block), F32)
            for start, size, _ in blocks:
                p = jnp.exp(st[pl.ds(start, size)] - top)
                st[pl.ds(start, size)] = p
                total = total + jnp.sum(p, axis=0, keepdims=True)
            inv = 1.0 / total
            for start, size, _ in blocks:
                wb[pl.ds(start, size)] = (st[pl.ds(start, size)] * inv).astype(BF16)
            attended = dot_tn(wb[keys], kv[h, 1, keys]).astype(BF16)
            oq[h, 0, q_rows] = attended
            product = g.astype(F32) * attended.astype(F32)
            delta = jnp.sum(product.T, axis=0, keepdims=True)
            inv_scale = inv * scale
            for start, size, _ in blocks:
                dp = dot_nt(kv[h, 1, pl.ds(start, size)], g)
                db[pl.ds(start, size)] = (st[pl.ds(start, size)] * inv_scale * (dp - delta)).astype(BF16)
            oq[h, 1, q_rows] = dot_tn(db[keys], kv[h, 0, keys]).astype(BF16)

            def put(ref, index, value):
                if qb == 0:
                    ref[index] = value.astype(ref.dtype)
                else:
                    ref[index] = (ref[index].astype(F32) + value).astype(ref.dtype)

            for kind, (left, right) in enumerate(((db, q), (wb, g))):
                part = jnp.dot(left[pl.ds(text_base, text)], right, preferred_element_type=F32)
                put(t_part, (h, kind), part)
                part = jnp.dot(left[pl.ds(own_base, slab)], right, preferred_element_type=F32)
                put(own_part, (h, kind), part)
                for side in range(2 if halo else 0):
                    part = jnp.dot(left[pl.ds(side * slab, slab)], right, preferred_element_type=F32)
                    put(z_part, (side, h, kind), part)

    def y_src(pair, h, owner):
        return (oq if pair == 0 else fin).at[h, :, rows_of(0, owner, cells)]

    def y_dst(pair, h, group):
        return res_out.at[group * heads + h, pl.ds(2 * pair, 2)]

    def y_copy(pair, h, d, source):
        return remote(
            y_src(pair, h, peer_of(d)), y_dst(pair, h, source),
            y_send.at[d - 1, pair], y_recv.at[d - 1, pair], wa=peer_of(d),
        )

    def y_local(pair, h):
        return pltpu.make_async_copy(y_src(pair, h, w), y_dst(pair, h, w), y_loc.at[pair])

    def g_copy(side, h, block):
        return remote(
            t_part.at[h, :, rows_of(0, block, text_rows)], t_got.at[side, h, block],
            g_send.at[side, block], g_recv.at[side, h, block],
            sa=after if side == 0 else before,
        )

    def g_valid(side, block):
        return s < block if side == 0 else s > block

    def g_relay(side, h):
        inward = has_prev if side == 0 else has_next
        blocks = range(n_sa)
        for block in (reversed(blocks) if side == 0 else blocks):
            @pl.when(g_valid(side, block))
            def _():
                @pl.when(inward)
                def _():
                    g_copy(side, h, block).wait_recv()
                    rows = pl.ds(block * text_rows, text_rows)
                    joined = t_part[h, :, rows].astype(F32) + t_got[side, h, block].astype(F32)
                    t_part[h, :, rows] = joined.astype(BF16)

                g_copy(side, h, block).start()

    def f_copy(h, d, source):
        return remote(
            t_fin.at[h], text_out.at[source * heads + h], f_send.at[d - 1], f_recv.at[d - 1], wa=peer_of(d),
        )

    def f_local(h):
        return pltpu.make_async_copy(t_fin.at[h], text_out.at[w * heads + h], f_loc)

    def finish(h, d):
        rows = rows_of(0, peer_of(d), cells)
        if near:
            @pl.when(jnp.logical_and(h < near, has_next))
            def _():
                r_copy(0, h, d).wait_recv()

            @pl.when(jnp.logical_and(h < near, has_prev))
            def _():
                r_copy(1, h, d).wait_recv()

            @pl.when(h < near)
            def _():
                whole = own_part[h, :, rows] + z_got[0, h, :, rows].astype(F32) + z_got[1, h, :, rows].astype(F32)
                fin[h, :, rows] = whole.astype(BF16)

        if near < heads:
            @pl.when(h >= near)
            def _():
                fin[h, :, rows] = own_part[h, :, rows].astype(BF16)

        if d:
            y_copy(1, h, d, w).start()
        else:
            y_local(1, h).start()

    def finish_text(h):
        @pl.when(has_prev)
        def _():
            g_copy(0, h, s).wait_recv()

        @pl.when(has_next)
        def _():
            g_copy(1, h, s).wait_recv()

        whole = t_part[h, :, rows_of(0, s, text_rows)].astype(F32)
        whole = whole + t_got[0, h, s].astype(F32) + t_got[1, h, s].astype(F32)
        t_fin[h] = whole.astype(BF16)
        for d in range(1, n_wa):
            f_copy(h, d, w).start()
        f_local(h).start()

    def attend(h):
        x_wait(1, h)

        @pl.when(jnp.logical_not(has_next))
        def _():
            for hop in range(n_sa - 1):
                t_in(0, h, hop).wait_recv()

        @pl.when(jnp.logical_not(has_prev))
        def _():
            for hop in range(n_sa - 1):
                t_in(1, h, hop).wait_recv()

        if near:
            @pl.when(jnp.logical_and(h < near, has_prev))
            def _():
                z_copy(0, h).wait_recv()

            @pl.when(jnp.logical_and(h < near, has_next))
            def _():
                z_copy(1, h).wait_recv()

            @pl.when(h < near)
            def _():
                compute(h, True)

        if near < heads:
            @pl.when(h >= near)
            def _():
                compute(h, False)

        for d in range(1, n_wa):
            y_copy(0, h, d, w).start()
        y_local(0, h).start()

    def give_back(h, d):
        @pl.when(has_prev)
        def _():
            r_copy(0, h, d).start()

        @pl.when(has_next)
        def _():
            r_copy(1, h, d).start()

    def at(h, count, body):
        @pl.when(jnp.logical_and(h >= 0, h < count))
        def _():
            body(h)

    def step(turn, c):
        i = turn - FEED
        at(turn, heads, feed)
        for hop in range(2, n_sa - 1):
            at(i + FEED - 1, heads, lambda h: t_forward(h, hop))
        at(i, heads, attend)
        for side in range(2):
            at(i - (s if side == 0 else n_sa - 1 - s), heads, lambda h: g_relay(side, h))
        if near:
            for d in range(1, n_wa):
                at(i - RETURN_LAG, near, lambda h: give_back(h, d))
            at(i - RETURN_LAG - 1, near, lambda h: give_back(h, 0))
        for d in range(1, n_wa):
            at(i - FINISH_LAG, heads, lambda h: finish(h, d))
        at(i - FINISH_LAG - 1, heads, lambda h: finish(h, 0))
        at(i - (n_sa - 1), heads, finish_text)
        return c

    lax.fori_loop(0, FEED + heads + max(n_sa - 1, FINISH_LAG + 1), step, 0)

    every = pl.ds(0, heads)
    for d in range(1, n_wa):
        remote(stage.at[d - 1], stage.at[d - 1], x_send.at[d - 1], x_recv.at[d - 1, 0, 0], wa=peer_of(d)).wait_send()
        for pair in range(2):
            for source, wait in ((w, "wait_send"), (source_of(d), "wait_recv")):
                group = res_out.at[pl.ds(source * heads, heads), pl.ds(2 * pair, 2)]
                getattr(remote(group, group, y_send.at[d - 1, pair], y_recv.at[d - 1, pair], wa=peer_of(d)), wait)()
        for source, wait in ((w, "wait_send"), (source_of(d), "wait_recv")):
            group = text_out.at[pl.ds(source * heads, heads)]
            getattr(remote(group, group, f_send.at[d - 1], f_recv.at[d - 1], wa=peer_of(d)), wait)()
    for pair in range(2):
        group = res_out.at[pl.ds(w * heads, heads), pl.ds(2 * pair, 2)]
        pltpu.make_async_copy(group, group, y_loc.at[pair]).wait()
    group = text_out.at[pl.ds(w * heads, heads)]
    pltpu.make_async_copy(group, group, f_loc).wait()
    for side in range(2):
        there = after if side == 0 else before
        block = kv.at[every, :, pl.ds(text_base, text_rows)]
        for hop in range(n_sa - 1):
            @pl.when(t_valid(side, hop))
            def _():
                remote(block, block, t_send.at[side, hop], t_recv.at[side, 0, hop], sa=there).wait_send()

        for owner in range(n_sa):
            @pl.when(g_valid(side, owner))
            def _():
                remote(block, block, g_send.at[side, owner], g_recv.at[side, 0, owner], sa=there).wait_send()

        if near:
            halo = kv.at[pl.ds(0, near), :, pl.ds(0, slab)]

            @pl.when(has_next if side == 0 else has_prev)
            def _():
                remote(halo, halo, z_send.at[side], z_recv.at[side, 0], sa=there).wait_send()

            @pl.when(has_prev if side == 0 else has_next)
            def _():
                remote(halo, halo, r_send.at[side], r_recv.at[side, 0, 0], sa=before if side == 0 else after).wait_send()


def hand_over(res, words, o_out, dq_out, dk_out, dv_out, dtk_out, dtv_out):
    def place(slot, c):
        columns = pl.ds(pl.multiple_of(slot * HEAD_DIM, HEAD_DIM), HEAD_DIM)
        for kind, out in enumerate((o_out, dq_out, dk_out, dv_out)):
            out[:, columns] = res[slot, kind]
        for kind, out in enumerate((dtk_out, dtv_out)):
            out[:, columns] = words[slot, kind].astype(F32)
        return c

    lax.fori_loop(0, res.shape[0], place, 0)


def attention(n_sa, n_wa, near, window, order, queries, keys, values, out_grad, text_keys, text_values):
    cells, channels = queries.shape
    heads = channels // HEAD_DIM // n_wa
    text_rows = text_keys.shape[0]
    slab, text = n_wa * cells, n_sa * text_rows
    n_keys = 3 * slab + text
    q_block = min(slab, Q_BLOCK)
    halo = max(near, 1)
    dma = pltpu.SemaphoreType.DMA
    anywhere = pl.BlockSpec(memory_space=pl.ANY)
    in_smem = pl.BlockSpec(memory_space=pltpu.SMEM)
    return pl.pallas_call(
        functools.partial(kernel, n_sa, n_wa, heads, near, cells, text_rows),
        out_shape=(
            jax.ShapeDtypeStruct((n_wa * heads, 4, cells, HEAD_DIM), BF16),
            jax.ShapeDtypeStruct((n_wa * heads, 2, text_rows, HEAD_DIM), BF16),
        ),
        in_specs=[in_smem] * 2 + [anywhere] * 6,
        out_specs=(anywhere,) * 2,
        scratch_shapes=[
            pltpu.VMEM((4, cells, channels), BF16),
            pltpu.VMEM((2, text_rows, channels), BF16),
            pltpu.VMEM((n_wa * heads, 4, cells, HEAD_DIM), BF16),
            pltpu.VMEM((n_wa * heads, 2, text_rows, HEAD_DIM), BF16),
            pltpu.VMEM((n_wa - 1, heads, 4, cells, HEAD_DIM), BF16),
            pltpu.VMEM((heads, 2, n_keys, HEAD_DIM), BF16),
            pltpu.VMEM((heads, 2, slab, HEAD_DIM), BF16),
            pltpu.VMEM((heads, 2, slab, HEAD_DIM), BF16),
            pltpu.VMEM((heads, 2, slab, HEAD_DIM), F32),
            pltpu.VMEM((2, halo, 2, slab, HEAD_DIM), BF16),
            pltpu.VMEM((2, halo, 2, slab, HEAD_DIM), BF16),
            pltpu.VMEM((heads, 2, slab, HEAD_DIM), BF16),
            pltpu.VMEM((heads, 2, text, HEAD_DIM), BF16),
            pltpu.VMEM((2, heads, n_sa, 2, text_rows, HEAD_DIM), BF16),
            pltpu.VMEM((heads, 2, text_rows, HEAD_DIM), BF16),
            pltpu.VMEM((n_keys, q_block), F32),
            pltpu.VMEM((n_keys, q_block), BF16),
            pltpu.VMEM((n_keys, q_block), BF16),
            dma((6,)),
            dma((n_wa - 1,)),
            dma((n_wa - 1, heads, 2)),
            dma((2, n_sa - 1)),
            dma((2, heads, n_sa - 1)),
            dma((2,)),
            dma((2, halo)),
            dma((2,)),
            dma((2, halo, n_wa)),
            dma((n_wa - 1, 2)),
            dma((n_wa - 1, 2)),
            dma((2,)),
            dma((2, n_sa)),
            dma((2, heads, n_sa)),
            dma((n_wa - 1,)),
            dma((n_wa - 1,)),
            dma(()),
        ],
        compiler_params=pltpu.CompilerParams(
            collective_id=near, has_side_effects=True, vmem_limit_bytes=VMEM_LIMIT
        ),
    )(window, order, keys, values, queries, out_grad, text_keys, text_values)


VMEM_LIMIT = 60 * 1024 * 1024


def shards(queries, keys, values, text_keys, text_values, out_grad, window_ext):
    n_sa, n_wa = lax.axis_size("sa"), lax.axis_size("wa")
    grid = queries.shape
    channels = grid[-1]
    cells = grid[0] * grid[1] * grid[2]
    text_rows = text_keys.shape[0]
    flat = (cells, channels)
    heads = channels // HEAD_DIM // n_wa
    order = jnp.arange(channels // HEAD_DIM, dtype=jnp.int32)
    res, words = attention(
        n_sa, n_wa, heads, window_ext.T, order, queries.reshape(flat), keys.reshape(flat),
        values.reshape(flat), out_grad.reshape(flat), text_keys, text_values,
    )
    in_vmem = pl.BlockSpec(memory_space=pltpu.VMEM)
    outs = pl.pallas_call(
        hand_over,
        out_shape=(jax.ShapeDtypeStruct(flat, BF16),) * 4
        + (jax.ShapeDtypeStruct((text_rows, channels), F32),) * 2,
        in_specs=[in_vmem] * 2,
        out_specs=(in_vmem,) * 6,
    )(res, words)
    return tuple(out.reshape(grid) for out in outs[:4]) + tuple(outs[4:])


def solution(mesh):
    cell = P(("clips", "sa"), None, "wa", "hp")
    text = P(("clips", "sa"), "hp")
    return jax.shard_map(
        shards,
        mesh=mesh,
        in_specs=(cell, cell, cell, text, text, cell, P("hp", None)),
        out_specs=(cell, cell, cell, cell, text, text),
        check_vma=False,
    )
```

```python
import functools

import jax
import jax.numpy as jnp
from jax import lax
from jax.experimental import pallas as pl
from jax.experimental.pallas import tpu as pltpu
from jax.sharding import PartitionSpec as P

HEAD_DIM = 128
NEG = -1e30
MESH = pl.DeviceIdType.MESH
F32 = jnp.float32
BF16 = jnp.bfloat16
KEY_BLOCK = 256
Q_BLOCK = 256
FEED = 3
FAR_LAG = 2


def dot_nt(a, b):
    return lax.dot_general(a, b, (((1,), (1,)), ((), ())), preferred_element_type=F32)


def dot_tn(a, b):
    return lax.dot_general(a, b, (((0,), (0,)), ((), ())), preferred_element_type=F32)


def kernel(
    n_sa, n_wa, heads, near, cells, text_rows,
    window, order, k_in, v_in, q_in, g_in, tk_in, tv_in,
    res_out, text_out,
    cell_in, words_in, by_head, words_by_head, stage, kv, qg, oq, own_part, z_part, z_got, fin, t_part, t_got, t_far, t_fin, st, wb, db,
    load, x_send, x_recv, t_send, t_recv, z_send, z_recv,
    r_send, r_recv, y_send, y_recv, y_loc, g_send, g_recv, f_send, f_recv, f_loc, far_send, far_recv,
):
    s = lax.axis_index("sa")
    w = lax.axis_index("wa")
    slab = n_wa * cells
    text = n_sa * text_rows
    own_base = 2 * slab
    text_base = 3 * slab
    scale = HEAD_DIM ** (-0.5)
    has_prev, has_next = s > 0, s < n_sa - 1
    before, after = lax.rem(s + n_sa - 1, n_sa), lax.rem(s + 1, n_sa)
    q_block = min(slab, Q_BLOCK)
    relayed = near
    return_lag = 2 if near == heads else 1
    finish_lag = return_lag + 2

    def rows_of(base, index, size):
        return pl.ds(pl.multiple_of(base + index * size, 16), size)

    def remote(src, dst, send, recv, **where):
        return pltpu.make_async_remote_copy(
            src_ref=src, dst_ref=dst, send_sem=send, recv_sem=recv,
            device_id=where, device_id_type=MESH,
        )

    def peer_of(d):
        return lax.rem(w + d, n_wa)

    def source_of(d):
        return lax.rem(w + n_wa - d, n_wa)

    loads = [
        pltpu.make_async_copy(ref, cell_in.at[kind], load.at[kind])
        for kind, ref in enumerate((k_in, v_in, q_in, g_in))
    ] + [
        pltpu.make_async_copy(ref, words_in.at[kind], load.at[4 + kind])
        for kind, ref in enumerate((tk_in, tv_in))
    ]
    for copy in loads:
        copy.start()

    barrier = pltpu.get_barrier_semaphore()
    for d in range(1, n_wa):
        pl.semaphore_signal(barrier, inc=1, device_id={"wa": peer_of(d)}, device_id_type=MESH)

    @pl.when(has_prev)
    def _():
        pl.semaphore_signal(barrier, inc=1, device_id={"sa": before}, device_id_type=MESH)

    @pl.when(has_next)
    def _():
        pl.semaphore_signal(barrier, inc=1, device_id={"sa": after}, device_id_type=MESH)

    def clear_side(side):
        def clear(h, c):
            if near:
                @pl.when(h < near)
                def _():
                    kv[h, :, pl.ds(side * slab, slab)] = jnp.zeros((2, slab, HEAD_DIM), BF16)
                    z_got[1 - side, h] = jnp.zeros((2, slab, HEAD_DIM), BF16)

            t_got[side, h, 0 if side == 0 else n_sa - 1] = jnp.zeros((2, text_rows, HEAD_DIM), BF16)
            return c

        lax.fori_loop(0, heads, clear, 0)

    @pl.when(jnp.logical_not(has_prev))
    def _():
        clear_side(0)

    @pl.when(jnp.logical_not(has_next))
    def _():
        clear_side(1)

    for copy in loads:
        copy.wait()

    def spread_heads(n, c):
        lanes = pl.ds(pl.multiple_of(n * HEAD_DIM, HEAD_DIM), HEAD_DIM)
        for kind in range(4):
            by_head[n, kind] = cell_in[kind, :, lanes]
        for kind in range(2):
            words_by_head[n, kind] = words_in[kind, :, lanes]
        return c

    lax.fori_loop(0, n_wa * heads, spread_heads, 0)

    def arrange(h, c):
        here = order[w * heads + h]
        kv[h, :, rows_of(text_base, s, text_rows)] = words_by_head[here]
        block = by_head[here]
        kv[h, :, rows_of(own_base, w, cells)] = block[:2]
        qg[h, :, rows_of(0, w, cells)] = block[2:]
        for d in range(1, n_wa):
            stage[d - 1, h] = by_head[order[peer_of(d) * heads + h]]
        return c

    lax.fori_loop(0, heads, arrange, 0)

    neighbours = n_wa - 1 + has_prev.astype(jnp.int32) + has_next.astype(jnp.int32)
    pl.semaphore_wait(barrier, neighbours)

    def x_slot(pair, h, source):
        if pair == 0:
            return kv.at[h, :, rows_of(own_base, source, cells)]
        return qg.at[h, :, rows_of(0, source, cells)]

    def x_copy(pair, h, d, source):
        return remote(
            stage.at[d - 1, h, pl.ds(2 * pair, 2)], x_slot(pair, h, source),
            x_send.at[d - 1], x_recv.at[d - 1, h, pair], wa=peer_of(d),
        )

    def x_wait(pair, h):
        for d in range(1, n_wa):
            x_copy(pair, h, d, source_of(d)).wait_recv()

    def t_slot(h, block):
        return kv.at[h, :, rows_of(text_base, block, text_rows)]

    def t_hop(side, h, hop, block):
        return remote(
            t_slot(h, block), t_slot(h, block), t_send.at[side, hop], t_recv.at[side, h, hop],
            sa=after if side == 0 else before,
        )

    def t_out(side, h, hop):
        return t_hop(side, h, hop, s - hop if side == 0 else s + hop)

    def t_in(side, h, hop):
        return t_hop(side, h, hop, s - 1 - hop if side == 0 else s + 1 + hop)

    def t_valid(side, hop):
        if side == 0:
            return jnp.logical_and(s >= hop, has_next)
        return jnp.logical_and(s + hop < n_sa, has_prev)

    def t_forward(h, hop):
        for side in range(2):
            @pl.when(t_valid(side, hop))
            def _():
                if hop:
                    t_in(side, h, hop - 1).wait_recv()
                t_out(side, h, hop).start()

    def z_copy(side, h):
        return remote(
            kv.at[h, :, pl.ds(own_base, slab)], kv.at[h, :, pl.ds(side * slab, slab)],
            z_send.at[side], z_recv.at[side, h], sa=after if side == 0 else before,
        )

    def r_copy(side, h, d):
        rows = rows_of(0, peer_of(d), cells)
        return remote(
            z_part.at[side, h, :, rows], z_got.at[side, h, :, rows],
            r_send.at[side], r_recv.at[side, h, d], sa=before if side == 0 else after,
        )

    def open_head(h, c):
        t_forward(h, 0)
        for d in range(1, n_wa):
            x_copy(0, h, d, w).start()

        @pl.when(h >= 1)
        def _():
            for d in range(1, n_wa):
                x_copy(1, h - 1, d, w).start()

        return c

    lax.fori_loop(0, heads, open_head, 0)
    for d in range(1, n_wa):
        x_copy(1, heads - 1, d, w).start()

    def feed(h):
        t_forward(h, 1)
        x_wait(0, h)
        if near:
            @pl.when(h < near)
            def _():
                @pl.when(has_next)
                def _():
                    z_copy(0, h).start()

                @pl.when(has_prev)
                def _():
                    z_copy(1, h).start()

    def compute(h, halo):
        ext_t = window[0, order[w * heads + h]]
        ext_w = window[2, order[w * heads + h]]
        base = 0 if halo else own_base
        span = text_base + text - base
        keys = pl.ds(base, span)
        spread = (
            jnp.logical_and(has_prev, ext_t >= 1),
            jnp.logical_and(has_next, ext_t >= 1),
            None,
        )
        for qb in range(slab // q_block):
            q_rows = pl.ds(qb * q_block, q_block)
            q = qg[h, 0, q_rows]
            g = qg[h, 1, q_rows]
            query_col = qb * (q_block // cells) + lax.broadcasted_iota(jnp.int32, (1, q_block), 1) // cells
            top = jnp.full((1, q_block), NEG, F32)
            blocks = []
            for j in range(0 if halo else 2, 3):
                far = 0.0 if spread[j] is None else jnp.where(spread[j], 0.0, NEG)
                for c in range(n_wa):
                    bias = jnp.where(jnp.abs(query_col - c) <= ext_w, far, NEG)
                    blocks.append(((j * n_wa + c) * cells, cells, bias))
            for b in range(0, text, KEY_BLOCK):
                blocks.append((text_base + b, min(KEY_BLOCK, text - b), None))
            for start, size, bias in blocks:
                sc = dot_nt(kv[h, 0, pl.ds(start, size)], q) * scale
                if bias is not None:
                    sc = sc + bias
                st[pl.ds(start, size)] = sc
                top = jnp.maximum(top, jnp.max(sc, axis=0, keepdims=True))
            total = jnp.zeros((1, q_block), F32)
            for start, size, _ in blocks:
                p = jnp.exp(st[pl.ds(start, size)] - top)
                st[pl.ds(start, size)] = p
                total = total + jnp.sum(p, axis=0, keepdims=True)
            inv = 1.0 / total
            for start, size, _ in blocks:
                wb[pl.ds(start, size)] = (st[pl.ds(start, size)] * inv).astype(BF16)
            attended = dot_tn(wb[keys], kv[h, 1, keys]).astype(BF16)
            oq[h, 0, q_rows] = attended
            product = g.astype(F32) * attended.astype(F32)
            delta = jnp.sum(product.T, axis=0, keepdims=True)
            inv_scale = inv * scale
            for start, size, _ in blocks:
                dp = dot_nt(kv[h, 1, pl.ds(start, size)], g)
                db[pl.ds(start, size)] = (st[pl.ds(start, size)] * inv_scale * (dp - delta)).astype(BF16)
            oq[h, 1, q_rows] = dot_tn(db[keys], kv[h, 0, keys]).astype(BF16)

            def put(ref, index, value):
                if qb == 0:
                    ref[index] = value.astype(ref.dtype)
                else:
                    ref[index] = (ref[index].astype(F32) + value).astype(ref.dtype)

            for kind, (left, right) in enumerate(((db, q), (wb, g))):
                part = jnp.dot(left[pl.ds(text_base, text)], right, preferred_element_type=F32)
                put(t_part, (h, kind), part)
                part = jnp.dot(left[pl.ds(own_base, slab)], right, preferred_element_type=F32)
                put(own_part, (h, kind), part)
                for side in range(2 if halo else 0):
                    part = jnp.dot(left[pl.ds(side * slab, slab)], right, preferred_element_type=F32)
                    put(z_part, (side, h, kind), part)

    def y_src(pair, h, owner):
        return (oq if pair == 0 else fin).at[h, :, rows_of(0, owner, cells)]

    def y_dst(pair, h, group):
        return res_out.at[group * heads + h, pl.ds(2 * pair, 2)]

    def y_copy(pair, h, d, source):
        return remote(
            y_src(pair, h, peer_of(d)), y_dst(pair, h, source),
            y_send.at[d - 1, pair], y_recv.at[d - 1, pair], wa=peer_of(d),
        )

    def y_local(pair, h):
        return pltpu.make_async_copy(y_src(pair, h, w), y_dst(pair, h, w), y_loc.at[pair])

    def g_copy(side, h, block):
        return remote(
            t_part.at[h, :, rows_of(0, block, text_rows)], t_got.at[side, h, block],
            g_send.at[side, block], g_recv.at[side, h, block],
            sa=after if side == 0 else before,
        )

    def g_valid(side, block):
        return s < block if side == 0 else s > block

    def g_relay(side, h):
        inward = has_prev if side == 0 else has_next
        blocks = range(n_sa)
        for block in (reversed(blocks) if side == 0 else blocks):
            @pl.when(g_valid(side, block))
            def _():
                @pl.when(inward)
                def _():
                    g_copy(side, h, block).wait_recv()
                    rows = pl.ds(block * text_rows, text_rows)
                    joined = t_part[h, :, rows].astype(F32) + t_got[side, h, block].astype(F32)
                    t_part[h, :, rows] = joined.astype(BF16)

                g_copy(side, h, block).start()

    def far_copy(h, step, there, source):
        return remote(
            t_part.at[h, :, rows_of(0, there, text_rows)], t_far.at[h - relayed, source],
            far_send, far_recv.at[h - relayed, source], sa=there,
        )

    def far_start(h):
        for step in range(n_sa - 1, 0, -1):
            for there, valid in ((s + step, s + step < n_sa), (s - step, s >= step)):
                @pl.when(valid)
                def _():
                    far_copy(h, step, there, s).start()

    def finish_far(h):
        for step in range(1, n_sa):
            source = lax.rem(s + step, n_sa)
            far_copy(h, step, source, source).wait_recv()
        whole = t_part[h, :, rows_of(0, s, text_rows)].astype(F32)
        for step in range(1, n_sa):
            whole = whole + t_far[h - relayed, lax.rem(s + step, n_sa)].astype(F32)
        give_text(h, whole)

    def f_copy(h, d, source):
        return remote(
            t_fin.at[h], text_out.at[source * heads + h], f_send.at[d - 1], f_recv.at[d - 1], wa=peer_of(d),
        )

    def f_local(h):
        return pltpu.make_async_copy(t_fin.at[h], text_out.at[w * heads + h], f_loc)

    def give_text(h, whole):
        t_fin[h] = whole.astype(BF16)
        for d in range(1, n_wa):
            f_copy(h, d, w).start()
        f_local(h).start()

    def finish(h, d):
        rows = rows_of(0, peer_of(d), cells)
        if near:
            @pl.when(jnp.logical_and(h < near, has_next))
            def _():
                r_copy(0, h, d).wait_recv()

            @pl.when(jnp.logical_and(h < near, has_prev))
            def _():
                r_copy(1, h, d).wait_recv()

            @pl.when(h < near)
            def _():
                whole = own_part[h, :, rows] + z_got[0, h, :, rows].astype(F32) + z_got[1, h, :, rows].astype(F32)
                fin[h, :, rows] = whole.astype(BF16)

        if near < heads:
            @pl.when(h >= near)
            def _():
                fin[h, :, rows] = own_part[h, :, rows].astype(BF16)

        if d:
            y_copy(1, h, d, w).start()
        else:
            y_local(1, h).start()

    def finish_text(h):
        @pl.when(has_prev)
        def _():
            g_copy(0, h, s).wait_recv()

        @pl.when(has_next)
        def _():
            g_copy(1, h, s).wait_recv()

        whole = t_part[h, :, rows_of(0, s, text_rows)].astype(F32)
        whole = whole + t_got[0, h, s].astype(F32) + t_got[1, h, s].astype(F32)
        give_text(h, whole)

    def attend(h):
        x_wait(1, h)

        @pl.when(jnp.logical_not(has_next))
        def _():
            for hop in range(n_sa - 1):
                t_in(0, h, hop).wait_recv()

        @pl.when(jnp.logical_not(has_prev))
        def _():
            for hop in range(n_sa - 1):
                t_in(1, h, hop).wait_recv()

        if near:
            @pl.when(jnp.logical_and(h < near, has_prev))
            def _():
                z_copy(0, h).wait_recv()

            @pl.when(jnp.logical_and(h < near, has_next))
            def _():
                z_copy(1, h).wait_recv()

            @pl.when(h < near)
            def _():
                compute(h, True)

        if near < heads:
            @pl.when(h >= near)
            def _():
                compute(h, False)

        for d in range(1, n_wa):
            y_copy(0, h, d, w).start()
        y_local(0, h).start()

    def give_back(h, d):
        @pl.when(has_prev)
        def _():
            r_copy(0, h, d).start()

        @pl.when(has_next)
        def _():
            r_copy(1, h, d).start()

    def at(h, first, count, body):
        @pl.when(jnp.logical_and(h >= first, h < count))
        def _():
            body(h)

    def step(turn, c):
        i = turn - FEED
        at(turn, 0, heads, feed)
        for hop in range(2, n_sa - 1):
            at(i + FEED - 1, 0, heads, lambda h: t_forward(h, hop))
        at(i, 0, heads, attend)
        if relayed < heads:
            at(i, relayed, heads, far_start)
        if near < heads:
            for d in (*range(1, n_wa), 0):
                at(i, near, heads, lambda h: finish(h, d))
        for side in range(2):
            at(i - (s if side == 0 else n_sa - 1 - s), 0, relayed, lambda h: g_relay(side, h))
        if near:
            for d in range(1, n_wa):
                at(i - return_lag, 0, near, lambda h: give_back(h, d))
            at(i - return_lag - 1, 0, near, lambda h: give_back(h, 0))
            for d in range(1, n_wa):
                at(i - finish_lag, 0, near, lambda h: finish(h, d))
            at(i - finish_lag - 1, 0, near, lambda h: finish(h, 0))
        if relayed:
            at(i - (n_sa - 1), 0, relayed, finish_text)
        if relayed < heads:
            at(i - FAR_LAG, relayed, heads, finish_far)
        return c

    lax.fori_loop(0, FEED + max(relayed + n_sa - 1, near + finish_lag + 1, heads + FAR_LAG), step, 0)

    every = pl.ds(0, heads)
    if relayed < heads:
        sent = t_far.at[:, pl.ds(0, n_sa - 1)]
        remote(sent, sent, far_send, far_recv.at[0, 0], sa=after).wait_send()
    for d in range(1, n_wa):
        remote(stage.at[d - 1], stage.at[d - 1], x_send.at[d - 1], x_recv.at[d - 1, 0, 0], wa=peer_of(d)).wait_send()
        for pair in range(2):
            for source, wait in ((w, "wait_send"), (source_of(d), "wait_recv")):
                group = res_out.at[pl.ds(source * heads, heads), pl.ds(2 * pair, 2)]
                getattr(remote(group, group, y_send.at[d - 1, pair], y_recv.at[d - 1, pair], wa=peer_of(d)), wait)()
        for source, wait in ((w, "wait_send"), (source_of(d), "wait_recv")):
            group = text_out.at[pl.ds(source * heads, heads)]
            getattr(remote(group, group, f_send.at[d - 1], f_recv.at[d - 1], wa=peer_of(d)), wait)()
    for pair in range(2):
        group = res_out.at[pl.ds(w * heads, heads), pl.ds(2 * pair, 2)]
        pltpu.make_async_copy(group, group, y_loc.at[pair]).wait()
    group = text_out.at[pl.ds(w * heads, heads)]
    pltpu.make_async_copy(group, group, f_loc).wait()
    for side in range(2):
        there = after if side == 0 else before
        block = kv.at[every, :, pl.ds(text_base, text_rows)]
        sums = kv.at[pl.ds(0, relayed), :, pl.ds(text_base, text_rows)] if relayed else None
        for hop in range(n_sa - 1):
            @pl.when(t_valid(side, hop))
            def _():
                remote(block, block, t_send.at[side, hop], t_recv.at[side, 0, hop], sa=there).wait_send()

        for owner in range(n_sa if relayed else 0):
            @pl.when(g_valid(side, owner))
            def _():
                remote(sums, sums, g_send.at[side, owner], g_recv.at[side, 0, owner], sa=there).wait_send()

        if near:
            halo = kv.at[pl.ds(0, near), :, pl.ds(0, slab)]

            @pl.when(has_next if side == 0 else has_prev)
            def _():
                remote(halo, halo, z_send.at[side], z_recv.at[side, 0], sa=there).wait_send()

            @pl.when(has_prev if side == 0 else has_next)
            def _():
                remote(halo, halo, r_send.at[side], r_recv.at[side, 0, 0], sa=before if side == 0 else after).wait_send()


def meet(n_hp, n_wa, scalars, window, most, order, theirs, send, recv):
    me = lax.axis_index("hp")
    barrier = pltpu.get_barrier_semaphore()
    copies = []
    for d in range(1, n_hp):
        peer = lax.rem(me + d, n_hp)
        pl.semaphore_signal(barrier, inc=1, device_id={"hp": peer}, device_id_type=MESH)
        copies.append(pltpu.make_async_remote_copy(
            src_ref=window, dst_ref=theirs.at[d - 1], send_sem=send.at[d - 1], recv_sem=recv.at[d - 1],
            device_id={"hp": peer}, device_id_type=MESH,
        ))
    pl.semaphore_wait(barrier, n_hp - 1)
    for copy in copies:
        copy.start()

    count = order.shape[0]
    heads = count // n_wa
    wide = [(scalars[0, n] >= 1).astype(jnp.int32) for n in range(count)]
    reached = sum(wide)
    seen = jnp.int32(0)
    ranks = []
    for n in range(count):
        ranks.append(jnp.where(wide[n] > 0, seen, reached + n - seen))
        seen = seen + wide[n]
    for slot in range(count):
        rank = slot % heads * n_wa + slot // heads
        order[slot] = sum(jnp.where(ranks[n] == rank, n, 0) for n in range(count))

    axis = lax.broadcasted_iota(jnp.int32, window.shape, 0)
    total = reached.astype(F32)
    for d, copy in enumerate(copies):
        copy.wait()
        other = jnp.sum(jnp.where(jnp.logical_and(axis == 0, theirs[d] >= 1), 1.0, 0.0))
        total = jnp.maximum(total, other)
    most[0] = total.astype(jnp.int32)


def hand_over(order, res, words, o_out, dq_out, dk_out, dv_out, dtk_out, dtv_out):
    def place(slot, c):
        columns = pl.ds(pl.multiple_of(order[slot] * HEAD_DIM, HEAD_DIM), HEAD_DIM)
        for kind, out in enumerate((o_out, dq_out, dk_out, dv_out)):
            out[:, columns] = res[slot, kind]
        for kind, out in enumerate((dtk_out, dtv_out)):
            out[:, columns] = words[slot, kind].astype(F32)
        return c

    lax.fori_loop(0, res.shape[0], place, 0)


def attention(n_sa, n_wa, near, window, order, queries, keys, values, out_grad, text_keys, text_values):
    cells, channels = queries.shape
    heads = channels // HEAD_DIM // n_wa
    text_rows = text_keys.shape[0]
    slab, text = n_wa * cells, n_sa * text_rows
    n_keys = 3 * slab + text
    q_block = min(slab, Q_BLOCK)
    halo = max(near, 1)
    dma = pltpu.SemaphoreType.DMA
    anywhere = pl.BlockSpec(memory_space=pl.ANY)
    in_smem = pl.BlockSpec(memory_space=pltpu.SMEM)
    return pl.pallas_call(
        functools.partial(kernel, n_sa, n_wa, heads, near, cells, text_rows),
        out_shape=(
            jax.ShapeDtypeStruct((n_wa * heads, 4, cells, HEAD_DIM), BF16),
            jax.ShapeDtypeStruct((n_wa * heads, 2, text_rows, HEAD_DIM), BF16),
        ),
        in_specs=[in_smem] * 2 + [anywhere] * 6,
        out_specs=(anywhere,) * 2,
        scratch_shapes=[
            pltpu.VMEM((4, cells, channels), BF16),
            pltpu.VMEM((2, text_rows, channels), BF16),
            pltpu.VMEM((n_wa * heads, 4, cells, HEAD_DIM), BF16),
            pltpu.VMEM((n_wa * heads, 2, text_rows, HEAD_DIM), BF16),
            pltpu.VMEM((n_wa - 1, heads, 4, cells, HEAD_DIM), BF16),
            pltpu.VMEM((heads, 2, n_keys, HEAD_DIM), BF16),
            pltpu.VMEM((heads, 2, slab, HEAD_DIM), BF16),
            pltpu.VMEM((heads, 2, slab, HEAD_DIM), BF16),
            pltpu.VMEM((heads, 2, slab, HEAD_DIM), F32),
            pltpu.VMEM((2, halo, 2, slab, HEAD_DIM), BF16),
            pltpu.VMEM((2, halo, 2, slab, HEAD_DIM), BF16),
            pltpu.VMEM((heads, 2, slab, HEAD_DIM), BF16),
            pltpu.VMEM((heads, 2, text, HEAD_DIM), BF16),
            pltpu.VMEM((2, heads, n_sa, 2, text_rows, HEAD_DIM), BF16),
            pltpu.VMEM((max(heads - near, 1), n_sa, 2, text_rows, HEAD_DIM), BF16),
            pltpu.VMEM((heads, 2, text_rows, HEAD_DIM), BF16),
            pltpu.VMEM((n_keys, q_block), F32),
            pltpu.VMEM((n_keys, q_block), BF16),
            pltpu.VMEM((n_keys, q_block), BF16),
            dma((6,)),
            dma((n_wa - 1,)),
            dma((n_wa - 1, heads, 2)),
            dma((2, n_sa - 1)),
            dma((2, heads, n_sa - 1)),
            dma((2,)),
            dma((2, halo)),
            dma((2,)),
            dma((2, halo, n_wa)),
            dma((n_wa - 1, 2)),
            dma((n_wa - 1, 2)),
            dma((2,)),
            dma((2, n_sa)),
            dma((2, heads, n_sa)),
            dma((n_wa - 1,)),
            dma((n_wa - 1,)),
            dma(()),
            dma(()),
            dma((max(heads - near, 1), n_sa)),
        ],
        compiler_params=pltpu.CompilerParams(
            collective_id=1 + near, has_side_effects=True, vmem_limit_bytes=VMEM_LIMIT
        ),
    )(window, order, keys, values, queries, out_grad, text_keys, text_values)


VMEM_LIMIT = 60 * 1024 * 1024


def shards(queries, keys, values, text_keys, text_values, out_grad, window_ext):
    n_sa, n_wa = lax.axis_size("sa"), lax.axis_size("wa")
    grid = queries.shape
    channels = grid[-1]
    cells = grid[0] * grid[1] * grid[2]
    text_rows = text_keys.shape[0]
    flat = (cells, channels)
    heads = channels // HEAD_DIM // n_wa
    extents = window_ext.T
    n_hp = lax.axis_size("hp")
    cut = -(-2 * heads // 3)
    most, order = pl.pallas_call(
        functools.partial(meet, n_hp, n_wa),
        out_shape=(jax.ShapeDtypeStruct((1,), jnp.int32), jax.ShapeDtypeStruct((n_wa * heads,), jnp.int32)),
        in_specs=[pl.BlockSpec(memory_space=pltpu.SMEM), pl.BlockSpec(memory_space=pltpu.VMEM)],
        out_specs=(pl.BlockSpec(memory_space=pltpu.SMEM),) * 2,
        scratch_shapes=[
            pltpu.VMEM((n_hp - 1, *extents.shape), jnp.int32),
            pltpu.SemaphoreType.DMA((n_hp - 1,)),
            pltpu.SemaphoreType.DMA((n_hp - 1,)),
        ],
        compiler_params=pltpu.CompilerParams(collective_id=0, has_side_effects=True),
    )(extents, extents)

    def run(near):
        return functools.partial(attention, n_sa, n_wa, near)

    res, words = lax.cond(
        most[0] <= n_wa * cut, run(cut), run(heads),
        extents, order, queries.reshape(flat), keys.reshape(flat),
        values.reshape(flat), out_grad.reshape(flat), text_keys, text_values,
    )
    in_vmem = pl.BlockSpec(memory_space=pltpu.VMEM)
    outs = pl.pallas_call(
        hand_over,
        out_shape=(jax.ShapeDtypeStruct(flat, BF16),) * 4
        + (jax.ShapeDtypeStruct((text_rows, channels), F32),) * 2,
        in_specs=[pl.BlockSpec(memory_space=pltpu.SMEM)] + [in_vmem] * 2,
        out_specs=(in_vmem,) * 6,
    )(order, res, words)
    return tuple(out.reshape(grid) for out in outs[:4]) + tuple(outs[4:])


def solution(mesh):
    cell = P(("clips", "sa"), None, "wa", "hp")
    text = P(("clips", "sa"), "hp")
    return jax.shard_map(
        shards,
        mesh=mesh,
        in_specs=(cell, cell, cell, text, text, cell, P("hp", None)),
        out_specs=(cell, cell, cell, cell, text, text),
        check_vma=False,
    )
```

```python
import functools

import jax
import jax.numpy as jnp
from jax import lax
from jax.experimental import pallas as pl
from jax.experimental.pallas import tpu as pltpu
from jax.sharding import PartitionSpec as P

HEAD_DIM = 128
NEG = -1e30
MESH = pl.DeviceIdType.MESH
F32 = jnp.float32
BF16 = jnp.bfloat16
KEY_BLOCK = 256
Q_BLOCK = 256
FEED = 3
FAR_LAG = 1


def dot_nt(a, b):
    return lax.dot_general(a, b, (((1,), (1,)), ((), ())), preferred_element_type=F32)


def dot_tn(a, b):
    return lax.dot_general(a, b, (((0,), (0,)), ((), ())), preferred_element_type=F32)


def kernel(
    n_sa, n_wa, heads, room, cells, text_rows,
    window, order, k_in, v_in, q_in, g_in, tk_in, tv_in,
    res_out, text_out,
    cell_in, words_in, kv_by_head, qg_by_head, words_by_head, stage, kv, qg, oq, own_part, z_part, z_got, fin, t_part, t_got, t_far, t_fin, st, wb, db,
    load, x_send, x_recv, t_send, t_recv, z_send, z_recv,
    r_send, r_recv, y_send, y_recv, y_loc, g_send, g_recv, f_send, f_recv, f_loc, far_send, far_recv,
):
    s = lax.axis_index("sa")
    w = lax.axis_index("wa")
    slab = n_wa * cells
    text = n_sa * text_rows
    own_base = 2 * slab
    text_base = 3 * slab
    scale = HEAD_DIM ** (-0.5)
    has_prev, has_next = s > 0, s < n_sa - 1
    before, after = lax.rem(s + n_sa - 1, n_sa), lax.rem(s + 1, n_sa)
    q_block = min(slab, Q_BLOCK)
    most_near = -(-room // n_wa)
    near = (room + n_wa - 1 - lax.rem(w + n_wa - lax.rem(lax.axis_index("hp"), n_wa), n_wa)) // n_wa
    some_far = room < n_wa * heads
    relayed = heads - min(2, heads - most_near)
    return_lag = 1 if some_far else 2
    finish_lag = return_lag + 2

    def rows_of(base, index, size):
        return pl.ds(pl.multiple_of(base + index * size, 16), size)

    def remote(src, dst, send, recv, **where):
        return pltpu.make_async_remote_copy(
            src_ref=src, dst_ref=dst, send_sem=send, recv_sem=recv,
            device_id=where, device_id_type=MESH,
        )

    def peer_of(d):
        return lax.rem(w + d, n_wa)

    def source_of(d):
        return lax.rem(w + n_wa - d, n_wa)

    word_loads = [
        pltpu.make_async_copy(ref, words_in.at[kind], load.at[4 + kind])
        for kind, ref in enumerate((tk_in, tv_in))
    ]
    cell_loads = [
        pltpu.make_async_copy(ref, cell_in.at[kind], load.at[kind])
        for kind, ref in enumerate((k_in, v_in, q_in, g_in))
    ]
    for copy in word_loads + cell_loads:
        copy.start()

    barrier = pltpu.get_barrier_semaphore()
    for d in range(1, n_wa):
        pl.semaphore_signal(barrier, inc=1, device_id={"wa": peer_of(d)}, device_id_type=MESH)

    @pl.when(has_prev)
    def _():
        pl.semaphore_signal(barrier, inc=1, device_id={"sa": before}, device_id_type=MESH)

    @pl.when(has_next)
    def _():
        pl.semaphore_signal(barrier, inc=1, device_id={"sa": after}, device_id_type=MESH)

    def lanes_of(n):
        return pl.ds(pl.multiple_of(n * HEAD_DIM, HEAD_DIM), HEAD_DIM)

    def spread_keys(n, c):
        for kind in range(2):
            words_by_head[n, kind] = words_in[kind, :, lanes_of(n)]
            kv_by_head[n, kind] = cell_in[kind, :, lanes_of(n)]
        return c

    def spread_queries(n, c):
        for kind in range(2):
            qg_by_head[n, kind] = cell_in[2 + kind, :, lanes_of(n)]
        return c

    def arrange_keys(h, c):
        here = order[w * heads + h]
        kv[h, :, rows_of(text_base, s, text_rows)] = words_by_head[here]
        kv[h, :, rows_of(own_base, w, cells)] = kv_by_head[here]
        for d in range(1, n_wa):
            stage[d - 1, h, pl.ds(0, 2)] = kv_by_head[order[peer_of(d) * heads + h]]
        return c

    def arrange_queries(h, c):
        qg[h, :, rows_of(0, w, cells)] = qg_by_head[order[w * heads + h]]
        for d in range(1, n_wa):
            stage[d - 1, h, pl.ds(2, 2)] = qg_by_head[order[peer_of(d) * heads + h]]
        return c

    for copy in word_loads + cell_loads[:2]:
        copy.wait()
    lax.fori_loop(0, n_wa * heads, spread_keys, 0)
    lax.fori_loop(0, heads, arrange_keys, 0)

    neighbours = n_wa - 1 + has_prev.astype(jnp.int32) + has_next.astype(jnp.int32)
    pl.semaphore_wait(barrier, neighbours)

    def x_slot(pair, h, source):
        if pair == 0:
            return kv.at[h, :, rows_of(own_base, source, cells)]
        return qg.at[h, :, rows_of(0, source, cells)]

    def x_copy(pair, h, d, source):
        return remote(
            stage.at[d - 1, h, pl.ds(2 * pair, 2)], x_slot(pair, h, source),
            x_send.at[d - 1], x_recv.at[d - 1, h, pair], wa=peer_of(d),
        )

    def x_wait(pair, h):
        for d in range(1, n_wa):
            x_copy(pair, h, d, source_of(d)).wait_recv()

    def t_slot(h, block):
        return kv.at[h, :, rows_of(text_base, block, text_rows)]

    def t_hop(side, h, hop, block):
        return remote(
            t_slot(h, block), t_slot(h, block), t_send.at[side, hop], t_recv.at[side, h, hop],
            sa=after if side == 0 else before,
        )

    def t_out(side, h, hop):
        return t_hop(side, h, hop, s - hop if side == 0 else s + hop)

    def t_in(side, h, hop):
        return t_hop(side, h, hop, s - 1 - hop if side == 0 else s + 1 + hop)

    def t_valid(side, hop):
        if side == 0:
            return jnp.logical_and(s >= hop, has_next)
        return jnp.logical_and(s + hop < n_sa, has_prev)

    def t_forward(h, hop):
        for side in range(2):
            @pl.when(t_valid(side, hop))
            def _():
                if hop:
                    t_in(side, h, hop - 1).wait_recv()
                t_out(side, h, hop).start()

    def z_copy(side, h):
        return remote(
            kv.at[h, :, pl.ds(own_base, slab)], kv.at[h, :, pl.ds(side * slab, slab)],
            z_send.at[side], z_recv.at[side, h], sa=after if side == 0 else before,
        )

    def r_copy(side, h, d):
        rows = rows_of(0, peer_of(d), cells)
        return remote(
            z_part.at[side, h, :, rows], z_got.at[side, h, :, rows],
            r_send.at[side], r_recv.at[side, h, d], sa=before if side == 0 else after,
        )

    def x_start(pair, h):
        for d in range(1, n_wa):
            x_copy(pair, h, d, w).start()

    def open_keys(h, c):
        t_forward(h, 0)
        x_start(0, h)
        return c

    def open_both(h, c):
        x_start(1, h - first)
        return open_keys(h, c)

    first = min(2, heads)
    lax.fori_loop(0, first, open_keys, 0)
    for copy in cell_loads[2:]:
        copy.wait()
    lax.fori_loop(0, n_wa * heads, spread_queries, 0)
    lax.fori_loop(0, heads, arrange_queries, 0)
    lax.fori_loop(first, heads, open_both, 0)
    for h in range(heads - first, heads):
        x_start(1, h)

    def clear_side(side):
        def clear(h, c):
            if most_near:
                @pl.when(h < near)
                def _():
                    kv[h, :, pl.ds(side * slab, slab)] = jnp.zeros((2, slab, HEAD_DIM), BF16)
                    z_got[1 - side, h] = jnp.zeros((2, slab, HEAD_DIM), BF16)

            t_got[side, h, 0 if side == 0 else n_sa - 1] = jnp.zeros((2, text_rows, HEAD_DIM), BF16)
            return c

        lax.fori_loop(0, heads, clear, 0)

    @pl.when(jnp.logical_not(has_prev))
    def _():
        clear_side(0)

    @pl.when(jnp.logical_not(has_next))
    def _():
        clear_side(1)

    def feed(h):
        t_forward(h, 1)
        x_wait(0, h)
        if most_near:
            @pl.when(h < near)
            def _():
                @pl.when(has_next)
                def _():
                    z_copy(0, h).start()

                @pl.when(has_prev)
                def _():
                    z_copy(1, h).start()

    def compute(h, halo):
        ext_t = window[0, order[w * heads + h]]
        ext_w = window[2, order[w * heads + h]]
        base = 0 if halo else own_base
        span = text_base + text - base
        keys = pl.ds(base, span)
        spread = (
            jnp.logical_and(has_prev, ext_t >= 1),
            jnp.logical_and(has_next, ext_t >= 1),
            None,
        )
        for qb in range(slab // q_block):
            q_rows = pl.ds(qb * q_block, q_block)
            q = qg[h, 0, q_rows]
            g = qg[h, 1, q_rows]
            query_col = qb * (q_block // cells) + lax.broadcasted_iota(jnp.int32, (1, q_block), 1) // cells
            top = jnp.full((1, q_block), NEG, F32)
            blocks = []
            for j in range(0 if halo else 2, 3):
                far = 0.0 if spread[j] is None else jnp.where(spread[j], 0.0, NEG)
                for c in range(n_wa):
                    bias = jnp.where(jnp.abs(query_col - c) <= ext_w, far, NEG)
                    blocks.append(((j * n_wa + c) * cells, cells, bias))
            for b in range(0, text, KEY_BLOCK):
                blocks.append((text_base + b, min(KEY_BLOCK, text - b), None))
            for start, size, bias in blocks:
                sc = dot_nt(kv[h, 0, pl.ds(start, size)], q) * scale
                if bias is not None:
                    sc = sc + bias
                st[pl.ds(start, size)] = sc
                top = jnp.maximum(top, jnp.max(sc, axis=0, keepdims=True))
            total = jnp.zeros((1, q_block), F32)
            for start, size, _ in blocks:
                p = jnp.exp(st[pl.ds(start, size)] - top)
                st[pl.ds(start, size)] = p
                total = total + jnp.sum(p, axis=0, keepdims=True)
            inv = 1.0 / total
            for start, size, _ in blocks:
                wb[pl.ds(start, size)] = (st[pl.ds(start, size)] * inv).astype(BF16)
            attended = dot_tn(wb[keys], kv[h, 1, keys]).astype(BF16)
            oq[h, 0, q_rows] = attended
            product = g.astype(F32) * attended.astype(F32)
            delta = jnp.sum(product.T, axis=0, keepdims=True)
            inv_scale = inv * scale
            for start, size, _ in blocks:
                dp = dot_nt(kv[h, 1, pl.ds(start, size)], g)
                db[pl.ds(start, size)] = (st[pl.ds(start, size)] * inv_scale * (dp - delta)).astype(BF16)
            oq[h, 1, q_rows] = dot_tn(db[keys], kv[h, 0, keys]).astype(BF16)

            def put(ref, index, value):
                if qb == 0:
                    ref[index] = value.astype(ref.dtype)
                else:
                    ref[index] = (ref[index].astype(F32) + value).astype(ref.dtype)

            for kind, (left, right) in enumerate(((db, q), (wb, g))):
                part = jnp.dot(left[pl.ds(text_base, text)], right, preferred_element_type=F32)
                put(t_part, (h, kind), part)
                part = jnp.dot(left[pl.ds(own_base, slab)], right, preferred_element_type=F32)
                put(own_part, (h, kind), part)
                for side in range(2 if halo else 0):
                    part = jnp.dot(left[pl.ds(side * slab, slab)], right, preferred_element_type=F32)
                    put(z_part, (side, h, kind), part)

    def y_src(pair, h, owner):
        return (oq if pair == 0 else fin).at[h, :, rows_of(0, owner, cells)]

    def y_dst(pair, h, group):
        return res_out.at[group * heads + h, pl.ds(2 * pair, 2)]

    def y_copy(pair, h, d, source):
        return remote(
            y_src(pair, h, peer_of(d)), y_dst(pair, h, source),
            y_send.at[d - 1, pair], y_recv.at[d - 1, pair], wa=peer_of(d),
        )

    def y_local(pair, h):
        return pltpu.make_async_copy(y_src(pair, h, w), y_dst(pair, h, w), y_loc.at[pair])

    def g_copy(side, h, block):
        return remote(
            t_part.at[h, :, rows_of(0, block, text_rows)], t_got.at[side, h, block],
            g_send.at[side, block], g_recv.at[side, h, block],
            sa=after if side == 0 else before,
        )

    def g_valid(side, block):
        return s < block if side == 0 else s > block

    def g_relay(side, h):
        inward = has_prev if side == 0 else has_next
        blocks = range(n_sa)
        for block in (reversed(blocks) if side == 0 else blocks):
            @pl.when(g_valid(side, block))
            def _():
                @pl.when(inward)
                def _():
                    g_copy(side, h, block).wait_recv()
                    rows = pl.ds(block * text_rows, text_rows)
                    joined = t_part[h, :, rows].astype(F32) + t_got[side, h, block].astype(F32)
                    t_part[h, :, rows] = joined.astype(BF16)

                g_copy(side, h, block).start()

    def far_copy(h, step, there, source):
        return remote(
            t_part.at[h, :, rows_of(0, there, text_rows)], t_far.at[h - relayed, source],
            far_send, far_recv.at[h - relayed, source], sa=there,
        )

    def far_start(h):
        for step in range(n_sa - 1, 0, -1):
            for there, valid in ((s + step, s + step < n_sa), (s - step, s >= step)):
                @pl.when(valid)
                def _():
                    far_copy(h, step, there, s).start()

    def finish_far(h):
        for step in range(1, n_sa):
            source = lax.rem(s + step, n_sa)
            far_copy(h, step, source, source).wait_recv()
        whole = t_part[h, :, rows_of(0, s, text_rows)].astype(F32)
        for step in range(1, n_sa):
            whole = whole + t_far[h - relayed, lax.rem(s + step, n_sa)].astype(F32)
        give_text(h, whole)

    def f_copy(h, d, source):
        return remote(
            t_fin.at[h], text_out.at[source * heads + h], f_send.at[d - 1], f_recv.at[d - 1], wa=peer_of(d),
        )

    def f_local(h):
        return pltpu.make_async_copy(t_fin.at[h], text_out.at[w * heads + h], f_loc)

    def give_text(h, whole):
        t_fin[h] = whole.astype(BF16)
        for d in range(1, n_wa):
            f_copy(h, d, w).start()
        f_local(h).start()

    def finish(h, d):
        rows = rows_of(0, peer_of(d), cells)
        if most_near:
            @pl.when(jnp.logical_and(h < near, has_next))
            def _():
                r_copy(0, h, d).wait_recv()

            @pl.when(jnp.logical_and(h < near, has_prev))
            def _():
                r_copy(1, h, d).wait_recv()

            @pl.when(h < near)
            def _():
                whole = own_part[h, :, rows] + z_got[0, h, :, rows].astype(F32) + z_got[1, h, :, rows].astype(F32)
                fin[h, :, rows] = whole.astype(BF16)

        if some_far:
            @pl.when(h >= near)
            def _():
                fin[h, :, rows] = own_part[h, :, rows].astype(BF16)

        if d:
            y_copy(1, h, d, w).start()
        else:
            y_local(1, h).start()

    def finish_text(h):
        @pl.when(has_prev)
        def _():
            g_copy(0, h, s).wait_recv()

        @pl.when(has_next)
        def _():
            g_copy(1, h, s).wait_recv()

        whole = t_part[h, :, rows_of(0, s, text_rows)].astype(F32)
        whole = whole + t_got[0, h, s].astype(F32) + t_got[1, h, s].astype(F32)
        give_text(h, whole)

    def attend(h):
        x_wait(1, h)

        @pl.when(jnp.logical_not(has_next))
        def _():
            for hop in range(n_sa - 1):
                t_in(0, h, hop).wait_recv()

        @pl.when(jnp.logical_not(has_prev))
        def _():
            for hop in range(n_sa - 1):
                t_in(1, h, hop).wait_recv()

        if most_near:
            @pl.when(jnp.logical_and(h < near, has_prev))
            def _():
                z_copy(0, h).wait_recv()

            @pl.when(jnp.logical_and(h < near, has_next))
            def _():
                z_copy(1, h).wait_recv()

            @pl.when(h < near)
            def _():
                compute(h, True)

        if some_far:
            @pl.when(h >= near)
            def _():
                compute(h, False)

        for d in range(1, n_wa):
            y_copy(0, h, d, w).start()
        y_local(0, h).start()

    def give_back(h, d):
        @pl.when(has_prev)
        def _():
            r_copy(0, h, d).start()

        @pl.when(has_next)
        def _():
            r_copy(1, h, d).start()

    def at(h, first, count, body):
        @pl.when(jnp.logical_and(h >= first, h < count))
        def _():
            body(h)

    def step(turn, c):
        i = turn - FEED
        at(turn, 0, heads, feed)
        for hop in range(2, n_sa - 1):
            at(i + FEED - 1, 0, heads, lambda h: t_forward(h, hop))
        at(i, 0, heads, attend)
        if relayed < heads:
            at(i, relayed, heads, far_start)
        if some_far:
            for d in (*range(1, n_wa), 0):
                at(i, near, heads, lambda h: finish(h, d))
        for side in range(2):
            at(i - (s if side == 0 else n_sa - 1 - s), 0, relayed, lambda h: g_relay(side, h))
        if most_near:
            for d in range(1, n_wa):
                at(i - return_lag, 0, near, lambda h: give_back(h, d))
            at(i - return_lag - 1, 0, near, lambda h: give_back(h, 0))
        if relayed:
            at(i - (n_sa - 1), 0, relayed, finish_text)
        if relayed < heads:
            at(i - FAR_LAG, relayed, heads, finish_far)
        if most_near:
            for d in range(1, n_wa):
                at(i - finish_lag, 0, near, lambda h: finish(h, d))
            at(i - finish_lag - 1, 0, near, lambda h: finish(h, 0))
        return c

    lax.fori_loop(0, FEED + max(relayed + n_sa - 1, most_near + finish_lag + 1, heads + FAR_LAG), step, 0)

    every = pl.ds(0, heads)
    if relayed < heads:
        sent = t_far.at[:, pl.ds(0, n_sa - 1)]
        remote(sent, sent, far_send, far_recv.at[0, 0], sa=after).wait_send()
    for d in range(1, n_wa):
        remote(stage.at[d - 1], stage.at[d - 1], x_send.at[d - 1], x_recv.at[d - 1, 0, 0], wa=peer_of(d)).wait_send()
        for pair in range(2):
            for source, wait in ((w, "wait_send"), (source_of(d), "wait_recv")):
                group = res_out.at[pl.ds(source * heads, heads), pl.ds(2 * pair, 2)]
                getattr(remote(group, group, y_send.at[d - 1, pair], y_recv.at[d - 1, pair], wa=peer_of(d)), wait)()
        for source, wait in ((w, "wait_send"), (source_of(d), "wait_recv")):
            group = text_out.at[pl.ds(source * heads, heads)]
            getattr(remote(group, group, f_send.at[d - 1], f_recv.at[d - 1], wa=peer_of(d)), wait)()
    for pair in range(2):
        group = res_out.at[pl.ds(w * heads, heads), pl.ds(2 * pair, 2)]
        pltpu.make_async_copy(group, group, y_loc.at[pair]).wait()
    group = text_out.at[pl.ds(w * heads, heads)]
    pltpu.make_async_copy(group, group, f_loc).wait()
    for side in range(2):
        there = after if side == 0 else before
        block = kv.at[every, :, pl.ds(text_base, text_rows)]
        sums = kv.at[pl.ds(0, relayed), :, pl.ds(text_base, text_rows)] if relayed else None
        for hop in range(n_sa - 1):
            @pl.when(t_valid(side, hop))
            def _():
                remote(block, block, t_send.at[side, hop], t_recv.at[side, 0, hop], sa=there).wait_send()

        for owner in range(n_sa if relayed else 0):
            @pl.when(g_valid(side, owner))
            def _():
                remote(sums, sums, g_send.at[side, owner], g_recv.at[side, 0, owner], sa=there).wait_send()

        if most_near:
            def close_near(h, c):
                @pl.when(has_next if side == 0 else has_prev)
                def _():
                    z_copy(side, h).wait_send()

                @pl.when(has_prev if side == 0 else has_next)
                def _():
                    part = z_part.at[side, h]
                    remote(
                        part, part, r_send.at[side], r_recv.at[side, h, 0],
                        sa=before if side == 0 else after,
                    ).wait_send()

                return c

            lax.fori_loop(0, near, close_near, 0)


def meet(n_hp, n_wa, rooms, scalars, window, most, order, theirs, send, recv):
    me = lax.axis_index("hp")
    barrier = pltpu.get_barrier_semaphore()
    copies = []
    for d in range(1, n_hp):
        peer = lax.rem(me + d, n_hp)
        pl.semaphore_signal(barrier, inc=1, device_id={"hp": peer}, device_id_type=MESH)
        copies.append(pltpu.make_async_remote_copy(
            src_ref=window, dst_ref=theirs.at[d - 1], send_sem=send.at[d - 1], recv_sem=recv.at[d - 1],
            device_id={"hp": peer}, device_id_type=MESH,
        ))
    pl.semaphore_wait(barrier, n_hp - 1)
    for copy in copies:
        copy.start()

    count = order.shape[0]
    heads = count // n_wa
    wide = [(scalars[0, n] >= 1).astype(jnp.int32) for n in range(count)]
    reached = sum(wide)
    seen = jnp.int32(0)
    ranks = []
    for n in range(count):
        ranks.append(jnp.where(wide[n] > 0, seen, reached + n - seen))
        seen = seen + wide[n]
    for slot in range(count):
        rank = slot % heads * n_wa + lax.rem(slot // heads + n_wa - lax.rem(me, n_wa), n_wa)
        order[slot] = sum(jnp.where(ranks[n] == rank, n, 0) for n in range(count))

    axis = lax.broadcasted_iota(jnp.int32, window.shape, 0)
    total = reached.astype(F32)
    for d, copy in enumerate(copies):
        copy.wait()
        other = jnp.sum(jnp.where(jnp.logical_and(axis == 0, theirs[d] >= 1), 1.0, 0.0))
        total = jnp.maximum(total, other)
    most[0] = sum((total > room).astype(jnp.int32) for room in rooms[:-1])


def hand_over(order, res, words, o_out, dq_out, dk_out, dv_out, dtk_out, dtv_out, cell_rows, word_rows, done):
    slots = res.shape[0]
    copies = []

    def columns(slot):
        return pl.ds(pl.multiple_of(order[slot] * HEAD_DIM, HEAD_DIM), HEAD_DIM)

    def send(source, out):
        copies.append(pltpu.make_async_copy(source, out, done.at[len(copies)]))
        copies[-1].start()

    for kind, out in enumerate((dtk_out, dtv_out)):
        def place(slot, c):
            word_rows[kind, :, columns(slot)] = words[slot, kind].astype(F32)
            return c

        lax.fori_loop(0, slots, place, 0)
        send(word_rows.at[kind], out)

    for kind, out in enumerate((o_out, dq_out, dk_out, dv_out)):
        def place(slot, c):
            cell_rows[kind, :, columns(slot)] = res[slot, kind]
            return c

        lax.fori_loop(0, slots, place, 0)
        send(cell_rows.at[kind], out)

    for copy in copies:
        copy.wait()


def attention(n_sa, n_wa, room, window, order, queries, keys, values, out_grad, text_keys, text_values):
    cells, channels = queries.shape
    heads = channels // HEAD_DIM // n_wa
    text_rows = text_keys.shape[0]
    slab, text = n_wa * cells, n_sa * text_rows
    n_keys = 3 * slab + text
    q_block = min(slab, Q_BLOCK)
    halo = -(-room // n_wa)
    dma = pltpu.SemaphoreType.DMA
    anywhere = pl.BlockSpec(memory_space=pl.ANY)
    in_smem = pl.BlockSpec(memory_space=pltpu.SMEM)
    return pl.pallas_call(
        functools.partial(kernel, n_sa, n_wa, heads, room, cells, text_rows),
        out_shape=(
            jax.ShapeDtypeStruct((n_wa * heads, 4, cells, HEAD_DIM), BF16),
            jax.ShapeDtypeStruct((n_wa * heads, 2, text_rows, HEAD_DIM), BF16),
        ),
        in_specs=[in_smem] * 2 + [anywhere] * 6,
        out_specs=(anywhere,) * 2,
        scratch_shapes=[
            pltpu.VMEM((4, cells, channels), BF16),
            pltpu.VMEM((2, text_rows, channels), BF16),
            pltpu.VMEM((n_wa * heads, 2, cells, HEAD_DIM), BF16),
            pltpu.VMEM((n_wa * heads, 2, cells, HEAD_DIM), BF16),
            pltpu.VMEM((n_wa * heads, 2, text_rows, HEAD_DIM), BF16),
            pltpu.VMEM((n_wa - 1, heads, 4, cells, HEAD_DIM), BF16),
            pltpu.VMEM((heads, 2, n_keys, HEAD_DIM), BF16),
            pltpu.VMEM((heads, 2, slab, HEAD_DIM), BF16),
            pltpu.VMEM((heads, 2, slab, HEAD_DIM), BF16),
            pltpu.VMEM((heads, 2, slab, HEAD_DIM), F32),
            pltpu.VMEM((2, halo, 2, slab, HEAD_DIM), BF16),
            pltpu.VMEM((2, halo, 2, slab, HEAD_DIM), BF16),
            pltpu.VMEM((heads, 2, slab, HEAD_DIM), BF16),
            pltpu.VMEM((heads, 2, text, HEAD_DIM), BF16),
            pltpu.VMEM((2, heads, n_sa, 2, text_rows, HEAD_DIM), BF16),
            pltpu.VMEM((max(min(2, heads - halo), 1), n_sa, 2, text_rows, HEAD_DIM), BF16),
            pltpu.VMEM((heads, 2, text_rows, HEAD_DIM), BF16),
            pltpu.VMEM((n_keys, q_block), F32),
            pltpu.VMEM((n_keys, q_block), BF16),
            pltpu.VMEM((n_keys, q_block), BF16),
            dma((6,)),
            dma((n_wa - 1,)),
            dma((n_wa - 1, heads, 2)),
            dma((2, n_sa - 1)),
            dma((2, heads, n_sa - 1)),
            dma((2,)),
            dma((2, halo)),
            dma((2,)),
            dma((2, halo, n_wa)),
            dma((n_wa - 1, 2)),
            dma((n_wa - 1, 2)),
            dma((2,)),
            dma((2, n_sa)),
            dma((2, heads, n_sa)),
            dma((n_wa - 1,)),
            dma((n_wa - 1,)),
            dma(()),
            dma(()),
            dma((max(min(2, heads - halo), 1), n_sa)),
        ],
        compiler_params=pltpu.CompilerParams(
            collective_id=1 + room, has_side_effects=True, vmem_limit_bytes=VMEM_LIMIT
        ),
    )(window, order, keys, values, queries, out_grad, text_keys, text_values)


VMEM_LIMIT = 60 * 1024 * 1024


def shards(queries, keys, values, text_keys, text_values, out_grad, window_ext):
    n_sa, n_wa = lax.axis_size("sa"), lax.axis_size("wa")
    grid = queries.shape
    channels = grid[-1]
    cells = grid[0] * grid[1] * grid[2]
    text_rows = text_keys.shape[0]
    flat = (cells, channels)
    heads = channels // HEAD_DIM // n_wa
    extents = window_ext.T
    n_hp = lax.axis_size("hp")
    every = n_wa * heads
    rooms = sorted({every // 2 + 1, -(-2 * every // 3), -(-5 * every // 6), every})
    branch, order = pl.pallas_call(
        functools.partial(meet, n_hp, n_wa, rooms),
        out_shape=(jax.ShapeDtypeStruct((1,), jnp.int32), jax.ShapeDtypeStruct((n_wa * heads,), jnp.int32)),
        in_specs=[pl.BlockSpec(memory_space=pltpu.SMEM), pl.BlockSpec(memory_space=pltpu.VMEM)],
        out_specs=(pl.BlockSpec(memory_space=pltpu.SMEM),) * 2,
        scratch_shapes=[
            pltpu.VMEM((n_hp - 1, *extents.shape), jnp.int32),
            pltpu.SemaphoreType.DMA((n_hp - 1,)),
            pltpu.SemaphoreType.DMA((n_hp - 1,)),
        ],
        compiler_params=pltpu.CompilerParams(collective_id=0, has_side_effects=True),
    )(extents, extents)

    res, words = lax.switch(
        branch[0], [functools.partial(attention, n_sa, n_wa, room) for room in rooms],
        extents, order, queries.reshape(flat), keys.reshape(flat),
        values.reshape(flat), out_grad.reshape(flat), text_keys, text_values,
    )
    in_vmem = pl.BlockSpec(memory_space=pltpu.VMEM)
    outs = pl.pallas_call(
        hand_over,
        out_shape=(jax.ShapeDtypeStruct(flat, BF16),) * 4
        + (jax.ShapeDtypeStruct((text_rows, channels), F32),) * 2,
        in_specs=[pl.BlockSpec(memory_space=pltpu.SMEM)] + [in_vmem] * 2,
        out_specs=(pl.BlockSpec(memory_space=pl.ANY),) * 6,
        scratch_shapes=[
            pltpu.VMEM((4, *flat), BF16),
            pltpu.VMEM((2, text_rows, channels), F32),
            pltpu.SemaphoreType.DMA((6,)),
        ],
    )(order, res, words)
    return tuple(out.reshape(grid) for out in outs[:4]) + tuple(outs[4:])


def solution(mesh):
    cell = P(("clips", "sa"), None, "wa", "hp")
    text = P(("clips", "sa"), "hp")
    return jax.shard_map(
        shards,
        mesh=mesh,
        in_specs=(cell, cell, cell, text, text, cell, P("hp", None)),
        out_specs=(cell, cell, cell, cell, text, text),
        check_vma=False,
    )
```

```python
import functools

import jax
import jax.numpy as jnp
from jax import lax
from jax.experimental import pallas as pl
from jax.experimental.pallas import tpu as pltpu
from jax.sharding import PartitionSpec as P

HEAD_DIM = 128
NEG = -1e30
MESH = pl.DeviceIdType.MESH
F32 = jnp.float32
BF16 = jnp.bfloat16
KEY_BLOCK = 256
Q_BLOCK = 256
FEED = 3
FAR_LAG = 1


def dot_nt(a, b):
    return lax.dot_general(a, b, (((1,), (1,)), ((), ())), preferred_element_type=F32)


def dot_tn(a, b):
    return lax.dot_general(a, b, (((0,), (0,)), ((), ())), preferred_element_type=F32)


def kernel(
    n_sa, n_wa, heads, room, cells, text_rows,
    window, order, k_in, v_in, q_in, g_in, tk_in, tv_in,
    res_out, text_out,
    cell_in, words_in, kv_by_head, qg_by_head, words_by_head, stage, kv, qg, oq, own_part, z_part, z_got, fin, t_part, t_got, t_far, t_fin, st, wb, db,
    load, x_send, x_recv, t_send, t_recv, z_send, z_recv,
    r_send, r_recv, y_send, y_recv, y_loc, g_send, g_recv, f_send, f_recv, f_loc, far_send, far_recv,
):
    s = lax.axis_index("sa")
    w = lax.axis_index("wa")
    slab = n_wa * cells
    text = n_sa * text_rows
    own_base = 2 * slab
    text_base = 3 * slab
    scale = HEAD_DIM ** (-0.5)
    has_prev, has_next = s > 0, s < n_sa - 1
    before, after = lax.rem(s + n_sa - 1, n_sa), lax.rem(s + 1, n_sa)
    q_block = min(slab, Q_BLOCK)
    most_near = -(-room // n_wa)
    near = (room + n_wa - 1 - lax.rem(w + n_wa - lax.rem(lax.axis_index("hp"), n_wa), n_wa)) // n_wa
    some_far = room < n_wa * heads
    relayed = heads - min(2, heads - most_near)
    return_lag = 1 if some_far else 2
    finish_lag = return_lag + 2

    def rows_of(base, index, size):
        return pl.ds(pl.multiple_of(base + index * size, 16), size)

    def remote(src, dst, send, recv, **where):
        return pltpu.make_async_remote_copy(
            src_ref=src, dst_ref=dst, send_sem=send, recv_sem=recv,
            device_id=where, device_id_type=MESH,
        )

    def peer_of(d):
        return lax.rem(w + d, n_wa)

    def source_of(d):
        return lax.rem(w + n_wa - d, n_wa)

    word_loads = [
        pltpu.make_async_copy(ref, words_in.at[kind], load.at[4 + kind])
        for kind, ref in enumerate((tk_in, tv_in))
    ]
    cell_loads = [
        pltpu.make_async_copy(ref, cell_in.at[kind], load.at[kind])
        for kind, ref in enumerate((k_in, v_in, q_in, g_in))
    ]
    for copy in word_loads + cell_loads:
        copy.start()

    barrier = pltpu.get_barrier_semaphore()
    for d in range(1, n_wa):
        pl.semaphore_signal(barrier, inc=1, device_id={"wa": peer_of(d)}, device_id_type=MESH)

    @pl.when(has_prev)
    def _():
        pl.semaphore_signal(barrier, inc=1, device_id={"sa": before}, device_id_type=MESH)

    @pl.when(has_next)
    def _():
        pl.semaphore_signal(barrier, inc=1, device_id={"sa": after}, device_id_type=MESH)

    def lanes_of(n):
        return pl.ds(pl.multiple_of(n * HEAD_DIM, HEAD_DIM), HEAD_DIM)

    def spread_keys(n, c):
        for kind in range(2):
            kv_by_head[n, kind] = cell_in[kind, :, lanes_of(n)]
        return c

    def spread_words(n, c):
        for kind in range(2):
            words_by_head[n, kind] = words_in[kind, :, lanes_of(n)]
        return c

    def arrange_words(h, c):
        kv[h, :, rows_of(text_base, s, text_rows)] = words_by_head[order[w * heads + h]]
        return c

    def spread_queries(n, c):
        for kind in range(2):
            qg_by_head[n, kind] = cell_in[2 + kind, :, lanes_of(n)]
        return c

    def arrange_keys(h, c):
        here = order[w * heads + h]
        kv[h, :, rows_of(own_base, w, cells)] = kv_by_head[here]
        for d in range(1, n_wa):
            stage[d - 1, h, pl.ds(0, 2)] = kv_by_head[order[peer_of(d) * heads + h]]
        return c

    def arrange_queries(h, c):
        qg[h, :, rows_of(0, w, cells)] = qg_by_head[order[w * heads + h]]
        for d in range(1, n_wa):
            stage[d - 1, h, pl.ds(2, 2)] = qg_by_head[order[peer_of(d) * heads + h]]
        return c

    for copy in word_loads:
        copy.wait()
    lax.fori_loop(0, n_wa * heads, spread_words, 0)
    lax.fori_loop(0, heads, arrange_words, 0)

    neighbours = n_wa - 1 + has_prev.astype(jnp.int32) + has_next.astype(jnp.int32)
    pl.semaphore_wait(barrier, neighbours)

    def x_slot(pair, h, source):
        if pair == 0:
            return kv.at[h, :, rows_of(own_base, source, cells)]
        return qg.at[h, :, rows_of(0, source, cells)]

    def x_copy(pair, h, d, source):
        return remote(
            stage.at[d - 1, h, pl.ds(2 * pair, 2)], x_slot(pair, h, source),
            x_send.at[d - 1], x_recv.at[d - 1, h, pair], wa=peer_of(d),
        )

    def x_wait(pair, h):
        for d in range(1, n_wa):
            x_copy(pair, h, d, source_of(d)).wait_recv()

    def t_slot(h, block):
        return kv.at[h, :, rows_of(text_base, block, text_rows)]

    def t_hop(side, h, hop, block):
        return remote(
            t_slot(h, block), t_slot(h, block), t_send.at[side, hop], t_recv.at[side, h, hop],
            sa=after if side == 0 else before,
        )

    def t_out(side, h, hop):
        return t_hop(side, h, hop, s - hop if side == 0 else s + hop)

    def t_in(side, h, hop):
        return t_hop(side, h, hop, s - 1 - hop if side == 0 else s + 1 + hop)

    def t_valid(side, hop):
        if side == 0:
            return jnp.logical_and(s >= hop, has_next)
        return jnp.logical_and(s + hop < n_sa, has_prev)

    def t_forward(h, hop):
        for side in range(2):
            @pl.when(t_valid(side, hop))
            def _():
                if hop:
                    t_in(side, h, hop - 1).wait_recv()
                t_out(side, h, hop).start()

    def z_copy(side, h):
        return remote(
            kv.at[h, :, pl.ds(own_base, slab)], kv.at[h, :, pl.ds(side * slab, slab)],
            z_send.at[side], z_recv.at[side, h], sa=after if side == 0 else before,
        )

    def r_copy(side, h, d):
        rows = rows_of(0, peer_of(d), cells)
        return remote(
            z_part.at[side, h, :, rows], z_got.at[side, h, :, rows],
            r_send.at[side], r_recv.at[side, h, d], sa=before if side == 0 else after,
        )

    def x_start(pair, h):
        for d in range(1, n_wa):
            x_copy(pair, h, d, w).start()

    def open_words(h, c):
        t_forward(h, 0)
        return c

    def open_keys(h, c):
        x_start(0, h)
        return c

    def open_both(h, c):
        x_start(1, h - first)
        return open_keys(h, c)

    first = min(2, heads)
    lax.fori_loop(0, heads, open_words, 0)
    for copy in cell_loads[:2]:
        copy.wait()
    lax.fori_loop(0, n_wa * heads, spread_keys, 0)
    lax.fori_loop(0, heads, arrange_keys, 0)
    lax.fori_loop(0, first, open_keys, 0)
    for copy in cell_loads[2:]:
        copy.wait()
    lax.fori_loop(0, n_wa * heads, spread_queries, 0)
    lax.fori_loop(0, heads, arrange_queries, 0)
    lax.fori_loop(first, heads, open_both, 0)
    for h in range(heads - first, heads):
        x_start(1, h)

    def clear_side(side):
        def clear(h, c):
            if most_near:
                @pl.when(h < near)
                def _():
                    kv[h, :, pl.ds(side * slab, slab)] = jnp.zeros((2, slab, HEAD_DIM), BF16)
                    z_got[1 - side, h] = jnp.zeros((2, slab, HEAD_DIM), BF16)

            t_got[side, h, 0 if side == 0 else n_sa - 1] = jnp.zeros((2, text_rows, HEAD_DIM), BF16)
            return c

        lax.fori_loop(0, heads, clear, 0)

    @pl.when(jnp.logical_not(has_prev))
    def _():
        clear_side(0)

    @pl.when(jnp.logical_not(has_next))
    def _():
        clear_side(1)

    def feed(h):
        t_forward(h, 1)
        x_wait(0, h)
        if most_near:
            @pl.when(h < near)
            def _():
                @pl.when(has_next)
                def _():
                    z_copy(0, h).start()

                @pl.when(has_prev)
                def _():
                    z_copy(1, h).start()

    def compute(h, halo):
        ext_t = window[0, order[w * heads + h]]
        ext_w = window[2, order[w * heads + h]]
        base = 0 if halo else own_base
        span = text_base + text - base
        keys = pl.ds(base, span)
        spread = (
            jnp.logical_and(has_prev, ext_t >= 1),
            jnp.logical_and(has_next, ext_t >= 1),
            None,
        )
        for qb in range(slab // q_block):
            q_rows = pl.ds(qb * q_block, q_block)
            q = qg[h, 0, q_rows]
            g = qg[h, 1, q_rows]
            query_col = qb * (q_block // cells) + lax.broadcasted_iota(jnp.int32, (1, q_block), 1) // cells
            top = jnp.full((1, q_block), NEG, F32)
            blocks = []
            for j in range(0 if halo else 2, 3):
                far = 0.0 if spread[j] is None else jnp.where(spread[j], 0.0, NEG)
                for c in range(n_wa):
                    bias = jnp.where(jnp.abs(query_col - c) <= ext_w, far, NEG)
                    blocks.append(((j * n_wa + c) * cells, cells, bias))
            for b in range(0, text, KEY_BLOCK):
                blocks.append((text_base + b, min(KEY_BLOCK, text - b), None))
            for start, size, bias in blocks:
                sc = dot_nt(kv[h, 0, pl.ds(start, size)], q) * scale
                if bias is not None:
                    sc = sc + bias
                st[pl.ds(start, size)] = sc
                top = jnp.maximum(top, jnp.max(sc, axis=0, keepdims=True))
            total = jnp.zeros((1, q_block), F32)
            for start, size, _ in blocks:
                p = jnp.exp(st[pl.ds(start, size)] - top)
                st[pl.ds(start, size)] = p
                total = total + jnp.sum(p, axis=0, keepdims=True)
            inv = 1.0 / total
            for start, size, _ in blocks:
                wb[pl.ds(start, size)] = (st[pl.ds(start, size)] * inv).astype(BF16)
            attended = dot_tn(wb[keys], kv[h, 1, keys]).astype(BF16)
            oq[h, 0, q_rows] = attended
            product = g.astype(F32) * attended.astype(F32)
            delta = jnp.sum(product.T, axis=0, keepdims=True)
            inv_scale = inv * scale
            for start, size, _ in blocks:
                dp = dot_nt(kv[h, 1, pl.ds(start, size)], g)
                db[pl.ds(start, size)] = (st[pl.ds(start, size)] * inv_scale * (dp - delta)).astype(BF16)
            def put(ref, index, value):
                if qb == 0:
                    ref[index] = value.astype(ref.dtype)
                else:
                    ref[index] = (ref[index].astype(F32) + value).astype(ref.dtype)

            sides = ((db, q), (wb, g))
            for kind, (left, right) in enumerate(sides):
                part = jnp.dot(left[pl.ds(text_base, text)], right, preferred_element_type=F32)
                put(t_part, (h, kind), part)
            if not halo and relayed < heads and qb == slab // q_block - 1:
                at(h, relayed, heads, far_start)
            oq[h, 1, q_rows] = dot_tn(db[keys], kv[h, 0, keys]).astype(BF16)
            for kind, (left, right) in enumerate(sides):
                part = jnp.dot(left[pl.ds(own_base, slab)], right, preferred_element_type=F32)
                put(own_part, (h, kind), part)
                for side in range(2 if halo else 0):
                    part = jnp.dot(left[pl.ds(side * slab, slab)], right, preferred_element_type=F32)
                    put(z_part, (side, h, kind), part)

    def y_src(pair, h, owner):
        return (oq if pair == 0 else fin).at[h, :, rows_of(0, owner, cells)]

    def y_dst(pair, h, group):
        return res_out.at[group * heads + h, pl.ds(2 * pair, 2)]

    def y_copy(pair, h, d, source):
        return remote(
            y_src(pair, h, peer_of(d)), y_dst(pair, h, source),
            y_send.at[d - 1, pair], y_recv.at[d - 1, pair], wa=peer_of(d),
        )

    def y_local(pair, h):
        return pltpu.make_async_copy(y_src(pair, h, w), y_dst(pair, h, w), y_loc.at[pair])

    def g_copy(side, h, block):
        return remote(
            t_part.at[h, :, rows_of(0, block, text_rows)], t_got.at[side, h, block],
            g_send.at[side, block], g_recv.at[side, h, block],
            sa=after if side == 0 else before,
        )

    def g_valid(side, block):
        return s < block if side == 0 else s > block

    def g_relay(side, h):
        inward = has_prev if side == 0 else has_next
        blocks = range(n_sa)
        for block in (reversed(blocks) if side == 0 else blocks):
            @pl.when(g_valid(side, block))
            def _():
                @pl.when(inward)
                def _():
                    g_copy(side, h, block).wait_recv()
                    rows = pl.ds(block * text_rows, text_rows)
                    joined = t_part[h, :, rows].astype(F32) + t_got[side, h, block].astype(F32)
                    t_part[h, :, rows] = joined.astype(BF16)

                g_copy(side, h, block).start()

    def far_copy(h, step, there, source):
        return remote(
            t_part.at[h, :, rows_of(0, there, text_rows)], t_far.at[h - relayed, source],
            far_send, far_recv.at[h - relayed, source], sa=there,
        )

    def far_start(h):
        for step in range(n_sa - 1, 0, -1):
            for there, valid in ((s + step, s + step < n_sa), (s - step, s >= step)):
                @pl.when(valid)
                def _():
                    far_copy(h, step, there, s).start()

    def finish_far(h):
        for step in range(1, n_sa):
            source = lax.rem(s + step, n_sa)
            far_copy(h, step, source, source).wait_recv()
        whole = t_part[h, :, rows_of(0, s, text_rows)].astype(F32)
        for step in range(1, n_sa):
            whole = whole + t_far[h - relayed, lax.rem(s + step, n_sa)].astype(F32)
        give_text(h, whole)

    def f_copy(h, d, source):
        return remote(
            t_fin.at[h], text_out.at[source * heads + h], f_send.at[d - 1], f_recv.at[d - 1], wa=peer_of(d),
        )

    def f_local(h):
        return pltpu.make_async_copy(t_fin.at[h], text_out.at[w * heads + h], f_loc)

    def give_text(h, whole):
        t_fin[h] = whole.astype(BF16)
        for d in range(1, n_wa):
            f_copy(h, d, w).start()
        f_local(h).start()

    def finish(h, d):
        rows = rows_of(0, peer_of(d), cells)
        if most_near:
            @pl.when(jnp.logical_and(h < near, has_next))
            def _():
                r_copy(0, h, d).wait_recv()

            @pl.when(jnp.logical_and(h < near, has_prev))
            def _():
                r_copy(1, h, d).wait_recv()

            @pl.when(h < near)
            def _():
                whole = own_part[h, :, rows] + z_got[0, h, :, rows].astype(F32) + z_got[1, h, :, rows].astype(F32)
                fin[h, :, rows] = whole.astype(BF16)

        if some_far:
            @pl.when(h >= near)
            def _():
                fin[h, :, rows] = own_part[h, :, rows].astype(BF16)

        if d:
            y_copy(1, h, d, w).start()
        else:
            y_local(1, h).start()

    def finish_text(h):
        @pl.when(has_prev)
        def _():
            g_copy(0, h, s).wait_recv()

        @pl.when(has_next)
        def _():
            g_copy(1, h, s).wait_recv()

        whole = t_part[h, :, rows_of(0, s, text_rows)].astype(F32)
        whole = whole + t_got[0, h, s].astype(F32) + t_got[1, h, s].astype(F32)
        give_text(h, whole)

    def attend(h):
        x_wait(1, h)

        @pl.when(jnp.logical_not(has_next))
        def _():
            for hop in range(n_sa - 1):
                t_in(0, h, hop).wait_recv()

        @pl.when(jnp.logical_not(has_prev))
        def _():
            for hop in range(n_sa - 1):
                t_in(1, h, hop).wait_recv()

        if most_near:
            @pl.when(jnp.logical_and(h < near, has_prev))
            def _():
                z_copy(0, h).wait_recv()

            @pl.when(jnp.logical_and(h < near, has_next))
            def _():
                z_copy(1, h).wait_recv()

            @pl.when(h < near)
            def _():
                compute(h, True)

        if some_far:
            @pl.when(h >= near)
            def _():
                compute(h, False)

        for d in range(1, n_wa):
            y_copy(0, h, d, w).start()
        y_local(0, h).start()

    def give_back(h, d):
        @pl.when(has_prev)
        def _():
            r_copy(0, h, d).start()

        @pl.when(has_next)
        def _():
            r_copy(1, h, d).start()

    def at(h, first, count, body):
        @pl.when(jnp.logical_and(h >= first, h < count))
        def _():
            body(h)

    def step(turn, c):
        i = turn - FEED
        at(turn, 0, heads, feed)
        for hop in range(2, n_sa - 1):
            at(i + FEED - 1, 0, heads, lambda h: t_forward(h, hop))
        at(i, 0, heads, attend)
        if some_far:
            for d in (*range(1, n_wa), 0):
                at(i, near, heads, lambda h: finish(h, d))
        for side in range(2):
            at(i - (s if side == 0 else n_sa - 1 - s), 0, relayed, lambda h: g_relay(side, h))
        if most_near:
            for d in range(1, n_wa):
                at(i - return_lag, 0, near, lambda h: give_back(h, d))
            at(i - return_lag - 1, 0, near, lambda h: give_back(h, 0))
        if relayed:
            at(i - (n_sa - 1), 0, relayed, finish_text)
        if relayed < heads:
            at(i - FAR_LAG, relayed, heads, finish_far)
        if most_near:
            for d in range(1, n_wa):
                at(i - finish_lag, 0, near, lambda h: finish(h, d))
            at(i - finish_lag - 1, 0, near, lambda h: finish(h, 0))
        return c

    lax.fori_loop(0, FEED + max(relayed + n_sa - 1, most_near + finish_lag + 1, heads + FAR_LAG), step, 0)

    every = pl.ds(0, heads)
    if relayed < heads:
        sent = t_far.at[:, pl.ds(0, n_sa - 1)]
        remote(sent, sent, far_send, far_recv.at[0, 0], sa=after).wait_send()
    for d in range(1, n_wa):
        remote(stage.at[d - 1], stage.at[d - 1], x_send.at[d - 1], x_recv.at[d - 1, 0, 0], wa=peer_of(d)).wait_send()
        for pair in range(2):
            for source, wait in ((w, "wait_send"), (source_of(d), "wait_recv")):
                group = res_out.at[pl.ds(source * heads, heads), pl.ds(2 * pair, 2)]
                getattr(remote(group, group, y_send.at[d - 1, pair], y_recv.at[d - 1, pair], wa=peer_of(d)), wait)()
        for source, wait in ((w, "wait_send"), (source_of(d), "wait_recv")):
            group = text_out.at[pl.ds(source * heads, heads)]
            getattr(remote(group, group, f_send.at[d - 1], f_recv.at[d - 1], wa=peer_of(d)), wait)()
    for pair in range(2):
        group = res_out.at[pl.ds(w * heads, heads), pl.ds(2 * pair, 2)]
        pltpu.make_async_copy(group, group, y_loc.at[pair]).wait()
    group = text_out.at[pl.ds(w * heads, heads)]
    pltpu.make_async_copy(group, group, f_loc).wait()
    for side in range(2):
        there = after if side == 0 else before
        block = kv.at[every, :, pl.ds(text_base, text_rows)]
        sums = kv.at[pl.ds(0, relayed), :, pl.ds(text_base, text_rows)] if relayed else None
        for hop in range(n_sa - 1):
            @pl.when(t_valid(side, hop))
            def _():
                remote(block, block, t_send.at[side, hop], t_recv.at[side, 0, hop], sa=there).wait_send()

        for owner in range(n_sa if relayed else 0):
            @pl.when(g_valid(side, owner))
            def _():
                remote(sums, sums, g_send.at[side, owner], g_recv.at[side, 0, owner], sa=there).wait_send()

        if most_near:
            def close_near(h, c):
                @pl.when(has_next if side == 0 else has_prev)
                def _():
                    z_copy(side, h).wait_send()

                @pl.when(has_prev if side == 0 else has_next)
                def _():
                    part = z_part.at[side, h]
                    remote(
                        part, part, r_send.at[side], r_recv.at[side, h, 0],
                        sa=before if side == 0 else after,
                    ).wait_send()

                return c

            lax.fori_loop(0, near, close_near, 0)


def meet(n_hp, n_wa, rooms, scalars, window, most, order, theirs, send, recv):
    me = lax.axis_index("hp")
    barrier = pltpu.get_barrier_semaphore()
    copies = []
    for d in range(1, n_hp):
        peer = lax.rem(me + d, n_hp)
        pl.semaphore_signal(barrier, inc=1, device_id={"hp": peer}, device_id_type=MESH)
        copies.append(pltpu.make_async_remote_copy(
            src_ref=window, dst_ref=theirs.at[d - 1], send_sem=send.at[d - 1], recv_sem=recv.at[d - 1],
            device_id={"hp": peer}, device_id_type=MESH,
        ))
    pl.semaphore_wait(barrier, n_hp - 1)
    for copy in copies:
        copy.start()

    count = order.shape[0]
    heads = count // n_wa
    wide = [(scalars[0, n] >= 1).astype(jnp.int32) for n in range(count)]
    reached = sum(wide)
    seen = jnp.int32(0)
    ranks = []
    for n in range(count):
        ranks.append(jnp.where(wide[n] > 0, seen, reached + n - seen))
        seen = seen + wide[n]
    for slot in range(count):
        rank = slot % heads * n_wa + lax.rem(slot // heads + n_wa - lax.rem(me, n_wa), n_wa)
        order[slot] = sum(jnp.where(ranks[n] == rank, n, 0) for n in range(count))

    axis = lax.broadcasted_iota(jnp.int32, window.shape, 0)
    total = reached.astype(F32)
    for d, copy in enumerate(copies):
        copy.wait()
        other = jnp.sum(jnp.where(jnp.logical_and(axis == 0, theirs[d] >= 1), 1.0, 0.0))
        total = jnp.maximum(total, other)
    most[0] = sum((total > room).astype(jnp.int32) for room in rooms[:-1])


def hand_over(order, res, words, o_out, dq_out, dk_out, dv_out, dtk_out, dtv_out, cell_rows, word_rows, done):
    slots = res.shape[0]
    copies = []

    def columns(slot):
        return pl.ds(pl.multiple_of(order[slot] * HEAD_DIM, HEAD_DIM), HEAD_DIM)

    def send(source, out):
        copies.append(pltpu.make_async_copy(source, out, done.at[len(copies)]))
        copies[-1].start()

    for kind, out in enumerate((dtk_out, dtv_out)):
        def place(slot, c):
            word_rows[kind, :, columns(slot)] = words[slot, kind].astype(F32)
            return c

        lax.fori_loop(0, slots, place, 0)
        send(word_rows.at[kind], out)

    for kind, out in enumerate((o_out, dq_out, dk_out, dv_out)):
        def place(slot, c):
            cell_rows[kind, :, columns(slot)] = res[slot, kind]
            return c

        lax.fori_loop(0, slots, place, 0)
        send(cell_rows.at[kind], out)

    for copy in copies:
        copy.wait()


def attention(n_sa, n_wa, room, window, order, queries, keys, values, out_grad, text_keys, text_values):
    cells, channels = queries.shape
    heads = channels // HEAD_DIM // n_wa
    text_rows = text_keys.shape[0]
    slab, text = n_wa * cells, n_sa * text_rows
    n_keys = 3 * slab + text
    q_block = min(slab, Q_BLOCK)
    halo = -(-room // n_wa)
    dma = pltpu.SemaphoreType.DMA
    anywhere = pl.BlockSpec(memory_space=pl.ANY)
    in_smem = pl.BlockSpec(memory_space=pltpu.SMEM)
    return pl.pallas_call(
        functools.partial(kernel, n_sa, n_wa, heads, room, cells, text_rows),
        out_shape=(
            jax.ShapeDtypeStruct((n_wa * heads, 4, cells, HEAD_DIM), BF16),
            jax.ShapeDtypeStruct((n_wa * heads, 2, text_rows, HEAD_DIM), BF16),
        ),
        in_specs=[in_smem] * 2 + [anywhere] * 6,
        out_specs=(anywhere,) * 2,
        scratch_shapes=[
            pltpu.VMEM((4, cells, channels), BF16),
            pltpu.VMEM((2, text_rows, channels), BF16),
            pltpu.VMEM((n_wa * heads, 2, cells, HEAD_DIM), BF16),
            pltpu.VMEM((n_wa * heads, 2, cells, HEAD_DIM), BF16),
            pltpu.VMEM((n_wa * heads, 2, text_rows, HEAD_DIM), BF16),
            pltpu.VMEM((n_wa - 1, heads, 4, cells, HEAD_DIM), BF16),
            pltpu.VMEM((heads, 2, n_keys, HEAD_DIM), BF16),
            pltpu.VMEM((heads, 2, slab, HEAD_DIM), BF16),
            pltpu.VMEM((heads, 2, slab, HEAD_DIM), BF16),
            pltpu.VMEM((heads, 2, slab, HEAD_DIM), F32),
            pltpu.VMEM((2, halo, 2, slab, HEAD_DIM), BF16),
            pltpu.VMEM((2, halo, 2, slab, HEAD_DIM), BF16),
            pltpu.VMEM((heads, 2, slab, HEAD_DIM), BF16),
            pltpu.VMEM((heads, 2, text, HEAD_DIM), BF16),
            pltpu.VMEM((2, heads, n_sa, 2, text_rows, HEAD_DIM), BF16),
            pltpu.VMEM((max(min(2, heads - halo), 1), n_sa, 2, text_rows, HEAD_DIM), BF16),
            pltpu.VMEM((heads, 2, text_rows, HEAD_DIM), BF16),
            pltpu.VMEM((n_keys, q_block), F32),
            pltpu.VMEM((n_keys, q_block), BF16),
            pltpu.VMEM((n_keys, q_block), BF16),
            dma((6,)),
            dma((n_wa - 1,)),
            dma((n_wa - 1, heads, 2)),
            dma((2, n_sa - 1)),
            dma((2, heads, n_sa - 1)),
            dma((2,)),
            dma((2, halo)),
            dma((2,)),
            dma((2, halo, n_wa)),
            dma((n_wa - 1, 2)),
            dma((n_wa - 1, 2)),
            dma((2,)),
            dma((2, n_sa)),
            dma((2, heads, n_sa)),
            dma((n_wa - 1,)),
            dma((n_wa - 1,)),
            dma(()),
            dma(()),
            dma((max(min(2, heads - halo), 1), n_sa)),
        ],
        compiler_params=pltpu.CompilerParams(
            collective_id=1 + room, has_side_effects=True, vmem_limit_bytes=VMEM_LIMIT
        ),
    )(window, order, keys, values, queries, out_grad, text_keys, text_values)


VMEM_LIMIT = 60 * 1024 * 1024


def shards(queries, keys, values, text_keys, text_values, out_grad, window_ext):
    n_sa, n_wa = lax.axis_size("sa"), lax.axis_size("wa")
    grid = queries.shape
    channels = grid[-1]
    cells = grid[0] * grid[1] * grid[2]
    text_rows = text_keys.shape[0]
    flat = (cells, channels)
    heads = channels // HEAD_DIM // n_wa
    extents = window_ext.T
    n_hp = lax.axis_size("hp")
    every = n_wa * heads
    rooms = sorted({every // 2 + 1, -(-2 * every // 3), -(-5 * every // 6), every})
    branch, order = pl.pallas_call(
        functools.partial(meet, n_hp, n_wa, rooms),
        out_shape=(jax.ShapeDtypeStruct((1,), jnp.int32), jax.ShapeDtypeStruct((n_wa * heads,), jnp.int32)),
        in_specs=[pl.BlockSpec(memory_space=pltpu.SMEM), pl.BlockSpec(memory_space=pltpu.VMEM)],
        out_specs=(pl.BlockSpec(memory_space=pltpu.SMEM),) * 2,
        scratch_shapes=[
            pltpu.VMEM((n_hp - 1, *extents.shape), jnp.int32),
            pltpu.SemaphoreType.DMA((n_hp - 1,)),
            pltpu.SemaphoreType.DMA((n_hp - 1,)),
        ],
        compiler_params=pltpu.CompilerParams(collective_id=0, has_side_effects=True),
    )(extents, extents)

    res, words = lax.switch(
        branch[0], [functools.partial(attention, n_sa, n_wa, room) for room in rooms],
        extents, order, queries.reshape(flat), keys.reshape(flat),
        values.reshape(flat), out_grad.reshape(flat), text_keys, text_values,
    )
    in_vmem = pl.BlockSpec(memory_space=pltpu.VMEM)
    outs = pl.pallas_call(
        hand_over,
        out_shape=(jax.ShapeDtypeStruct(flat, BF16),) * 4
        + (jax.ShapeDtypeStruct((text_rows, channels), F32),) * 2,
        in_specs=[pl.BlockSpec(memory_space=pltpu.SMEM)] + [in_vmem] * 2,
        out_specs=(pl.BlockSpec(memory_space=pl.ANY),) * 6,
        scratch_shapes=[
            pltpu.VMEM((4, *flat), BF16),
            pltpu.VMEM((2, text_rows, channels), F32),
            pltpu.SemaphoreType.DMA((6,)),
        ],
    )(order, res, words)
    return tuple(out.reshape(grid) for out in outs[:4]) + tuple(outs[4:])


def solution(mesh):
    cell = P(("clips", "sa"), None, "wa", "hp")
    text = P(("clips", "sa"), "hp")
    return jax.shard_map(
        shards,
        mesh=mesh,
        in_specs=(cell, cell, cell, text, text, cell, P("hp", None)),
        out_specs=(cell, cell, cell, cell, text, text),
        check_vma=False,
    )
```

```python
import functools

import jax
import jax.numpy as jnp
from jax import lax
from jax.experimental import pallas as pl
from jax.experimental.pallas import tpu as pltpu
from jax.sharding import PartitionSpec as P

HEAD_DIM = 128
NEG = -1e30
MESH = pl.DeviceIdType.MESH
F32 = jnp.float32
BF16 = jnp.bfloat16
KEY_BLOCK = 256
Q_BLOCK = 256
FEED = 3
FAR_LAG = 1


def dot_nt(a, b):
    return lax.dot_general(a, b, (((1,), (1,)), ((), ())), preferred_element_type=F32)


def dot_tn(a, b):
    return lax.dot_general(a, b, (((0,), (0,)), ((), ())), preferred_element_type=F32)


def kernel(
    n_sa, n_wa, heads, room, cells, text_rows,
    window, order, k_in, v_in, q_in, g_in, tk_in, tv_in,
    res_out, text_out,
    cell_in, words_in, kv_by_head, qg_by_head, words_by_head, stage, kv, qg, oq, own_part, z_part, z_got, fin, t_part, t_got, t_far, t_fin, st, wb, db,
    load, x_send, x_recv, t_send, t_recv, z_send, z_recv,
    r_send, r_recv, y_send, y_recv, y_loc, g_send, g_recv, f_send, f_recv, f_loc, far_send, far_recv,
):
    s = lax.axis_index("sa")
    w = lax.axis_index("wa")
    slab = n_wa * cells
    text = n_sa * text_rows
    own_base = 2 * slab
    text_base = 3 * slab
    scale = HEAD_DIM ** (-0.5)
    has_prev, has_next = s > 0, s < n_sa - 1
    before, after = lax.rem(s + n_sa - 1, n_sa), lax.rem(s + 1, n_sa)
    q_block = min(slab, Q_BLOCK)
    most_near = -(-room // n_wa)
    near = (room + n_wa - 1 - lax.rem(w + n_wa - lax.rem(lax.axis_index("hp"), n_wa), n_wa)) // n_wa
    some_far = room < n_wa * heads
    relayed = heads - min(2, heads - most_near)
    return_lag = 1 if most_near + 2 <= heads else 2
    finish_lag = return_lag + 2

    def rows_of(base, index, size):
        return pl.ds(pl.multiple_of(base + index * size, 16), size)

    def remote(src, dst, send, recv, **where):
        return pltpu.make_async_remote_copy(
            src_ref=src, dst_ref=dst, send_sem=send, recv_sem=recv,
            device_id=where, device_id_type=MESH,
        )

    def peer_of(d):
        return lax.rem(w + d, n_wa)

    def source_of(d):
        return lax.rem(w + n_wa - d, n_wa)

    word_loads = [
        pltpu.make_async_copy(ref, words_in.at[kind], load.at[4 + kind])
        for kind, ref in enumerate((tk_in, tv_in))
    ]
    cell_loads = [
        pltpu.make_async_copy(ref, cell_in.at[kind], load.at[kind])
        for kind, ref in enumerate((k_in, v_in, q_in, g_in))
    ]
    for copy in word_loads + cell_loads:
        copy.start()

    barrier = pltpu.get_barrier_semaphore()
    for d in range(1, n_wa):
        pl.semaphore_signal(barrier, inc=1, device_id={"wa": peer_of(d)}, device_id_type=MESH)

    @pl.when(has_prev)
    def _():
        pl.semaphore_signal(barrier, inc=1, device_id={"sa": before}, device_id_type=MESH)

    @pl.when(has_next)
    def _():
        pl.semaphore_signal(barrier, inc=1, device_id={"sa": after}, device_id_type=MESH)

    def lanes_of(n):
        return pl.ds(pl.multiple_of(n * HEAD_DIM, HEAD_DIM), HEAD_DIM)

    def spread_keys(n, c):
        for kind in range(2):
            kv_by_head[n, kind] = cell_in[kind, :, lanes_of(n)]
        return c

    def spread_words(n, c):
        for kind in range(2):
            words_by_head[n, kind] = words_in[kind, :, lanes_of(n)]
        return c

    def arrange_words(h, c):
        kv[h, :, rows_of(text_base, s, text_rows)] = words_by_head[order[w * heads + h]]
        return c

    def spread_queries(n, c):
        for kind in range(2):
            qg_by_head[n, kind] = cell_in[2 + kind, :, lanes_of(n)]
        return c

    def arrange_keys(h, c):
        here = order[w * heads + h]
        kv[h, :, rows_of(own_base, w, cells)] = kv_by_head[here]
        for d in range(1, n_wa):
            stage[d - 1, h, pl.ds(0, 2)] = kv_by_head[order[peer_of(d) * heads + h]]
        return c

    def arrange_queries(h, c):
        qg[h, :, rows_of(0, w, cells)] = qg_by_head[order[w * heads + h]]
        for d in range(1, n_wa):
            stage[d - 1, h, pl.ds(2, 2)] = qg_by_head[order[peer_of(d) * heads + h]]
        return c

    for copy in word_loads:
        copy.wait()
    lax.fori_loop(0, n_wa * heads, spread_words, 0)
    lax.fori_loop(0, heads, arrange_words, 0)

    neighbours = n_wa - 1 + has_prev.astype(jnp.int32) + has_next.astype(jnp.int32)
    pl.semaphore_wait(barrier, neighbours)

    def x_slot(pair, h, source):
        if pair == 0:
            return kv.at[h, :, rows_of(own_base, source, cells)]
        return qg.at[h, :, rows_of(0, source, cells)]

    def x_copy(pair, h, d, source):
        return remote(
            stage.at[d - 1, h, pl.ds(2 * pair, 2)], x_slot(pair, h, source),
            x_send.at[d - 1], x_recv.at[d - 1, h, pair], wa=peer_of(d),
        )

    def x_wait(pair, h):
        for d in range(1, n_wa):
            x_copy(pair, h, d, source_of(d)).wait_recv()

    def t_slot(h, block):
        return kv.at[h, :, rows_of(text_base, block, text_rows)]

    def t_hop(side, h, hop, block):
        return remote(
            t_slot(h, block), t_slot(h, block), t_send.at[side, hop], t_recv.at[side, h, hop],
            sa=after if side == 0 else before,
        )

    def t_out(side, h, hop):
        return t_hop(side, h, hop, s - hop if side == 0 else s + hop)

    def t_in(side, h, hop):
        return t_hop(side, h, hop, s - 1 - hop if side == 0 else s + 1 + hop)

    def t_valid(side, hop):
        if side == 0:
            return jnp.logical_and(s >= hop, has_next)
        return jnp.logical_and(s + hop < n_sa, has_prev)

    def t_forward(h, hop):
        for side in range(2):
            @pl.when(t_valid(side, hop))
            def _():
                if hop:
                    t_in(side, h, hop - 1).wait_recv()
                t_out(side, h, hop).start()

    def z_copy(side, h):
        return remote(
            kv.at[h, :, pl.ds(own_base, slab)], kv.at[h, :, pl.ds(side * slab, slab)],
            z_send.at[side], z_recv.at[side, h], sa=after if side == 0 else before,
        )

    def r_copy(side, h, d):
        rows = rows_of(0, peer_of(d), cells)
        return remote(
            z_part.at[side, h, :, rows], z_got.at[side, h, :, rows],
            r_send.at[side], r_recv.at[side, h, d], sa=before if side == 0 else after,
        )

    def x_start(pair, h):
        for d in range(1, n_wa):
            x_copy(pair, h, d, w).start()

    def open_words(h, c):
        t_forward(h, 0)
        return c

    def open_keys(h, c):
        x_start(0, h)
        return c

    def open_both(h, c):
        x_start(1, h - first)
        return open_keys(h, c)

    first = min(2, heads)
    lax.fori_loop(0, heads, open_words, 0)
    for copy in cell_loads[:2]:
        copy.wait()
    lax.fori_loop(0, n_wa * heads, spread_keys, 0)
    lax.fori_loop(0, heads, arrange_keys, 0)
    lax.fori_loop(0, first, open_keys, 0)
    for copy in cell_loads[2:]:
        copy.wait()
    lax.fori_loop(0, n_wa * heads, spread_queries, 0)
    lax.fori_loop(0, heads, arrange_queries, 0)
    lax.fori_loop(first, heads, open_both, 0)
    for h in range(heads - first, heads):
        x_start(1, h)

    def clear_side(side):
        def clear(h, c):
            if most_near:
                @pl.when(h < near)
                def _():
                    kv[h, :, pl.ds(side * slab, slab)] = jnp.zeros((2, slab, HEAD_DIM), BF16)
                    z_got[1 - side, h] = jnp.zeros((2, slab, HEAD_DIM), BF16)

            t_got[side, h, 0 if side == 0 else n_sa - 1] = jnp.zeros((2, text_rows, HEAD_DIM), BF16)
            return c

        lax.fori_loop(0, heads, clear, 0)

    @pl.when(jnp.logical_not(has_prev))
    def _():
        clear_side(0)

    @pl.when(jnp.logical_not(has_next))
    def _():
        clear_side(1)

    def feed(h):
        t_forward(h, 1)
        x_wait(0, h)
        if most_near:
            @pl.when(h < near)
            def _():
                @pl.when(has_next)
                def _():
                    z_copy(0, h).start()

                @pl.when(has_prev)
                def _():
                    z_copy(1, h).start()

    def compute(h, halo):
        ext_t = window[0, order[w * heads + h]]
        ext_w = window[2, order[w * heads + h]]
        base = 0 if halo else own_base
        span = text_base + text - base
        keys = pl.ds(base, span)
        spread = (
            jnp.logical_and(has_prev, ext_t >= 1),
            jnp.logical_and(has_next, ext_t >= 1),
            None,
        )
        for qb in range(slab // q_block):
            q_rows = pl.ds(qb * q_block, q_block)
            q = qg[h, 0, q_rows]
            g = qg[h, 1, q_rows]
            query_col = qb * (q_block // cells) + lax.broadcasted_iota(jnp.int32, (1, q_block), 1) // cells
            top = jnp.full((1, q_block), NEG, F32)
            blocks = []
            for j in range(0 if halo else 2, 3):
                far = 0.0 if spread[j] is None else jnp.where(spread[j], 0.0, NEG)
                for c in range(n_wa):
                    bias = jnp.where(jnp.abs(query_col - c) <= ext_w, far, NEG)
                    blocks.append(((j * n_wa + c) * cells, cells, bias))
            for b in range(0, text, KEY_BLOCK):
                blocks.append((text_base + b, min(KEY_BLOCK, text - b), None))
            for start, size, bias in blocks:
                sc = dot_nt(kv[h, 0, pl.ds(start, size)], q) * scale
                if bias is not None:
                    sc = sc + bias
                st[pl.ds(start, size)] = sc
                top = jnp.maximum(top, jnp.max(sc, axis=0, keepdims=True))
            total = jnp.zeros((1, q_block), F32)
            for start, size, _ in blocks:
                p = jnp.exp(st[pl.ds(start, size)] - top)
                st[pl.ds(start, size)] = p
                total = total + jnp.sum(p, axis=0, keepdims=True)
            inv = 1.0 / total
            for start, size, _ in blocks:
                wb[pl.ds(start, size)] = (st[pl.ds(start, size)] * inv).astype(BF16)
            attended = dot_tn(wb[keys], kv[h, 1, keys]).astype(BF16)
            oq[h, 0, q_rows] = attended
            product = g.astype(F32) * attended.astype(F32)
            delta = jnp.sum(product.T, axis=0, keepdims=True)
            inv_scale = inv * scale
            for start, size, _ in blocks:
                dp = dot_nt(kv[h, 1, pl.ds(start, size)], g)
                db[pl.ds(start, size)] = (st[pl.ds(start, size)] * inv_scale * (dp - delta)).astype(BF16)
            def put(ref, index, value):
                if qb == 0:
                    ref[index] = value.astype(ref.dtype)
                else:
                    ref[index] = (ref[index].astype(F32) + value).astype(ref.dtype)

            sides = ((db, q), (wb, g))
            for kind, (left, right) in enumerate(sides):
                part = jnp.dot(left[pl.ds(text_base, text)], right, preferred_element_type=F32)
                put(t_part, (h, kind), part)
            if not halo and relayed < heads and qb == slab // q_block - 1:
                at(h, relayed, heads, far_start)
            oq[h, 1, q_rows] = dot_tn(db[keys], kv[h, 0, keys]).astype(BF16)
            for kind, (left, right) in enumerate(sides):
                part = jnp.dot(left[pl.ds(own_base, slab)], right, preferred_element_type=F32)
                put(own_part, (h, kind), part)
                for side in range(2 if halo else 0):
                    part = jnp.dot(left[pl.ds(side * slab, slab)], right, preferred_element_type=F32)
                    put(z_part, (side, h, kind), part)

    def y_src(pair, h, owner):
        return (oq if pair == 0 else fin).at[h, :, rows_of(0, owner, cells)]

    def y_dst(pair, h, group):
        return res_out.at[group * heads + h, pl.ds(2 * pair, 2)]

    def y_copy(pair, h, d, source):
        return remote(
            y_src(pair, h, peer_of(d)), y_dst(pair, h, source),
            y_send.at[d - 1, pair], y_recv.at[d - 1, pair], wa=peer_of(d),
        )

    def y_local(pair, h):
        return pltpu.make_async_copy(y_src(pair, h, w), y_dst(pair, h, w), y_loc.at[pair])

    def g_copy(side, h, block):
        return remote(
            t_part.at[h, :, rows_of(0, block, text_rows)], t_got.at[side, h, block],
            g_send.at[side, block], g_recv.at[side, h, block],
            sa=after if side == 0 else before,
        )

    def g_valid(side, block):
        return s < block if side == 0 else s > block

    def g_relay(side, h):
        inward = has_prev if side == 0 else has_next
        blocks = range(n_sa)
        for block in (reversed(blocks) if side == 0 else blocks):
            @pl.when(g_valid(side, block))
            def _():
                @pl.when(inward)
                def _():
                    g_copy(side, h, block).wait_recv()
                    rows = pl.ds(block * text_rows, text_rows)
                    joined = t_part[h, :, rows].astype(F32) + t_got[side, h, block].astype(F32)
                    t_part[h, :, rows] = joined.astype(BF16)

                g_copy(side, h, block).start()

    def far_copy(h, step, there, source):
        return remote(
            t_part.at[h, :, rows_of(0, there, text_rows)], t_far.at[h - relayed, source],
            far_send, far_recv.at[h - relayed, source], sa=there,
        )

    def far_start(h):
        for step in range(n_sa - 1, 0, -1):
            for there, valid in ((s + step, s + step < n_sa), (s - step, s >= step)):
                @pl.when(valid)
                def _():
                    far_copy(h, step, there, s).start()

    def finish_far(h):
        for step in range(1, n_sa):
            source = lax.rem(s + step, n_sa)
            far_copy(h, step, source, source).wait_recv()
        whole = t_part[h, :, rows_of(0, s, text_rows)].astype(F32)
        for step in range(1, n_sa):
            whole = whole + t_far[h - relayed, lax.rem(s + step, n_sa)].astype(F32)
        give_text(h, whole)

    def f_copy(h, d, source):
        return remote(
            t_fin.at[h], text_out.at[source * heads + h], f_send.at[d - 1], f_recv.at[d - 1], wa=peer_of(d),
        )

    def f_local(h):
        return pltpu.make_async_copy(t_fin.at[h], text_out.at[w * heads + h], f_loc)

    def give_text(h, whole):
        t_fin[h] = whole.astype(BF16)
        for d in range(1, n_wa):
            f_copy(h, d, w).start()
        f_local(h).start()

    def finish(h, d):
        rows = rows_of(0, peer_of(d), cells)
        if most_near:
            @pl.when(jnp.logical_and(h < near, has_next))
            def _():
                r_copy(0, h, d).wait_recv()

            @pl.when(jnp.logical_and(h < near, has_prev))
            def _():
                r_copy(1, h, d).wait_recv()

            @pl.when(h < near)
            def _():
                whole = own_part[h, :, rows] + z_got[0, h, :, rows].astype(F32) + z_got[1, h, :, rows].astype(F32)
                fin[h, :, rows] = whole.astype(BF16)

        if some_far:
            @pl.when(h >= near)
            def _():
                fin[h, :, rows] = own_part[h, :, rows].astype(BF16)

        if d:
            y_copy(1, h, d, w).start()
        else:
            y_local(1, h).start()

    def finish_text(h):
        @pl.when(has_prev)
        def _():
            g_copy(0, h, s).wait_recv()

        @pl.when(has_next)
        def _():
            g_copy(1, h, s).wait_recv()

        whole = t_part[h, :, rows_of(0, s, text_rows)].astype(F32)
        whole = whole + t_got[0, h, s].astype(F32) + t_got[1, h, s].astype(F32)
        give_text(h, whole)

    def attend(h):
        x_wait(1, h)

        @pl.when(jnp.logical_not(has_next))
        def _():
            for hop in range(n_sa - 1):
                t_in(0, h, hop).wait_recv()

        @pl.when(jnp.logical_not(has_prev))
        def _():
            for hop in range(n_sa - 1):
                t_in(1, h, hop).wait_recv()

        if most_near:
            @pl.when(jnp.logical_and(h < near, has_prev))
            def _():
                z_copy(0, h).wait_recv()

            @pl.when(jnp.logical_and(h < near, has_next))
            def _():
                z_copy(1, h).wait_recv()

            @pl.when(h < near)
            def _():
                compute(h, True)

        if some_far:
            @pl.when(h >= near)
            def _():
                compute(h, False)

        for d in range(1, n_wa):
            y_copy(0, h, d, w).start()
        y_local(0, h).start()

    def give_back(h, d):
        @pl.when(has_prev)
        def _():
            r_copy(0, h, d).start()

        @pl.when(has_next)
        def _():
            r_copy(1, h, d).start()

    def at(h, first, count, body):
        @pl.when(jnp.logical_and(h >= first, h < count))
        def _():
            body(h)

    def step(turn, c):
        i = turn - FEED
        at(turn, 0, heads, feed)
        for hop in range(2, n_sa - 1):
            at(i + FEED - 1, 0, heads, lambda h: t_forward(h, hop))
        at(i, 0, heads, attend)
        if some_far:
            for d in (*range(1, n_wa), 0):
                at(i, near, heads, lambda h: finish(h, d))
        for side in range(2):
            at(i - (s if side == 0 else n_sa - 1 - s), 0, relayed, lambda h: g_relay(side, h))
        if most_near:
            for d in range(1, n_wa):
                at(i - return_lag, 0, near, lambda h: give_back(h, d))
            at(i - return_lag - 1, 0, near, lambda h: give_back(h, 0))
        if relayed:
            at(i - (n_sa - 1), 0, relayed, finish_text)
        if relayed < heads:
            at(i - FAR_LAG, relayed, heads, finish_far)
        if most_near:
            for d in range(1, n_wa):
                at(i - finish_lag, 0, near, lambda h: finish(h, d))
            at(i - finish_lag - 1, 0, near, lambda h: finish(h, 0))
        return c

    lax.fori_loop(0, FEED + max(relayed + n_sa - 1, most_near + finish_lag + 1, heads + FAR_LAG), step, 0)

    every = pl.ds(0, heads)
    if relayed < heads:
        sent = t_far.at[:, pl.ds(0, n_sa - 1)]
        remote(sent, sent, far_send, far_recv.at[0, 0], sa=after).wait_send()
    for d in range(1, n_wa):
        remote(stage.at[d - 1], stage.at[d - 1], x_send.at[d - 1], x_recv.at[d - 1, 0, 0], wa=peer_of(d)).wait_send()
        for pair in range(2):
            for source, wait in ((w, "wait_send"), (source_of(d), "wait_recv")):
                group = res_out.at[pl.ds(source * heads, heads), pl.ds(2 * pair, 2)]
                getattr(remote(group, group, y_send.at[d - 1, pair], y_recv.at[d - 1, pair], wa=peer_of(d)), wait)()
        for source, wait in ((w, "wait_send"), (source_of(d), "wait_recv")):
            group = text_out.at[pl.ds(source * heads, heads)]
            getattr(remote(group, group, f_send.at[d - 1], f_recv.at[d - 1], wa=peer_of(d)), wait)()
    for pair in range(2):
        group = res_out.at[pl.ds(w * heads, heads), pl.ds(2 * pair, 2)]
        pltpu.make_async_copy(group, group, y_loc.at[pair]).wait()
    group = text_out.at[pl.ds(w * heads, heads)]
    pltpu.make_async_copy(group, group, f_loc).wait()
    for side in range(2):
        there = after if side == 0 else before
        block = kv.at[every, :, pl.ds(text_base, text_rows)]
        sums = kv.at[pl.ds(0, relayed), :, pl.ds(text_base, text_rows)] if relayed else None
        for hop in range(n_sa - 1):
            @pl.when(t_valid(side, hop))
            def _():
                remote(block, block, t_send.at[side, hop], t_recv.at[side, 0, hop], sa=there).wait_send()

        for owner in range(n_sa if relayed else 0):
            @pl.when(g_valid(side, owner))
            def _():
                remote(sums, sums, g_send.at[side, owner], g_recv.at[side, 0, owner], sa=there).wait_send()

        if most_near:
            def close_near(h, c):
                @pl.when(has_next if side == 0 else has_prev)
                def _():
                    z_copy(side, h).wait_send()

                @pl.when(has_prev if side == 0 else has_next)
                def _():
                    part = z_part.at[side, h]
                    remote(
                        part, part, r_send.at[side], r_recv.at[side, h, 0],
                        sa=before if side == 0 else after,
                    ).wait_send()

                return c

            lax.fori_loop(0, near, close_near, 0)


def meet(n_hp, n_wa, rooms, scalars, window, most, order, theirs, send, recv):
    me = lax.axis_index("hp")
    barrier = pltpu.get_barrier_semaphore()
    copies = []
    for d in range(1, n_hp):
        peer = lax.rem(me + d, n_hp)
        pl.semaphore_signal(barrier, inc=1, device_id={"hp": peer}, device_id_type=MESH)
        copies.append(pltpu.make_async_remote_copy(
            src_ref=window, dst_ref=theirs.at[d - 1], send_sem=send.at[d - 1], recv_sem=recv.at[d - 1],
            device_id={"hp": peer}, device_id_type=MESH,
        ))
    pl.semaphore_wait(barrier, n_hp - 1)
    for copy in copies:
        copy.start()

    count = order.shape[0]
    heads = count // n_wa
    wide = [(scalars[0, n] >= 1).astype(jnp.int32) for n in range(count)]
    reached = sum(wide)
    seen = jnp.int32(0)
    ranks = []
    for n in range(count):
        ranks.append(jnp.where(wide[n] > 0, seen, reached + n - seen))
        seen = seen + wide[n]
    for slot in range(count):
        rank = slot % heads * n_wa + lax.rem(slot // heads + n_wa - lax.rem(me, n_wa), n_wa)
        order[slot] = sum(jnp.where(ranks[n] == rank, n, 0) for n in range(count))

    axis = lax.broadcasted_iota(jnp.int32, window.shape, 0)
    total = reached.astype(F32)
    for d, copy in enumerate(copies):
        copy.wait()
        other = jnp.sum(jnp.where(jnp.logical_and(axis == 0, theirs[d] >= 1), 1.0, 0.0))
        total = jnp.maximum(total, other)
    most[0] = sum((total > room).astype(jnp.int32) for room in rooms[:-1])


def hand_over(order, res, words, o_out, dq_out, dk_out, dv_out, dtk_out, dtv_out, cell_rows, word_rows, done):
    slots = res.shape[0]
    copies = []

    def columns(slot):
        return pl.ds(pl.multiple_of(order[slot] * HEAD_DIM, HEAD_DIM), HEAD_DIM)

    def send(source, out):
        copies.append(pltpu.make_async_copy(source, out, done.at[len(copies)]))
        copies[-1].start()

    for kind, out in enumerate((dtk_out, dtv_out)):
        def place(slot, c):
            word_rows[kind, :, columns(slot)] = words[slot, kind].astype(F32)
            return c

        lax.fori_loop(0, slots, place, 0)
        send(word_rows.at[kind], out)

    for kind, out in enumerate((o_out, dq_out, dk_out, dv_out)):
        def place(slot, c):
            cell_rows[kind, :, columns(slot)] = res[slot, kind]
            return c

        lax.fori_loop(0, slots, place, 0)
        send(cell_rows.at[kind], out)

    for copy in copies:
        copy.wait()


def attention(n_sa, n_wa, room, window, order, queries, keys, values, out_grad, text_keys, text_values):
    cells, channels = queries.shape
    heads = channels // HEAD_DIM // n_wa
    text_rows = text_keys.shape[0]
    slab, text = n_wa * cells, n_sa * text_rows
    n_keys = 3 * slab + text
    q_block = min(slab, Q_BLOCK)
    halo = -(-room // n_wa)
    dma = pltpu.SemaphoreType.DMA
    anywhere = pl.BlockSpec(memory_space=pl.ANY)
    in_smem = pl.BlockSpec(memory_space=pltpu.SMEM)
    return pl.pallas_call(
        functools.partial(kernel, n_sa, n_wa, heads, room, cells, text_rows),
        out_shape=(
            jax.ShapeDtypeStruct((n_wa * heads, 4, cells, HEAD_DIM), BF16),
            jax.ShapeDtypeStruct((n_wa * heads, 2, text_rows, HEAD_DIM), BF16),
        ),
        in_specs=[in_smem] * 2 + [anywhere] * 6,
        out_specs=(anywhere,) * 2,
        scratch_shapes=[
            pltpu.VMEM((4, cells, channels), BF16),
            pltpu.VMEM((2, text_rows, channels), BF16),
            pltpu.VMEM((n_wa * heads, 2, cells, HEAD_DIM), BF16),
            pltpu.VMEM((n_wa * heads, 2, cells, HEAD_DIM), BF16),
            pltpu.VMEM((n_wa * heads, 2, text_rows, HEAD_DIM), BF16),
            pltpu.VMEM((n_wa - 1, heads, 4, cells, HEAD_DIM), BF16),
            pltpu.VMEM((heads, 2, n_keys, HEAD_DIM), BF16),
            pltpu.VMEM((heads, 2, slab, HEAD_DIM), BF16),
            pltpu.VMEM((heads, 2, slab, HEAD_DIM), BF16),
            pltpu.VMEM((heads, 2, slab, HEAD_DIM), F32),
            pltpu.VMEM((2, halo, 2, slab, HEAD_DIM), BF16),
            pltpu.VMEM((2, halo, 2, slab, HEAD_DIM), BF16),
            pltpu.VMEM((heads, 2, slab, HEAD_DIM), BF16),
            pltpu.VMEM((heads, 2, text, HEAD_DIM), BF16),
            pltpu.VMEM((2, heads, n_sa, 2, text_rows, HEAD_DIM), BF16),
            pltpu.VMEM((max(min(2, heads - halo), 1), n_sa, 2, text_rows, HEAD_DIM), BF16),
            pltpu.VMEM((heads, 2, text_rows, HEAD_DIM), BF16),
            pltpu.VMEM((n_keys, q_block), F32),
            pltpu.VMEM((n_keys, q_block), BF16),
            pltpu.VMEM((n_keys, q_block), BF16),
            dma((6,)),
            dma((n_wa - 1,)),
            dma((n_wa - 1, heads, 2)),
            dma((2, n_sa - 1)),
            dma((2, heads, n_sa - 1)),
            dma((2,)),
            dma((2, halo)),
            dma((2,)),
            dma((2, halo, n_wa)),
            dma((n_wa - 1, 2)),
            dma((n_wa - 1, 2)),
            dma((2,)),
            dma((2, n_sa)),
            dma((2, heads, n_sa)),
            dma((n_wa - 1,)),
            dma((n_wa - 1,)),
            dma(()),
            dma(()),
            dma((max(min(2, heads - halo), 1), n_sa)),
        ],
        compiler_params=pltpu.CompilerParams(
            collective_id=1 + room, has_side_effects=True, vmem_limit_bytes=VMEM_LIMIT
        ),
    )(window, order, keys, values, queries, out_grad, text_keys, text_values)


VMEM_LIMIT = 60 * 1024 * 1024


def shards(queries, keys, values, text_keys, text_values, out_grad, window_ext):
    n_sa, n_wa = lax.axis_size("sa"), lax.axis_size("wa")
    grid = queries.shape
    channels = grid[-1]
    cells = grid[0] * grid[1] * grid[2]
    text_rows = text_keys.shape[0]
    flat = (cells, channels)
    heads = channels // HEAD_DIM // n_wa
    extents = window_ext.T
    n_hp = lax.axis_size("hp")
    every = n_wa * heads
    rooms = sorted({every // 2 + 1, -(-3 * every // 4), -(-5 * every // 6), every})
    branch, order = pl.pallas_call(
        functools.partial(meet, n_hp, n_wa, rooms),
        out_shape=(jax.ShapeDtypeStruct((1,), jnp.int32), jax.ShapeDtypeStruct((n_wa * heads,), jnp.int32)),
        in_specs=[pl.BlockSpec(memory_space=pltpu.SMEM), pl.BlockSpec(memory_space=pltpu.VMEM)],
        out_specs=(pl.BlockSpec(memory_space=pltpu.SMEM),) * 2,
        scratch_shapes=[
            pltpu.VMEM((n_hp - 1, *extents.shape), jnp.int32),
            pltpu.SemaphoreType.DMA((n_hp - 1,)),
            pltpu.SemaphoreType.DMA((n_hp - 1,)),
        ],
        compiler_params=pltpu.CompilerParams(collective_id=0, has_side_effects=True),
    )(extents, extents)

    res, words = lax.switch(
        branch[0], [functools.partial(attention, n_sa, n_wa, room) for room in rooms],
        extents, order, queries.reshape(flat), keys.reshape(flat),
        values.reshape(flat), out_grad.reshape(flat), text_keys, text_values,
    )
    in_vmem = pl.BlockSpec(memory_space=pltpu.VMEM)
    outs = pl.pallas_call(
        hand_over,
        out_shape=(jax.ShapeDtypeStruct(flat, BF16),) * 4
        + (jax.ShapeDtypeStruct((text_rows, channels), F32),) * 2,
        in_specs=[pl.BlockSpec(memory_space=pltpu.SMEM)] + [in_vmem] * 2,
        out_specs=(pl.BlockSpec(memory_space=pl.ANY),) * 6,
        scratch_shapes=[
            pltpu.VMEM((4, *flat), BF16),
            pltpu.VMEM((2, text_rows, channels), F32),
            pltpu.SemaphoreType.DMA((6,)),
        ],
    )(order, res, words)
    return tuple(out.reshape(grid) for out in outs[:4]) + tuple(outs[4:])


def solution(mesh):
    cell = P(("clips", "sa"), None, "wa", "hp")
    text = P(("clips", "sa"), "hp")
    return jax.shard_map(
        shards,
        mesh=mesh,
        in_specs=(cell, cell, cell, text, text, cell, P("hp", None)),
        out_specs=(cell, cell, cell, cell, text, text),
        check_vma=False,
    )
```

```python
import functools

import jax
import jax.numpy as jnp
from jax import lax
from jax.experimental import pallas as pl
from jax.experimental.pallas import tpu as pltpu
from jax.sharding import PartitionSpec as P

HEAD_DIM = 128
NEG = -1e30
MESH = pl.DeviceIdType.MESH
F32 = jnp.float32
BF16 = jnp.bfloat16
KEY_BLOCK = 128
Q_BLOCK = 256
FEED = 3
FAR_LAG = 1


def dot_nt(a, b):
    return lax.dot_general(a, b, (((1,), (1,)), ((), ())), preferred_element_type=F32)


def dot_tn(a, b):
    return lax.dot_general(a, b, (((0,), (0,)), ((), ())), preferred_element_type=F32)


def kernel(
    n_sa, n_wa, heads, room, cells, text_rows,
    window, order, k_in, v_in, q_in, g_in, tk_in, tv_in,
    res_out, text_out,
    cell_in, words_in, kv_by_head, qg_by_head, words_by_head, stage, kv, qg, oq, own_part, z_part, z_got, fin, t_part, t_got, t_far, t_fin, st, wb, db,
    load, x_send, x_recv, t_send, t_recv, z_send, z_recv,
    r_send, r_recv, y_send, y_recv, y_loc, g_send, g_recv, f_send, f_recv, f_loc, far_send, far_recv,
):
    s = lax.axis_index("sa")
    w = lax.axis_index("wa")
    slab = n_wa * cells
    text = n_sa * text_rows
    own_base = 2 * slab
    text_base = 3 * slab
    scale = HEAD_DIM ** (-0.5)
    has_prev, has_next = s > 0, s < n_sa - 1
    before, after = lax.rem(s + n_sa - 1, n_sa), lax.rem(s + 1, n_sa)
    q_block = min(slab, Q_BLOCK)
    most_near = -(-room // n_wa)
    near = (room + n_wa - 1 - lax.rem(w + n_wa - lax.rem(lax.axis_index("hp"), n_wa), n_wa)) // n_wa
    some_far = room < n_wa * heads
    relayed = heads - min(2, heads - most_near)
    return_lag = 1 if most_near + 2 <= heads else 2
    finish_lag = 3

    def rows_of(base, index, size):
        return pl.ds(pl.multiple_of(base + index * size, 16), size)

    def remote(src, dst, send, recv, **where):
        return pltpu.make_async_remote_copy(
            src_ref=src, dst_ref=dst, send_sem=send, recv_sem=recv,
            device_id=where, device_id_type=MESH,
        )

    def peer_of(d):
        return lax.rem(w + d, n_wa)

    def source_of(d):
        return lax.rem(w + n_wa - d, n_wa)

    word_loads = [
        pltpu.make_async_copy(ref, words_in.at[kind], load.at[4 + kind])
        for kind, ref in enumerate((tk_in, tv_in))
    ]
    cell_loads = [
        pltpu.make_async_copy(ref, cell_in.at[kind], load.at[kind])
        for kind, ref in enumerate((k_in, v_in, q_in, g_in))
    ]
    for copy in word_loads + cell_loads:
        copy.start()

    barrier = pltpu.get_barrier_semaphore()
    for d in range(1, n_wa):
        pl.semaphore_signal(barrier, inc=1, device_id={"wa": peer_of(d)}, device_id_type=MESH)

    @pl.when(has_prev)
    def _():
        pl.semaphore_signal(barrier, inc=1, device_id={"sa": before}, device_id_type=MESH)

    @pl.when(has_next)
    def _():
        pl.semaphore_signal(barrier, inc=1, device_id={"sa": after}, device_id_type=MESH)

    def lanes_of(n):
        return pl.ds(pl.multiple_of(n * HEAD_DIM, HEAD_DIM), HEAD_DIM)

    def spread_keys(n, c):
        for kind in range(2):
            kv_by_head[n, kind] = cell_in[kind, :, lanes_of(n)]
        return c

    def spread_words(n, c):
        for kind in range(2):
            words_by_head[n, kind] = words_in[kind, :, lanes_of(n)]
        return c

    def arrange_words(h, c):
        kv[h, :, rows_of(text_base, s, text_rows)] = words_by_head[order[w * heads + h]]
        return c

    def spread_queries(n, c):
        for kind in range(2):
            qg_by_head[n, kind] = cell_in[2 + kind, :, lanes_of(n)]
        return c

    def arrange_keys(h, c):
        here = order[w * heads + h]
        kv[h, :, rows_of(own_base, w, cells)] = kv_by_head[here]
        for d in range(1, n_wa):
            stage[d - 1, h, pl.ds(0, 2)] = kv_by_head[order[peer_of(d) * heads + h]]
        return c

    def arrange_queries(h, c):
        qg[h, :, rows_of(0, w, cells)] = qg_by_head[order[w * heads + h]]
        for d in range(1, n_wa):
            stage[d - 1, h, pl.ds(2, 2)] = qg_by_head[order[peer_of(d) * heads + h]]
        return c

    for copy in word_loads:
        copy.wait()
    lax.fori_loop(0, n_wa * heads, spread_words, 0)
    lax.fori_loop(0, heads, arrange_words, 0)

    neighbours = n_wa - 1 + has_prev.astype(jnp.int32) + has_next.astype(jnp.int32)
    pl.semaphore_wait(barrier, neighbours)

    def x_slot(pair, h, source):
        if pair == 0:
            return kv.at[h, :, rows_of(own_base, source, cells)]
        return qg.at[h, :, rows_of(0, source, cells)]

    def x_copy(pair, h, d, source):
        return remote(
            stage.at[d - 1, h, pl.ds(2 * pair, 2)], x_slot(pair, h, source),
            x_send.at[d - 1], x_recv.at[d - 1, h, pair], wa=peer_of(d),
        )

    def x_wait(pair, h):
        for d in range(1, n_wa):
            x_copy(pair, h, d, source_of(d)).wait_recv()

    def t_slot(h, block):
        return kv.at[h, :, rows_of(text_base, block, text_rows)]

    def t_hop(side, h, hop, block):
        return remote(
            t_slot(h, block), t_slot(h, block), t_send.at[side, hop], t_recv.at[side, h, hop],
            sa=after if side == 0 else before,
        )

    def t_out(side, h, hop):
        return t_hop(side, h, hop, s - hop if side == 0 else s + hop)

    def t_in(side, h, hop):
        return t_hop(side, h, hop, s - 1 - hop if side == 0 else s + 1 + hop)

    def t_valid(side, hop):
        if side == 0:
            return jnp.logical_and(s >= hop, has_next)
        return jnp.logical_and(s + hop < n_sa, has_prev)

    def t_forward(h, hop):
        for side in range(2):
            @pl.when(t_valid(side, hop))
            def _():
                if hop:
                    t_in(side, h, hop - 1).wait_recv()
                t_out(side, h, hop).start()

    def z_copy(side, h):
        return remote(
            kv.at[h, :, pl.ds(own_base, slab)], kv.at[h, :, pl.ds(side * slab, slab)],
            z_send.at[side], z_recv.at[side, h], sa=after if side == 0 else before,
        )

    def r_copy(side, h, d):
        rows = rows_of(0, peer_of(d), cells)
        return remote(
            z_part.at[side, h, :, rows], z_got.at[side, h, :, rows],
            r_send.at[side], r_recv.at[side, h, d], sa=before if side == 0 else after,
        )

    def x_start(pair, h):
        for d in range(1, n_wa):
            x_copy(pair, h, d, w).start()

    def open_words(h, c):
        t_forward(h, 0)
        return c

    def open_keys(h, c):
        x_start(0, h)
        return c

    def open_both(h, c):
        x_start(1, h - first)
        return open_keys(h, c)

    first = min(3, heads)
    lax.fori_loop(0, heads, open_words, 0)
    for copy in cell_loads[:2]:
        copy.wait()
    lax.fori_loop(0, n_wa * heads, spread_keys, 0)
    lax.fori_loop(0, heads, arrange_keys, 0)
    lax.fori_loop(0, first, open_keys, 0)
    for copy in cell_loads[2:]:
        copy.wait()
    lax.fori_loop(0, n_wa * heads, spread_queries, 0)
    lax.fori_loop(0, heads, arrange_queries, 0)
    lax.fori_loop(first, heads, open_both, 0)
    for h in range(heads - first, heads):
        x_start(1, h)

    def clear_side(side):
        def clear(h, c):
            if most_near:
                @pl.when(h < near)
                def _():
                    kv[h, :, pl.ds(side * slab, slab)] = jnp.zeros((2, slab, HEAD_DIM), BF16)
                    z_got[1 - side, h] = jnp.zeros((2, slab, HEAD_DIM), BF16)

            t_got[side, h, 0 if side == 0 else n_sa - 1] = jnp.zeros((2, text_rows, HEAD_DIM), BF16)
            return c

        lax.fori_loop(0, heads, clear, 0)

    @pl.when(jnp.logical_not(has_prev))
    def _():
        clear_side(0)

    @pl.when(jnp.logical_not(has_next))
    def _():
        clear_side(1)

    def feed(h):
        t_forward(h, 1)
        x_wait(0, h)
        if most_near:
            @pl.when(h < near)
            def _():
                @pl.when(has_next)
                def _():
                    z_copy(0, h).start()

                @pl.when(has_prev)
                def _():
                    z_copy(1, h).start()

    def compute(h, halo):
        ext_t = window[0, order[w * heads + h]]
        ext_w = window[2, order[w * heads + h]]
        base = 0 if halo else own_base
        span = text_base + text - base
        keys = pl.ds(base, span)
        spread = (
            jnp.logical_and(has_prev, ext_t >= 1),
            jnp.logical_and(has_next, ext_t >= 1),
            None,
        )
        for qb in range(slab // q_block):
            q_rows = pl.ds(qb * q_block, q_block)
            q = qg[h, 0, q_rows]
            g = qg[h, 1, q_rows]
            query_col = qb * (q_block // cells) + lax.broadcasted_iota(jnp.int32, (1, q_block), 1) // cells
            top = jnp.full((1, q_block), NEG, F32)
            blocks = []
            for j in range(0 if halo else 2, 3):
                far = 0.0 if spread[j] is None else jnp.where(spread[j], 0.0, NEG)
                for c in range(n_wa):
                    bias = jnp.where(jnp.abs(query_col - c) <= ext_w, far, NEG)
                    blocks.append(((j * n_wa + c) * cells, cells, bias))
            for b in range(0, text, KEY_BLOCK):
                blocks.append((text_base + b, min(KEY_BLOCK, text - b), None))
            for start, size, bias in blocks:
                sc = dot_nt(kv[h, 0, pl.ds(start, size)], q) * scale
                if bias is not None:
                    sc = sc + bias
                st[pl.ds(start, size)] = sc
                top = jnp.maximum(top, jnp.max(sc, axis=0, keepdims=True))
            total = jnp.zeros((1, q_block), F32)
            for start, size, _ in blocks:
                p = jnp.exp(st[pl.ds(start, size)] - top)
                st[pl.ds(start, size)] = p
                total = total + jnp.sum(p, axis=0, keepdims=True)
            inv = 1.0 / total
            for start, size, _ in blocks:
                wb[pl.ds(start, size)] = (st[pl.ds(start, size)] * inv).astype(BF16)
            attended = dot_tn(wb[keys], kv[h, 1, keys]).astype(BF16)
            oq[h, 0, q_rows] = attended
            product = g.astype(F32) * attended.astype(F32)
            delta = jnp.sum(product.T, axis=0, keepdims=True)
            inv_scale = inv * scale
            for start, size, _ in blocks:
                dp = dot_nt(kv[h, 1, pl.ds(start, size)], g)
                db[pl.ds(start, size)] = (st[pl.ds(start, size)] * inv_scale * (dp - delta)).astype(BF16)
            def put(ref, index, value):
                if qb == 0:
                    ref[index] = value.astype(ref.dtype)
                else:
                    ref[index] = (ref[index].astype(F32) + value).astype(ref.dtype)

            sides = ((db, q), (wb, g))
            for kind, (left, right) in enumerate(sides):
                part = jnp.dot(left[pl.ds(text_base, text)], right, preferred_element_type=F32)
                put(t_part, (h, kind), part)
            if not halo and relayed < heads and qb == slab // q_block - 1:
                at(h, relayed, heads, far_start)
            oq[h, 1, q_rows] = dot_tn(db[keys], kv[h, 0, keys]).astype(BF16)
            for kind, (left, right) in enumerate(sides):
                part = jnp.dot(left[pl.ds(own_base, slab)], right, preferred_element_type=F32)
                put(own_part, (h, kind), part)
                for side in range(2 if halo else 0):
                    part = jnp.dot(left[pl.ds(side * slab, slab)], right, preferred_element_type=F32)
                    put(z_part, (side, h, kind), part)

    def y_src(pair, h, owner):
        return (oq if pair == 0 else fin).at[h, :, rows_of(0, owner, cells)]

    def y_dst(pair, h, group):
        return res_out.at[group * heads + h, pl.ds(2 * pair, 2)]

    def y_copy(pair, h, d, source):
        return remote(
            y_src(pair, h, peer_of(d)), y_dst(pair, h, source),
            y_send.at[d - 1, pair], y_recv.at[d - 1, pair], wa=peer_of(d),
        )

    def y_local(pair, h):
        return pltpu.make_async_copy(y_src(pair, h, w), y_dst(pair, h, w), y_loc.at[pair])

    def g_copy(side, h, block):
        return remote(
            t_part.at[h, :, rows_of(0, block, text_rows)], t_got.at[side, h, block],
            g_send.at[side, block], g_recv.at[side, h, block],
            sa=after if side == 0 else before,
        )

    def g_valid(side, block):
        return s < block if side == 0 else s > block

    def g_relay(side, h):
        inward = has_prev if side == 0 else has_next
        blocks = range(n_sa)
        for block in (reversed(blocks) if side == 0 else blocks):
            @pl.when(g_valid(side, block))
            def _():
                @pl.when(inward)
                def _():
                    g_copy(side, h, block).wait_recv()
                    rows = pl.ds(block * text_rows, text_rows)
                    joined = t_part[h, :, rows].astype(F32) + t_got[side, h, block].astype(F32)
                    t_part[h, :, rows] = joined.astype(BF16)

                g_copy(side, h, block).start()

    def far_copy(h, step, there, source):
        return remote(
            t_part.at[h, :, rows_of(0, there, text_rows)], t_far.at[h - relayed, source],
            far_send, far_recv.at[h - relayed, source], sa=there,
        )

    def far_start(h):
        for step in range(n_sa - 1, 0, -1):
            for there, valid in ((s + step, s + step < n_sa), (s - step, s >= step)):
                @pl.when(valid)
                def _():
                    far_copy(h, step, there, s).start()

    def finish_far(h):
        for step in range(1, n_sa):
            source = lax.rem(s + step, n_sa)
            far_copy(h, step, source, source).wait_recv()
        whole = t_part[h, :, rows_of(0, s, text_rows)].astype(F32)
        for step in range(1, n_sa):
            whole = whole + t_far[h - relayed, lax.rem(s + step, n_sa)].astype(F32)
        give_text(h, whole)

    def f_copy(h, d, source):
        return remote(
            t_fin.at[h], text_out.at[source * heads + h], f_send.at[d - 1], f_recv.at[d - 1], wa=peer_of(d),
        )

    def f_local(h):
        return pltpu.make_async_copy(t_fin.at[h], text_out.at[w * heads + h], f_loc)

    def give_text(h, whole):
        t_fin[h] = whole.astype(BF16)
        for d in range(1, n_wa):
            f_copy(h, d, w).start()
        f_local(h).start()

    def finish(h, d):
        rows = rows_of(0, peer_of(d), cells)
        if most_near:
            @pl.when(jnp.logical_and(h < near, has_next))
            def _():
                r_copy(0, h, d).wait_recv()

            @pl.when(jnp.logical_and(h < near, has_prev))
            def _():
                r_copy(1, h, d).wait_recv()

            @pl.when(h < near)
            def _():
                whole = own_part[h, :, rows] + z_got[0, h, :, rows].astype(F32) + z_got[1, h, :, rows].astype(F32)
                fin[h, :, rows] = whole.astype(BF16)

        if some_far:
            @pl.when(h >= near)
            def _():
                fin[h, :, rows] = own_part[h, :, rows].astype(BF16)

        if d:
            y_copy(1, h, d, w).start()
        else:
            y_local(1, h).start()

    def finish_text(h):
        @pl.when(has_prev)
        def _():
            g_copy(0, h, s).wait_recv()

        @pl.when(has_next)
        def _():
            g_copy(1, h, s).wait_recv()

        whole = t_part[h, :, rows_of(0, s, text_rows)].astype(F32)
        whole = whole + t_got[0, h, s].astype(F32) + t_got[1, h, s].astype(F32)
        give_text(h, whole)

    def attend(h):
        x_wait(1, h)

        @pl.when(jnp.logical_not(has_next))
        def _():
            for hop in range(n_sa - 1):
                t_in(0, h, hop).wait_recv()

        @pl.when(jnp.logical_not(has_prev))
        def _():
            for hop in range(n_sa - 1):
                t_in(1, h, hop).wait_recv()

        if most_near:
            @pl.when(jnp.logical_and(h < near, has_prev))
            def _():
                z_copy(0, h).wait_recv()

            @pl.when(jnp.logical_and(h < near, has_next))
            def _():
                z_copy(1, h).wait_recv()

            @pl.when(h < near)
            def _():
                compute(h, True)

        if some_far:
            @pl.when(h >= near)
            def _():
                compute(h, False)

        for d in range(1, n_wa):
            y_copy(0, h, d, w).start()
        y_local(0, h).start()

    def give_back(h, d):
        @pl.when(has_prev)
        def _():
            r_copy(0, h, d).start()

        @pl.when(has_next)
        def _():
            r_copy(1, h, d).start()

    def at(h, first, count, body):
        @pl.when(jnp.logical_and(h >= first, h < count))
        def _():
            body(h)

    def step(turn, c):
        i = turn - FEED
        at(turn, 0, heads, feed)
        for hop in range(2, n_sa - 1):
            at(i + FEED - 1, 0, heads, lambda h: t_forward(h, hop))
        at(i, 0, heads, attend)
        if some_far:
            for d in (*range(1, n_wa), 0):
                at(i, near, heads, lambda h: finish(h, d))
        for side in range(2):
            at(i - (s if side == 0 else n_sa - 1 - s), 0, relayed, lambda h: g_relay(side, h))
        if most_near:
            for d in range(1, n_wa):
                at(i - return_lag, 0, near, lambda h: give_back(h, d))
            at(i - return_lag - 1, 0, near, lambda h: give_back(h, 0))
        if relayed:
            at(i - (n_sa - 1), 0, relayed, finish_text)
        if relayed < heads:
            at(i - FAR_LAG, relayed, heads, finish_far)
        if most_near:
            for d in range(1, n_wa):
                at(i - finish_lag, 0, near, lambda h: finish(h, d))
            at(i - finish_lag - 1, 0, near, lambda h: finish(h, 0))
        return c

    lax.fori_loop(0, FEED + max(relayed + n_sa - 1, most_near + finish_lag + 1, heads + FAR_LAG), step, 0)

    every = pl.ds(0, heads)
    if relayed < heads:
        sent = t_far.at[:, pl.ds(0, n_sa - 1)]
        remote(sent, sent, far_send, far_recv.at[0, 0], sa=after).wait_send()
    for d in range(1, n_wa):
        remote(stage.at[d - 1], stage.at[d - 1], x_send.at[d - 1], x_recv.at[d - 1, 0, 0], wa=peer_of(d)).wait_send()
        for pair in range(2):
            for source, wait in ((w, "wait_send"), (source_of(d), "wait_recv")):
                group = res_out.at[pl.ds(source * heads, heads), pl.ds(2 * pair, 2)]
                getattr(remote(group, group, y_send.at[d - 1, pair], y_recv.at[d - 1, pair], wa=peer_of(d)), wait)()
        for source, wait in ((w, "wait_send"), (source_of(d), "wait_recv")):
            group = text_out.at[pl.ds(source * heads, heads)]
            getattr(remote(group, group, f_send.at[d - 1], f_recv.at[d - 1], wa=peer_of(d)), wait)()
    for pair in range(2):
        group = res_out.at[pl.ds(w * heads, heads), pl.ds(2 * pair, 2)]
        pltpu.make_async_copy(group, group, y_loc.at[pair]).wait()
    group = text_out.at[pl.ds(w * heads, heads)]
    pltpu.make_async_copy(group, group, f_loc).wait()
    for side in range(2):
        there = after if side == 0 else before
        block = kv.at[every, :, pl.ds(text_base, text_rows)]
        sums = kv.at[pl.ds(0, relayed), :, pl.ds(text_base, text_rows)] if relayed else None
        for hop in range(n_sa - 1):
            @pl.when(t_valid(side, hop))
            def _():
                remote(block, block, t_send.at[side, hop], t_recv.at[side, 0, hop], sa=there).wait_send()

        for owner in range(n_sa if relayed else 0):
            @pl.when(g_valid(side, owner))
            def _():
                remote(sums, sums, g_send.at[side, owner], g_recv.at[side, 0, owner], sa=there).wait_send()

        if most_near:
            def close_near(h, c):
                @pl.when(has_next if side == 0 else has_prev)
                def _():
                    z_copy(side, h).wait_send()

                @pl.when(has_prev if side == 0 else has_next)
                def _():
                    part = z_part.at[side, h]
                    remote(
                        part, part, r_send.at[side], r_recv.at[side, h, 0],
                        sa=before if side == 0 else after,
                    ).wait_send()

                return c

            lax.fori_loop(0, near, close_near, 0)


def meet(n_hp, n_wa, rooms, scalars, window, most, order, theirs, send, recv):
    me = lax.axis_index("hp")
    barrier = pltpu.get_barrier_semaphore()
    copies = []
    for d in range(1, n_hp):
        peer = lax.rem(me + d, n_hp)
        pl.semaphore_signal(barrier, inc=1, device_id={"hp": peer}, device_id_type=MESH)
        copies.append(pltpu.make_async_remote_copy(
            src_ref=window, dst_ref=theirs.at[d - 1], send_sem=send.at[d - 1], recv_sem=recv.at[d - 1],
            device_id={"hp": peer}, device_id_type=MESH,
        ))
    pl.semaphore_wait(barrier, n_hp - 1)
    for copy in copies:
        copy.start()

    count = order.shape[0]
    heads = count // n_wa
    wide = [(scalars[0, n] >= 1).astype(jnp.int32) for n in range(count)]
    reached = sum(wide)
    seen = jnp.int32(0)
    ranks = []
    for n in range(count):
        ranks.append(jnp.where(wide[n] > 0, seen, reached + n - seen))
        seen = seen + wide[n]
    for slot in range(count):
        rank = slot % heads * n_wa + lax.rem(slot // heads + n_wa - lax.rem(me, n_wa), n_wa)
        order[slot] = sum(jnp.where(ranks[n] == rank, n, 0) for n in range(count))

    axis = lax.broadcasted_iota(jnp.int32, window.shape, 0)
    total = reached.astype(F32)
    for d, copy in enumerate(copies):
        copy.wait()
        other = jnp.sum(jnp.where(jnp.logical_and(axis == 0, theirs[d] >= 1), 1.0, 0.0))
        total = jnp.maximum(total, other)
    most[0] = sum((total > room).astype(jnp.int32) for room in rooms[:-1])


def hand_over(order, res, words, o_out, dq_out, dk_out, dv_out, dtk_out, dtv_out, cell_rows, word_rows, done):
    slots = res.shape[0]
    copies = []

    def columns(slot):
        return pl.ds(pl.multiple_of(order[slot] * HEAD_DIM, HEAD_DIM), HEAD_DIM)

    def send(source, out):
        copies.append(pltpu.make_async_copy(source, out, done.at[len(copies)]))
        copies[-1].start()

    for kind, out in enumerate((dtk_out, dtv_out)):
        def place(slot, c):
            word_rows[kind, :, columns(slot)] = words[slot, kind].astype(F32)
            return c

        lax.fori_loop(0, slots, place, 0)
        send(word_rows.at[kind], out)

    for kind, out in enumerate((o_out, dq_out, dk_out, dv_out)):
        def place(slot, c):
            cell_rows[kind, :, columns(slot)] = res[slot, kind]
            return c

        lax.fori_loop(0, slots, place, 0)
        send(cell_rows.at[kind], out)

    for copy in copies:
        copy.wait()


def attention(n_sa, n_wa, room, window, order, queries, keys, values, out_grad, text_keys, text_values):
    cells, channels = queries.shape
    heads = channels // HEAD_DIM // n_wa
    text_rows = text_keys.shape[0]
    slab, text = n_wa * cells, n_sa * text_rows
    n_keys = 3 * slab + text
    q_block = min(slab, Q_BLOCK)
    halo = -(-room // n_wa)
    dma = pltpu.SemaphoreType.DMA
    anywhere = pl.BlockSpec(memory_space=pl.ANY)
    in_smem = pl.BlockSpec(memory_space=pltpu.SMEM)
    return pl.pallas_call(
        functools.partial(kernel, n_sa, n_wa, heads, room, cells, text_rows),
        out_shape=(
            jax.ShapeDtypeStruct((n_wa * heads, 4, cells, HEAD_DIM), BF16),
            jax.ShapeDtypeStruct((n_wa * heads, 2, text_rows, HEAD_DIM), BF16),
        ),
        in_specs=[in_smem] * 2 + [anywhere] * 6,
        out_specs=(anywhere,) * 2,
        scratch_shapes=[
            pltpu.VMEM((4, cells, channels), BF16),
            pltpu.VMEM((2, text_rows, channels), BF16),
            pltpu.VMEM((n_wa * heads, 2, cells, HEAD_DIM), BF16),
            pltpu.VMEM((n_wa * heads, 2, cells, HEAD_DIM), BF16),
            pltpu.VMEM((n_wa * heads, 2, text_rows, HEAD_DIM), BF16),
            pltpu.VMEM((n_wa - 1, heads, 4, cells, HEAD_DIM), BF16),
            pltpu.VMEM((heads, 2, n_keys, HEAD_DIM), BF16),
            pltpu.VMEM((heads, 2, slab, HEAD_DIM), BF16),
            pltpu.VMEM((heads, 2, slab, HEAD_DIM), BF16),
            pltpu.VMEM((heads, 2, slab, HEAD_DIM), F32),
            pltpu.VMEM((2, halo, 2, slab, HEAD_DIM), BF16),
            pltpu.VMEM((2, halo, 2, slab, HEAD_DIM), BF16),
            pltpu.VMEM((heads, 2, slab, HEAD_DIM), BF16),
            pltpu.VMEM((heads, 2, text, HEAD_DIM), BF16),
            pltpu.VMEM((2, heads, n_sa, 2, text_rows, HEAD_DIM), BF16),
            pltpu.VMEM((max(min(2, heads - halo), 1), n_sa, 2, text_rows, HEAD_DIM), BF16),
            pltpu.VMEM((heads, 2, text_rows, HEAD_DIM), BF16),
            pltpu.VMEM((n_keys, q_block), F32),
            pltpu.VMEM((n_keys, q_block), BF16),
            pltpu.VMEM((n_keys, q_block), BF16),
            dma((6,)),
            dma((n_wa - 1,)),
            dma((n_wa - 1, heads, 2)),
            dma((2, n_sa - 1)),
            dma((2, heads, n_sa - 1)),
            dma((2,)),
            dma((2, halo)),
            dma((2,)),
            dma((2, halo, n_wa)),
            dma((n_wa - 1, 2)),
            dma((n_wa - 1, 2)),
            dma((2,)),
            dma((2, n_sa)),
            dma((2, heads, n_sa)),
            dma((n_wa - 1,)),
            dma((n_wa - 1,)),
            dma(()),
            dma(()),
            dma((max(min(2, heads - halo), 1), n_sa)),
        ],
        compiler_params=pltpu.CompilerParams(
            collective_id=1 + room, has_side_effects=True, vmem_limit_bytes=VMEM_LIMIT
        ),
    )(window, order, keys, values, queries, out_grad, text_keys, text_values)


VMEM_LIMIT = 60 * 1024 * 1024


def shards(queries, keys, values, text_keys, text_values, out_grad, window_ext):
    n_sa, n_wa = lax.axis_size("sa"), lax.axis_size("wa")
    grid = queries.shape
    channels = grid[-1]
    cells = grid[0] * grid[1] * grid[2]
    text_rows = text_keys.shape[0]
    flat = (cells, channels)
    heads = channels // HEAD_DIM // n_wa
    extents = window_ext.T
    n_hp = lax.axis_size("hp")
    every = n_wa * heads
    rooms = sorted({every // 2 + 1, -(-3 * every // 4), -(-5 * every // 6), every})
    branch, order = pl.pallas_call(
        functools.partial(meet, n_hp, n_wa, rooms),
        out_shape=(jax.ShapeDtypeStruct((1,), jnp.int32), jax.ShapeDtypeStruct((n_wa * heads,), jnp.int32)),
        in_specs=[pl.BlockSpec(memory_space=pltpu.SMEM), pl.BlockSpec(memory_space=pltpu.VMEM)],
        out_specs=(pl.BlockSpec(memory_space=pltpu.SMEM),) * 2,
        scratch_shapes=[
            pltpu.VMEM((n_hp - 1, *extents.shape), jnp.int32),
            pltpu.SemaphoreType.DMA((n_hp - 1,)),
            pltpu.SemaphoreType.DMA((n_hp - 1,)),
        ],
        compiler_params=pltpu.CompilerParams(collective_id=0, has_side_effects=True),
    )(extents, extents)

    res, words = lax.switch(
        branch[0], [functools.partial(attention, n_sa, n_wa, room) for room in rooms],
        extents, order, queries.reshape(flat), keys.reshape(flat),
        values.reshape(flat), out_grad.reshape(flat), text_keys, text_values,
    )
    in_vmem = pl.BlockSpec(memory_space=pltpu.VMEM)
    outs = pl.pallas_call(
        hand_over,
        out_shape=(jax.ShapeDtypeStruct(flat, BF16),) * 4
        + (jax.ShapeDtypeStruct((text_rows, channels), F32),) * 2,
        in_specs=[pl.BlockSpec(memory_space=pltpu.SMEM)] + [in_vmem] * 2,
        out_specs=(pl.BlockSpec(memory_space=pl.ANY),) * 6,
        scratch_shapes=[
            pltpu.VMEM((4, *flat), BF16),
            pltpu.VMEM((2, text_rows, channels), F32),
            pltpu.SemaphoreType.DMA((6,)),
        ],
    )(order, res, words)
    return tuple(out.reshape(grid) for out in outs[:4]) + tuple(outs[4:])


def solution(mesh):
    cell = P(("clips", "sa"), None, "wa", "hp")
    text = P(("clips", "sa"), "hp")
    return jax.shard_map(
        shards,
        mesh=mesh,
        in_specs=(cell, cell, cell, text, text, cell, P("hp", None)),
        out_specs=(cell, cell, cell, cell, text, text),
        check_vma=False,
    )
```
